32 devices in a mesh: fsdp: 8 (over y, x, core), tp: 4 (over z).
Axes of the slice: x: 2, y: 2, z: 4, core: 2. Of those that a mesh axis runs over, the one named last changes fastest.
Arguments:
- tokens: bfloat16 [4096, 2048], P(('fsdp', 'tp')), may hold values from -6 to 6
- cotangent: bfloat16 [4096, 2048], P(('fsdp', 'tp')), may hold values from -6 to 6
- attention_gain: bfloat16 [2, 2048], P(None, 'fsdp'), may hold values from 0.5 to 1.5
- query_weight: bfloat16 [2, 2048, 2048], P(None, 'fsdp', 'tp'), may hold values from -0.125 to 0.125
- key_weight: bfloat16 [2, 2048, 256], P(None, 'fsdp', 'tp'), may hold values from -0.125 to 0.125
- value_weight: bfloat16 [2, 2048, 256], P(None, 'fsdp', 'tp'), may hold values from -0.125 to 0.125
- output_weight: bfloat16 [2, 2048, 2048], P(None, 'tp', 'fsdp'), may hold values from -0.75 to 0.75
- feed_gain: bfloat16 [2, 2048], P(None, 'fsdp'), may hold values from 0.5 to 1.5
- gate_weight: bfloat16 [2, 2048, 5632], P(None, 'fsdp', 'tp'), may hold values from -0.125 to 0.125
- up_weight: bfloat16 [2, 2048, 5632], P(None, 'fsdp', 'tp'), may hold values from -0.125 to 0.125
- down_weight: bfloat16 [2, 5632, 2048], P(None, 'tp', 'fsdp'), may hold values from -0.078125 to 0.078125
Outputs:
- block_out: bfloat16 [4096, 2048], P(('fsdp', 'tp'))
- tokens_grad: float32 [4096, 2048], P(('fsdp', 'tp'))
- attention_gain_grad: float32 [2, 2048], P(None, 'fsdp')
- query_grad: float32 [2, 2048, 2048], P(None, 'fsdp', 'tp')
- key_grad: float32 [2, 2048, 256], P(None, 'fsdp', 'tp')
- value_grad: float32 [2, 2048, 256], P(None, 'fsdp', 'tp')
- output_grad: float32 [2, 2048, 2048], P(None, 'tp', 'fsdp')
- feed_gain_grad: float32 [2, 2048], P(None, 'fsdp')
- gate_grad: float32 [2, 2048, 5632], P(None, 'fsdp', 'tp')
- up_grad: float32 [2, 2048, 5632], P(None, 'fsdp', 'tp')
- down_grad: float32 [2, 5632, 2048], P(None, 'tp', 'fsdp')
The draws below stay inside these ranges and needn't reach their ends.
All inputs are finite; a program needn't handle non-finite values.
Results may differ from the reference program's by a relative error of at most 0.025.
Values may be sent and summed in bfloat16 or wider, within the bound.
No kernel may reach another device: no remote copies, remote signals or barrier semaphores. Data moves between devices by JAX's collectives and lax.ppermute only.
A program may use at most 256 MiB of HBM per device.

```python
import math
import jax
import jax.numpy as jnp
from jax import lax

D = 2048
HQ = 32
KV = 4
HD = 64
FF = 5632
LAYERS = 2
SEQ_LEN = 512
TOKENS = 4096


def raised(entries, key, source, target, blocks, factor):
    owner, partner = [(jnp.arange(entries.shape[axis_at]) // (entries.shape[axis_at] // blocks)).reshape([-1 if axis == axis_at else 1 for axis in range(entries.ndim)]) for axis_at in (source, target)]
    chosen = jax.random.permutation(key, blocks)[partner]
    strong = (owner == chosen) | (owner == (partner + blocks // 2) % blocks)
    return jnp.where(strong, factor * entries, entries)


def steps_of(rng, shape, split, smallest, largest):
    factor_of, own = 1.0, jax.random.fold_in(rng, 6)
    for axis_at, shards_of in split:
        steps = jnp.exp(jax.random.uniform(jax.random.fold_in(own, axis_at), (shards_of,), jnp.float32, smallest / len(split), largest / len(split)))
        factor_of = factor_of * jnp.repeat(steps, shape[axis_at] // shards_of).reshape([-1 if axis == axis_at else 1 for axis in range(len(shape))])
    return factor_of


def bell_draw(stream_key, shape, scale, limit, split=(), dtype=jnp.bfloat16):
    level = steps_of(stream_key, shape, split, -0.22, 0.18) if split else 1.0
    result = jax.random.normal(stream_key, shape, jnp.float32) * scale * level
    return jnp.minimum(jnp.maximum(result, -limit), limit).astype(dtype)


def heavy_noise(rng, shape, deviation, reach, shards, heavy, held_as=jnp.bfloat16):
    entries = deviation * jax.random.normal(rng, shape, jnp.float32)
    if shards:
        entries = entries * steps_of(rng, shape, shards, -0.22, 0.18)
    return jnp.clip(raised(entries, jax.random.fold_in(rng, 3), *heavy), -reach, reach).astype(held_as)


def setup_inputs(seed: int = 0) -> dict:
    seeds = jax.random.split(jax.random.key(seed), 12)
    return {
        "tokens": heavy_noise(seeds[0], (TOKENS, D), 1.0, 6.0, ((0, 32),), (0, 1, 32, 2.75)),
        "cotangent": heavy_noise(seeds[1], (TOKENS, D), 1.0, 6.0, ((0, 32),), (0, 1, 32, 2.75)),
        "attention_gain": jnp.clip(1.0 + 0.1 * jax.random.normal(seeds[2], (LAYERS, D), jnp.float32), 0.5, 1.5).astype(jnp.bfloat16),
        "query_weight": bell_draw(seeds[3], (LAYERS, D, D), D ** -0.5, 0.125, ((1, 8), (2, 4))),
        "key_weight": bell_draw(seeds[4], (LAYERS, D, KV * HD), D ** -0.5, 0.125, ((1, 8), (2, 4))),
        "value_weight": bell_draw(seeds[5], (LAYERS, D, KV * HD), D ** -0.5, 0.125, ((1, 8), (2, 4))),
        "output_weight": bell_draw(seeds[6], (LAYERS, D, D), (D // 32) ** -0.5, 0.75, ((1, 4), (2, 8))),
        "feed_gain": jnp.clip(1.0 + 0.1 * jax.random.normal(seeds[7], (LAYERS, D), jnp.float32), 0.5, 1.5).astype(jnp.bfloat16),
        "gate_weight": bell_draw(seeds[8], (LAYERS, D, FF), D ** -0.5, 0.125, ((1, 8), (2, 4))),
        "up_weight": bell_draw(seeds[9], (LAYERS, D, FF), D ** -0.5, 0.125, ((1, 8), (2, 4))),
        "down_weight": bell_draw(seeds[10], (LAYERS, FF, D), FF ** -0.5, 0.078125, ((1, 4), (2, 8))),
    }


@jax.custom_vjp
def low(v):
    return lax.optimization_barrier(v.astype(jnp.bfloat16)).astype(jnp.float32)

@jax.custom_vjp
def low_back(v):
    return v

def low_keep(v):
    return (low(v), None)

def low_pass(kept, grad):
    return (grad,)

def back_keep(v):
    return (v, None)

def back_low(kept, grad):
    return (low(grad),)
low.defvjp(low_keep, low_pass)
low_back.defvjp(back_keep, back_low)
epsilon = 1e-05
theta = 10000.0
masked_score = -1e+30
highest = lax.Precision.HIGHEST

def norm_rows(residual, scales):
    inverse = lax.rsqrt(lax.optimization_barrier(jnp.mean(residual * residual, axis=-1, keepdims=True)) + epsilon)
    return residual * inverse * scales

def angle_tables(row_count):
    half_width = HD // 2
    positions = (jnp.arange(row_count) % SEQ_LEN).astype(jnp.float32)
    exponent = 2.0 * jnp.arange(half_width).astype(jnp.float32) / HD
    frequency = theta ** (-exponent)
    angles = positions[:, None] * frequency[None, :]
    return (jnp.cos(angles), jnp.sin(angles))

def rotate(values, cosine, sine_table):
    half_width = values.shape[-1] // 2
    first_half = values[..., :half_width]
    second_half = values[..., half_width:]
    cos_rows = cosine[:, None, :]
    sin_rows = sine_table[:, None, :]
    return jnp.concatenate([first_half * cos_rows - second_half * sin_rows, second_half * cos_rows + first_half * sin_rows], axis=-1)

def causal_mask(seq_length):
    row_index = jnp.arange(seq_length)
    return row_index[:, None] >= row_index[None, :]

def attend(operands):
    query_seq, key_seq, value_seq = operands
    repeat = HQ // KV
    grouped = query_seq.reshape(SEQ_LEN, KV, repeat, HD)
    scores = low_back(jnp.einsum('qgrd,kgd->grqk', grouped, key_seq, precision=highest)) * HD ** (-0.5)
    scores = jnp.where(causal_mask(SEQ_LEN), scores, masked_score)
    probabilities = jax.nn.softmax(scores, axis=-1)
    mixed_heads = jnp.einsum('grqk,kgd->qgrd', low(probabilities), value_seq, precision=highest)
    return mixed_heads.reshape(SEQ_LEN, HQ * HD)

def layer_forward(residual, weights):
    attention_scale, query_matrix, key_matrix, value_matrix, output_matrix, feed_scale, gate_matrix, up_matrix, down_matrix = weights
    row_count = residual.shape[0]
    seq_count = row_count // SEQ_LEN
    cosine, sine_table = angle_tables(row_count)
    normed = low(norm_rows(residual, attention_scale))
    query_lin = low_back(jnp.dot(normed, query_matrix, precision=highest))
    key_lin = low_back(jnp.dot(normed, key_matrix, precision=highest))
    value_used = low(low_back(jnp.dot(normed, value_matrix, precision=highest)))
    query_used = low(rotate(query_lin.reshape(row_count, HQ, HD), cosine, sine_table))
    key_used = low(rotate(key_lin.reshape(row_count, KV, HD), cosine, sine_table))
    mixed_heads = lax.map(jax.checkpoint(attend), (query_used.reshape(seq_count, SEQ_LEN, HQ, HD), key_used.reshape(seq_count, SEQ_LEN, KV, HD), value_used.reshape(seq_count, SEQ_LEN, KV, HD)))
    mixed_heads = low(low_back(mixed_heads.reshape(row_count, HQ * HD)))
    hidden = residual + low_back(jnp.dot(mixed_heads, output_matrix, precision=highest))
    feed_normed = low(norm_rows(hidden, feed_scale))
    gate_lin = low_back(jnp.dot(feed_normed, gate_matrix, precision=highest))
    up_lin = low_back(jnp.dot(feed_normed, up_matrix, precision=highest))
    activated = low(jax.nn.silu(gate_lin) * up_lin)
    return hidden + low_back(jnp.dot(activated, down_matrix, precision=highest))

def block_forward(residual, weights):
    for layer_index in range(LAYERS):
        residual = layer_forward(residual, tuple((stacked[layer_index] for stacked in weights)))
    return residual

def reference(tokens, cotangent, attention_gain, query_weight, key_weight, value_weight, output_weight, feed_gain, gate_weight, up_weight, down_weight):
    weights = tuple((stacked.astype(jnp.float32) for stacked in (attention_gain, query_weight, key_weight, value_weight, output_weight, feed_gain, gate_weight, up_weight, down_weight)))
    seq_total = TOKENS // SEQ_LEN
    batch_seqs = math.gcd(seq_total, 8)
    batch_count = seq_total // batch_seqs
    batch_rows = batch_seqs * SEQ_LEN
    inputs = tokens.astype(jnp.float32).reshape(batch_count, batch_rows, D)
    upstream = cotangent.astype(jnp.float32).reshape(batch_count, batch_rows, D)

    def one_batch(totals, batch_pair):
        batch_in, batch_cot = batch_pair
        outputs, pullback = jax.vjp(block_forward, batch_in, weights)
        grad_in, grad_weights = pullback(batch_cot)
        totals = jax.tree.map(lambda running, addend: running + addend, totals, grad_weights)
        return (totals, (outputs.astype(jnp.bfloat16), grad_in))
    zero_grads = jax.tree.map(jnp.zeros_like, weights)
    totals, (outputs, grad_in) = lax.scan(one_batch, zero_grads, (inputs, upstream))
    return (outputs.reshape(TOKENS, D), grad_in.reshape(TOKENS, D), totals[0], totals[1], totals[2], totals[3], totals[4], totals[5], totals[6], totals[7], totals[8])
```

```python
import jax
import jax.numpy as jnp
from jax import lax
from jax.sharding import PartitionSpec as P

HD = 64
SEQ_LEN = 512
epsilon = 1e-05
theta = 10000.0
masked_score = -1e30
f32 = jnp.float32
bf16 = jnp.bfloat16


def norm_rows(residual, scales):
    inverse = lax.rsqrt(jnp.mean(residual * residual, axis=-1, keepdims=True) + epsilon)
    return residual * inverse * scales


def swiglu(gate_lin, up_lin):
    return jax.nn.silu(gate_lin) * up_lin


def angle_tables(positions):
    half_width = HD // 2
    exponent = 2.0 * jnp.arange(half_width).astype(f32) / HD
    frequency = theta ** (-exponent)
    angles = positions.astype(f32)[:, None] * frequency[None, :]
    return jnp.cos(angles), jnp.sin(angles)


def rotate(values, cosine, sine_table):
    half_width = values.shape[-1] // 2
    first_half = values[..., :half_width]
    second_half = values[..., half_width:]
    cos_rows = cosine[:, None, :]
    sin_rows = sine_table[:, None, :]
    return jnp.concatenate(
        [
            first_half * cos_rows - second_half * sin_rows,
            second_half * cos_rows + first_half * sin_rows,
        ],
        axis=-1,
    )


def attend_forward(query_seq, key_seq, value_seq, mask):
    rows, head_count, head_width = query_seq.shape
    group_count = key_seq.shape[1]
    repeat = head_count // group_count
    grouped = query_seq.reshape(rows, group_count, repeat, head_width)
    scores = jnp.einsum("qgrd,kgd->grqk", grouped, key_seq, preferred_element_type=f32)
    scores = jnp.where(mask, scores * head_width ** (-0.5), masked_score)
    largest = jnp.max(scores, axis=-1, keepdims=True)
    exp_scores = jnp.exp(scores - largest)
    totals = jnp.sum(exp_scores, axis=-1, keepdims=True)
    probabilities = exp_scores / totals
    log_total = largest + jnp.log(totals)
    mixed = jnp.einsum(
        "grqk,kgd->qgrd", probabilities.astype(bf16), value_seq, preferred_element_type=f32
    )
    return mixed.reshape(rows, head_count * head_width).astype(bf16), log_total


def attend_backward(query_seq, key_seq, value_seq, log_total, grad_mixed, mask):
    rows, head_count, head_width = query_seq.shape
    group_count = key_seq.shape[1]
    repeat = head_count // group_count
    score_scale = head_width ** (-0.5)
    grouped = query_seq.reshape(rows, group_count, repeat, head_width)
    scores = jnp.einsum("qgrd,kgd->grqk", grouped, key_seq, preferred_element_type=f32)
    scores = jnp.where(mask, scores * score_scale, masked_score)
    probabilities = jnp.exp(scores - log_total)
    grad_grouped = grad_mixed.reshape(rows, group_count, repeat, head_width)
    grad_value = jnp.einsum(
        "grqk,qgrd->kgd", probabilities.astype(bf16), grad_grouped, preferred_element_type=f32
    )
    grad_probs = jnp.einsum(
        "qgrd,kgd->grqk", grad_grouped, value_seq, preferred_element_type=f32
    )
    inner_sum = jnp.sum(probabilities * grad_probs, axis=-1, keepdims=True)
    grad_scores = (probabilities * (grad_probs - inner_sum) * score_scale).astype(bf16)
    grad_query = jnp.einsum("grqk,kgd->qgrd", grad_scores, key_seq, preferred_element_type=f32)
    grad_key = jnp.einsum("grqk,qgrd->kgd", grad_scores, grouped, preferred_element_type=f32)
    return grad_query.reshape(rows, head_count, head_width), grad_key, grad_value


def shift(values):
    size = lax.axis_size("tp")
    return lax.ppermute(values, "tp", [(i, (i + 1) % size) for i in range(size)])


def ring_gather(values):
    slots = [values]
    for _ in range(lax.axis_size("tp") - 1):
        slots.append(shift(slots[-1]))
    return slots


def ring_sum(parts):
    running = parts[1].astype(bf16)
    for part in parts[2:]:
        running = (shift(running).astype(f32) + part).astype(bf16)
    return shift(running).astype(f32) + parts[0]


def dot(a, b):
    return jnp.dot(a, b, preferred_element_type=f32)


def dot_t(a, b):
    return lax.dot_general(a, b, (((1,), (1,)), ((), ())), preferred_element_type=f32)


def t_dot(a, b):
    return lax.dot_general(a, b, (((0,), (0,)), ((), ())), preferred_element_type=f32)


def gather_weight(values):
    return lax.all_gather(values, "fsdp", axis=0, tiled=True)


def scatter_weight(values):
    return lax.psum_scatter(values.astype(bf16), "fsdp", scatter_dimension=0, tiled=True)


def local(
    tokens,
    cotangent,
    attention_gain,
    query_weight,
    key_weight,
    value_weight,
    output_weight,
    feed_gain,
    gate_weight,
    up_weight,
    down_weight,
):
    layer_count = query_weight.shape[0]
    local_rows = tokens.shape[0]
    size = lax.axis_size("tp")
    me = lax.axis_index("tp")
    group_rows = local_rows * size
    q_width = query_weight.shape[2]
    k_width = key_weight.shape[2]
    head_local = q_width // HD
    group_local = k_width // HD
    qkv_width = q_width + 2 * k_width
    hidden_width = gate_weight.shape[2]

    row_index = (
        ((me - jnp.arange(size)) % size)[:, None] * local_rows + jnp.arange(local_rows)[None, :]
    ).reshape(group_rows)
    cosine, sine = angle_tables(row_index % SEQ_LEN)
    mask = (row_index[:, None] >= row_index[None, :]) & (
        (row_index // SEQ_LEN)[:, None] == (row_index // SEQ_LEN)[None, :]
    )

    gains = lax.all_gather(
        jnp.concatenate([attention_gain, feed_gain], axis=0), "fsdp", axis=1, tiled=True
    ).astype(f32)
    attention_gains = gains[:layer_count]
    feed_gains = gains[layer_count:]
    attention_sets, feed_sets = [], []
    for l in range(layer_count):
        attention_sets.append(
            gather_weight(
                jnp.concatenate(
                    [query_weight[l], key_weight[l], value_weight[l], output_weight[l].T], axis=1
                )
            )
        )
        feed_sets.append(
            gather_weight(
                jnp.concatenate([gate_weight[l], up_weight[l], down_weight[l].T], axis=1)
            )
        )

    token_slots = ring_gather(tokens)
    cotangent_slots = ring_gather(cotangent)

    residual = tokens.astype(f32)
    kept = []
    block_out = None
    for l in range(layer_count):
        weight_qkv = attention_sets[l][:, :qkv_width]
        weight_out_t = attention_sets[l][:, qkv_width:]
        weight_gu = feed_sets[l][:, : 2 * hidden_width]
        weight_down_t = feed_sets[l][:, 2 * hidden_width :]
        if l == 0:
            normed_slots = [
                norm_rows(t.astype(f32), attention_gains[l]).astype(bf16) for t in token_slots
            ]
        else:
            normed_slots = ring_gather(norm_rows(residual, attention_gains[l]).astype(bf16))
        qkv = jnp.concatenate([dot(x, weight_qkv) for x in normed_slots], axis=0)
        query_used = rotate(
            qkv[:, :q_width].reshape(group_rows, head_local, HD), cosine, sine
        ).astype(bf16)
        key_used = rotate(
            qkv[:, q_width : q_width + k_width].reshape(group_rows, group_local, HD), cosine, sine
        ).astype(bf16)
        value_used = qkv[:, q_width + k_width :].reshape(group_rows, group_local, HD).astype(bf16)
        mixed, log_total = attend_forward(query_used, key_used, value_used, mask)
        mixed_slots = [mixed[s * local_rows : (s + 1) * local_rows] for s in range(size)]
        hidden = residual + ring_sum([dot_t(m, weight_out_t) for m in mixed_slots])
        feed_slots = ring_gather(norm_rows(hidden, feed_gains[l]).astype(bf16))
        gu_slots = [dot(x, weight_gu) for x in feed_slots]
        activated_slots = [
            swiglu(gu[:, :hidden_width], gu[:, hidden_width:]).astype(bf16) for gu in gu_slots
        ]
        kept.append(
            (residual, normed_slots, query_used, key_used, value_used, mixed, log_total, hidden,
             feed_slots, gu_slots, activated_slots)
        )
        residual = hidden + ring_sum([dot_t(a, weight_down_t) for a in activated_slots])
    block_out = residual.astype(bf16)

    grad_resid = cotangent.astype(f32)
    grads = [None] * layer_count
    for l in range(layer_count - 1, -1, -1):
        (residual, normed_slots, query_used, key_used, value_used, mixed, log_total, hidden,
         feed_slots, gu_slots, activated_slots) = kept[l]
        weight_qkv = attention_sets[l][:, :qkv_width]
        weight_out_t = attention_sets[l][:, qkv_width:]
        weight_gu = feed_sets[l][:, : 2 * hidden_width]
        weight_down_t = feed_sets[l][:, 2 * hidden_width :]
        if l == layer_count - 1:
            grad_slots = cotangent_slots
        else:
            grad_slots = ring_gather(grad_resid.astype(bf16))
        down_grad = scatter_weight(
            t_dot(jnp.concatenate(grad_slots, axis=0), jnp.concatenate(activated_slots, axis=0))
        )
        grad_gu_slots = []
        for g, gu in zip(grad_slots, gu_slots):
            grad_act = dot(g, weight_down_t)
            pair = jax.vjp(swiglu, gu[:, :hidden_width], gu[:, hidden_width:])[1](grad_act)
            grad_gu_slots.append(jnp.concatenate([p.astype(bf16) for p in pair], axis=1))
        grad_normed = ring_sum([dot_t(g, weight_gu) for g in grad_gu_slots])
        gu_grad = scatter_weight(
            t_dot(jnp.concatenate(feed_slots, axis=0), jnp.concatenate(grad_gu_slots, axis=0))
        )
        grad_hidden, feed_gain_part = jax.vjp(norm_rows, hidden, feed_gains[l])[1](grad_normed)
        grad_resid = grad_resid + grad_hidden
        mid_slots = ring_gather(grad_resid.astype(bf16))
        grad_mixed = jnp.concatenate(
            [dot(g, weight_out_t).astype(bf16) for g in mid_slots], axis=0
        )
        out_part = t_dot(jnp.concatenate(mid_slots, axis=0), mixed)
        grad_query, grad_key, grad_value = attend_backward(
            query_used, key_used, value_used, log_total, grad_mixed, mask
        )
        grad_qkv = jnp.concatenate(
            [
                rotate(grad_query, cosine, -sine).reshape(group_rows, q_width).astype(bf16),
                rotate(grad_key, cosine, -sine).reshape(group_rows, k_width).astype(bf16),
                grad_value.reshape(group_rows, k_width).astype(bf16),
            ],
            axis=1,
        )
        grad_normed = ring_sum(
            [
                dot_t(grad_qkv[s * local_rows : (s + 1) * local_rows], weight_qkv)
                for s in range(size)
            ]
        )
        qkv_part = t_dot(jnp.concatenate(normed_slots, axis=0), grad_qkv)
        attention_grad = scatter_weight(
            jnp.concatenate([qkv_part.astype(bf16), out_part.astype(bf16)], axis=1)
        )
        grad_before, attention_gain_part = jax.vjp(norm_rows, residual, attention_gains[l])[1](
            grad_normed
        )
        grad_resid = grad_resid + grad_before
        grads[l] = (attention_gain_part, feed_gain_part, attention_grad, gu_grad, down_grad)

    gain_parts = jnp.stack([g[0] for g in grads] + [g[1] for g in grads])
    gain_sums = lax.psum(gain_parts, ("fsdp", "tp"))
    width = attention_gain.shape[1]
    gain_sums = lax.dynamic_slice_in_dim(gain_sums, lax.axis_index("fsdp") * width, width, axis=1)
    parts = [g[2].astype(f32) for g in grads]
    return (
        block_out,
        grad_resid,
        gain_sums[:layer_count],
        jnp.stack([p[:, :q_width] for p in parts]),
        jnp.stack([p[:, q_width : q_width + k_width] for p in parts]),
        jnp.stack([p[:, q_width + k_width : qkv_width] for p in parts]),
        jnp.stack([p[:, qkv_width:].T for p in parts]),
        gain_sums[layer_count:],
        jnp.stack([g[3][:, :hidden_width].astype(f32) for g in grads]),
        jnp.stack([g[3][:, hidden_width:].astype(f32) for g in grads]),
        jnp.stack([g[4].astype(f32).T for g in grads]),
    )


def solution(mesh):
    rows = P(("fsdp", "tp"), None)
    gain = P(None, "fsdp")
    column = P(None, "fsdp", "tp")
    row = P(None, "tp", "fsdp")
    weights = (gain, column, column, column, row, gain, column, column, row)
    return jax.shard_map(
        local,
        mesh=mesh,
        in_specs=(rows, rows) + weights,
        out_specs=(rows, rows) + weights,
        check_vma=False,
    )
```

```python
import jax
import jax.numpy as jnp
from jax import lax
from jax.sharding import PartitionSpec as P

HD = 64
SEQ_LEN = 512
epsilon = 1e-05
theta = 10000.0
masked_score = -1e30
f32 = jnp.float32
bf16 = jnp.bfloat16


def norm_rows(residual, scales):
    inverse = lax.rsqrt(jnp.mean(residual * residual, axis=-1, keepdims=True) + epsilon)
    return residual * inverse * scales


def swiglu(gate_lin, up_lin):
    return jax.nn.silu(gate_lin) * up_lin


def angle_tables(positions):
    half_width = HD // 2
    exponent = 2.0 * jnp.arange(half_width).astype(f32) / HD
    frequency = theta ** (-exponent)
    angles = positions.astype(f32)[:, None] * frequency[None, :]
    return jnp.cos(angles), jnp.sin(angles)


def rotate(values, cosine, sine_table):
    half_width = values.shape[-1] // 2
    first_half = values[..., :half_width]
    second_half = values[..., half_width:]
    cos_rows = cosine[:, None, :]
    sin_rows = sine_table[:, None, :]
    return jnp.concatenate(
        [
            first_half * cos_rows - second_half * sin_rows,
            second_half * cos_rows + first_half * sin_rows,
        ],
        axis=-1,
    )


def attend_forward(query_seq, key_seq, value_seq, mask):
    rows, head_count, head_width = query_seq.shape
    group_count = key_seq.shape[1]
    repeat = head_count // group_count
    grouped = query_seq.reshape(rows, group_count, repeat, head_width)
    scores = jnp.einsum("qgrd,kgd->grqk", grouped, key_seq, preferred_element_type=f32)
    scores = jnp.where(mask, scores * head_width ** (-0.5), masked_score)
    largest = jnp.max(scores, axis=-1, keepdims=True)
    exp_scores = jnp.exp(scores - largest)
    totals = jnp.sum(exp_scores, axis=-1, keepdims=True)
    probabilities = exp_scores / totals
    log_total = largest + jnp.log(totals)
    mixed = jnp.einsum(
        "grqk,kgd->qgrd", probabilities.astype(bf16), value_seq, preferred_element_type=f32
    )
    return mixed.reshape(rows, head_count * head_width).astype(bf16), log_total


def attend_backward(query_seq, key_seq, value_seq, log_total, grad_mixed, mask):
    rows, head_count, head_width = query_seq.shape
    group_count = key_seq.shape[1]
    repeat = head_count // group_count
    score_scale = head_width ** (-0.5)
    grouped = query_seq.reshape(rows, group_count, repeat, head_width)
    scores = jnp.einsum("qgrd,kgd->grqk", grouped, key_seq, preferred_element_type=f32)
    scores = jnp.where(mask, scores * score_scale, masked_score)
    probabilities = jnp.exp(scores - log_total)
    grad_grouped = grad_mixed.reshape(rows, group_count, repeat, head_width)
    grad_value = jnp.einsum(
        "grqk,qgrd->kgd", probabilities.astype(bf16), grad_grouped, preferred_element_type=f32
    )
    grad_probs = jnp.einsum(
        "qgrd,kgd->grqk", grad_grouped, value_seq, preferred_element_type=f32
    )
    inner_sum = jnp.sum(probabilities * grad_probs, axis=-1, keepdims=True)
    grad_scores = (probabilities * (grad_probs - inner_sum) * score_scale).astype(bf16)
    grad_query = jnp.einsum("grqk,kgd->qgrd", grad_scores, key_seq, preferred_element_type=f32)
    grad_key = jnp.einsum("grqk,qgrd->kgd", grad_scores, grouped, preferred_element_type=f32)
    return grad_query.reshape(rows, head_count, head_width), grad_key, grad_value


def shift(values):
    size = lax.axis_size("tp")
    return lax.ppermute(values, "tp", [(i, (i + 1) % size) for i in range(size)])


def dot(a, b):
    return jnp.dot(a, b, preferred_element_type=f32)


def dot_t(a, b):
    return lax.dot_general(a, b, (((1,), (1,)), ((), ())), preferred_element_type=f32)


def t_dot(a, b):
    return lax.dot_general(a, b, (((0,), (0,)), ((), ())), preferred_element_type=f32)


def gather_weight(values):
    return lax.all_gather(values, "fsdp", axis=0, tiled=True)


def scatter_weight(values):
    return lax.psum_scatter(values.astype(bf16), "fsdp", scatter_dimension=0, tiled=True)


def step(moving, work=None, inputs=()):
    moving, inputs = lax.optimization_barrier((tuple(moving), tuple(inputs)))
    moved = tuple(shift(m) for m in moving)
    results = () if work is None else work(*inputs)
    return lax.optimization_barrier((moved, results))


def butterfly(values, axis, keep_slice):
    size = lax.axis_size(axis)
    me = lax.axis_index(axis)
    bit = size // 2
    while bit:
        pairs = [(i, i ^ bit) for i in range(size)]
        if keep_slice:
            low, high = jnp.split(values, 2, axis=-1)
            upper = (me // bit) % 2 == 1
            mine = jnp.where(upper, high, low)
            values = mine + lax.ppermute(jnp.where(upper, low, high), axis, pairs)
        else:
            values = values + lax.ppermute(values, axis, pairs)
        bit //= 2
    return values


def local(
    tokens,
    cotangent,
    attention_gain,
    query_weight,
    key_weight,
    value_weight,
    output_weight,
    feed_gain,
    gate_weight,
    up_weight,
    down_weight,
):
    layer_count = query_weight.shape[0]
    local_rows = tokens.shape[0]
    size = lax.axis_size("tp")
    me = lax.axis_index("tp")
    group_rows = local_rows * size
    q_width = query_weight.shape[2]
    k_width = key_weight.shape[2]
    head_local = q_width // HD
    group_local = k_width // HD
    qkv_width = q_width + 2 * k_width
    ff = gate_weight.shape[2]
    assert size == 4 and layer_count == 2

    row_index = (
        ((me - jnp.arange(size)) % size)[:, None] * local_rows + jnp.arange(local_rows)[None, :]
    ).reshape(group_rows)
    cosine, sine = angle_tables(row_index % SEQ_LEN)
    mask = (row_index[:, None] >= row_index[None, :]) & (
        (row_index // SEQ_LEN)[:, None] == (row_index // SEQ_LEN)[None, :]
    )

    def attention_shard(l):
        return jnp.concatenate(
            [query_weight[l], key_weight[l], value_weight[l], output_weight[l].T], axis=1
        )

    def feed_shard(l):
        return jnp.concatenate([gate_weight[l], up_weight[l], down_weight[l].T], axis=1)

    def slot(values, s):
        return values[s * local_rows : (s + 1) * local_rows]

    def cat(parts):
        return jnp.concatenate(parts, axis=0)

    def norm_low(values, gain):
        return norm_rows(values, gain).astype(bf16)

    def act_of(gu):
        return swiglu(gu[:, :ff], gu[:, ff:]).astype(bf16)

    def grad_gu_of(gu, grad_act):
        pair = jax.vjp(swiglu, gu[:, :ff], gu[:, ff:])[1](grad_act)
        return jnp.concatenate([p.astype(bf16) for p in pair], axis=1)

    def attention(normed, weights):
        qkv = dot(normed, weights[:, :qkv_width])
        query_used = rotate(
            qkv[:, :q_width].reshape(group_rows, head_local, HD), cosine, sine
        ).astype(bf16)
        key_used = rotate(
            qkv[:, q_width : q_width + k_width].reshape(group_rows, group_local, HD), cosine, sine
        ).astype(bf16)
        value_used = qkv[:, q_width + k_width :].reshape(group_rows, group_local, HD).astype(bf16)
        mixed, log_total = attend_forward(query_used, key_used, value_used, mask)
        return query_used, key_used, value_used, log_total, mixed

    def attention_back(saved, grad_mixed):
        query_used, key_used, value_used, log_total = saved
        grad_query, grad_key, grad_value = attend_backward(
            query_used, key_used, value_used, log_total, grad_mixed, mask
        )
        return jnp.concatenate(
            [
                rotate(grad_query, cosine, -sine).reshape(group_rows, q_width).astype(bf16),
                rotate(grad_key, cosine, -sine).reshape(group_rows, k_width).astype(bf16),
                grad_value.reshape(group_rows, k_width).astype(bf16),
            ],
            axis=1,
        )

    def add_low(moved, part):
        return (moved.astype(f32) + part).astype(bf16)

    weights_a, weights_f = [None, None], [None, None]
    weights_a[0] = gather_weight(attention_shard(0))
    gains = lax.all_gather(
        jnp.concatenate([attention_gain, feed_gain], axis=0), "fsdp", axis=1, tiled=True
    ).astype(f32)
    gain_a, gain_f = gains[:layer_count], gains[layer_count:]
    (t1,), (shard_f0,) = step([tokens], lambda: (feed_shard(0),))
    weights_f[0] = gather_weight(shard_f0)
    (t2,), (shard_a1, shard_f1) = step([t1], lambda: (attention_shard(1), feed_shard(1)))
    weights_a[1] = gather_weight(shard_a1)
    weights_f[1] = gather_weight(shard_f1)
    (t3,), _ = step([t2])
    tokens_all = cat([tokens, t1, t2, t3])
    (c1,), (normed0,) = step(
        [cotangent], lambda t, g: (norm_low(t.astype(f32), g),), (tokens_all, gain_a[0])
    )
    (c2,), att0 = step([c1], attention, (normed0, weights_a[0]))

    residual0 = tokens.astype(f32)

    def attention_out(mixed, weights, residual, movings, fillers):
        wo = weights[:, qkv_width:]
        _, (p1,) = step([], lambda m, w: (dot_t(slot(m, 1), w).astype(bf16),), (mixed, wo))
        (r, *x0), (p2, p3, p0) = step(
            [p1] + movings[0],
            lambda m, w: tuple(dot_t(slot(m, s), w) for s in (2, 3, 0)),
            (mixed, wo),
        )
        (r, *x1), _ = step([add_low(r, p2)] + movings[1])
        (r, *x2), _ = step([add_low(r, p3)] + movings[2])
        return residual + (r.astype(f32) + p0), (x0, x1, x2)

    def feed_forward(hidden, gain, weights):
        def up_of(x, w):
            gu = dot(x, w[:, : 2 * ff])
            return gu, act_of(gu)

        def slot_of(x, w, kind=f32):
            gu, act = up_of(x, w)
            return gu, act, dot_t(act, w[:, 2 * ff :]).astype(kind)

        x0 = norm_low(hidden, gain)
        (x1,), (gu0, act0) = step([x0], up_of, (x0, weights))
        (x2,), (gu1, act1, p1) = step([x1], lambda x, w: slot_of(x, w, bf16), (x1, weights))
        (x3,), (gu2, act2, p2) = step([x2], slot_of, (x2, weights))
        (r,), (gu3, act3, p3) = step([p1], slot_of, (x3, weights))
        (r,), (p0,) = step(
            [add_low(r, p2)], lambda a, w: (dot_t(a, w[:, 2 * ff :]),), (act0, weights)
        )
        (r,), _ = step([add_low(r, p3)])
        return hidden + (r.astype(f32) + p0), [x0, x1, x2, x3], [gu0, gu1, gu2, gu3], [
            act0, act1, act2, act3]

    hidden0, _ = attention_out(att0[-1], weights_a[0], residual0, ([], [], []), None)
    residual1, feed0, gu0, act0 = feed_forward(hidden0, gain_f[0], weights_f[0])

    n0 = norm_low(residual1, gain_a[1])
    (n1,), _ = step([n0])
    (n2,), _ = step([n1])
    (n3,), _ = step([n2])
    normed1 = cat([n0, n1, n2, n3])
    (c3,), att1 = step([c2], attention, (normed1, weights_a[1]))
    cot = [cotangent, c1, c2, c3]
    cot_all = cat(cot)
    hidden1, _ = attention_out(att1[-1], weights_a[1], residual1, ([], [], []), None)

    wf = weights_f[1]

    def up_back(x, g, w):
        gu = dot(x, w[:, : 2 * ff])
        grad_gu = grad_gu_of(gu, g)
        return act_of(gu), grad_gu, dot_t(grad_gu, w[:, : 2 * ff])

    x0 = norm_low(hidden1, gain_f[1])
    (x1,), (grad_act,) = step([x0], lambda c, w: (dot(c, w[:, 2 * ff :]),), (cot_all, wf))
    (x2,), (a1, q1, p1) = step([x1], lambda *t: up_back(*t), (x1, slot(grad_act, 1), wf))
    p1 = p1.astype(bf16)
    (x3,), (a2, q2, p2) = step([x2], up_back, (x2, slot(grad_act, 2), wf))
    (r,), (a3, q3, p3) = step([p1], up_back, (x3, slot(grad_act, 3), wf))
    (r,), (a0, q0, p0) = step([add_low(r, p2)], up_back, (x0, slot(grad_act, 0), wf))
    act1 = [a0, a1, a2, a3]
    feed1 = [x0, x1, x2, x3]
    grad_gu1 = [q0, q1, q2, q3]

    def outer(a, b):
        return (t_dot(cat(a), cat(b)).astype(bf16),)

    (r,), (down_part1,) = step([add_low(r, p3)], lambda *v: outer(v[:4], v[4:]), cot + act1)
    down_grad1 = scatter_weight(down_part1)
    grad_normed = r.astype(f32) + p0
    grad_hidden, feed_gain_part1 = jax.vjp(norm_rows, hidden1, gain_f[1])[1](grad_normed)
    grad_resid = cotangent.astype(f32) + grad_hidden

    def attention_grads(m0, saved, normed, weights, mixed, fill, fill_inputs, low, low_work):
        wo = weights[:, qkv_width:]
        wq = weights[:, :qkv_width]
        (m1,), f0 = step([m0], fill[0], fill_inputs[0])
        (m2,), f1 = step([m1], fill[1], fill_inputs[1])
        (m3,), f2 = step([m2], fill[2], fill_inputs[2])
        mid_all = cat([m0, m1, m2, m3])
        moved, (grad_qkv, p1) = step(
            low,
            lambda s, m, w, v: (
                lambda g: (g, dot_t(slot(g, 1), v).astype(bf16))
            )(attention_back(s, dot(m, w).astype(bf16))),
            (saved, mid_all, wo, wq),
        )
        (r,), (p2, p3, p0, out_part) = step(
            [p1],
            lambda g, w, a, m: tuple(dot_t(slot(g, s), w) for s in (2, 3, 0))
            + (t_dot(a, m).astype(bf16),),
            (grad_qkv, wq, mid_all, mixed),
        )
        (r,), (qkv_part,) = step(
            [add_low(r, p2)], lambda a, g: (t_dot(a, g).astype(bf16),), (normed, grad_qkv)
        )
        attention_grad = scatter_weight(jnp.concatenate([qkv_part, out_part], axis=1))
        (r,), f3 = step([add_low(r, p3)], fill[3], fill_inputs[3])
        return r.astype(f32) + p0, attention_grad, moved, f0, f1, f2, f3

    none = (None, ())
    grad_normed, attention_grad1, low, (gu_part1,), (low1,), (low2, low3, low0), _ = (
        attention_grads(
            grad_resid.astype(bf16),
            att1[:4],
            normed1,
            weights_a[1],
            att1[4],
            (
                lambda *v: outer(v[:4], v[4:]),
                lambda a, w: (dot_t(a, w[:, 2 * ff :]).astype(bf16),),
                lambda a, b, c, w: tuple(dot_t(v, w[:, 2 * ff :]) for v in (a, b, c)),
                None,
            ),
            (tuple(feed1 + grad_gu1), (act1[1], wf), (act1[2], act1[3], act1[0], wf), ()),
            [],
            None,
        )
    )
    gu_grad1 = scatter_weight(gu_part1)
    grad_before, attention_gain_part1 = jax.vjp(norm_rows, residual1, gain_a[1])[1](grad_normed)
    grad_resid = grad_resid + grad_before

    wf = weights_f[0]

    def back_of(g, gu, w):
        grad_gu = grad_gu_of(gu, dot(g, w[:, 2 * ff :]))
        return grad_gu, dot_t(grad_gu, w[:, : 2 * ff])

    g0 = grad_resid.astype(bf16)
    (g1,), (q0, p0) = step([g0], back_of, (g0, gu0[0], wf))
    (g2,), (q1, p1) = step([g1], back_of, (g1, gu0[1], wf))
    p1 = p1.astype(bf16)
    (g3,), (q2, p2) = step([g2], back_of, (g2, gu0[2], wf))
    (r,), (q3, p3) = step([p1], back_of, (g3, gu0[3], wf))
    (r,), (down_part0,) = step(
        [add_low(r, p2)], lambda *v: outer(v[:4], v[4:]), [g0, g1, g2, g3] + act0
    )
    down_grad0 = scatter_weight(down_part0)
    (r,), (gu_part0,) = step(
        [add_low(r, p3)], lambda *v: outer(v[:4], v[4:]), feed0 + [q0, q1, q2, q3]
    )
    gu_grad0 = scatter_weight(gu_part0)
    grad_normed = r.astype(f32) + p0
    grad_hidden, feed_gain_part0 = jax.vjp(norm_rows, hidden0, gain_f[0])[1](grad_normed)
    grad_resid = grad_resid + grad_hidden

    grad_normed, attention_grad0, (lowr,), _, _, _, _ = attention_grads(
        grad_resid.astype(bf16),
        att0[:4],
        normed0,
        weights_a[0],
        att0[4],
        (None,) * 4,
        ((),) * 4,
        [low1],
        None,
    )
    (lowr,), _ = step([add_low(lowr, low2)])
    (lowr,), _ = step([add_low(lowr, low3)])
    block_out = (hidden1 + (lowr.astype(f32) + low0)).astype(bf16)
    grad_before, attention_gain_part0 = jax.vjp(norm_rows, residual0, gain_a[0])[1](grad_normed)
    grad_resid = grad_resid + grad_before

    gain_sums = jnp.stack(
        [attention_gain_part0, attention_gain_part1, feed_gain_part0, feed_gain_part1]
    )
    gain_sums = butterfly(butterfly(gain_sums, "fsdp", True), "tp", False)
    att_grads = [attention_grad0.astype(f32), attention_grad1.astype(f32)]
    gu_grads = [gu_grad0, gu_grad1]
    down_grads = [down_grad0, down_grad1]
    return (
        block_out,
        grad_resid,
        gain_sums[:layer_count],
        jnp.stack([p[:, :q_width] for p in att_grads]),
        jnp.stack([p[:, q_width : q_width + k_width] for p in att_grads]),
        jnp.stack([p[:, q_width + k_width : qkv_width] for p in att_grads]),
        jnp.stack([p[:, qkv_width:].T for p in att_grads]),
        gain_sums[layer_count:],
        jnp.stack([g[:, :ff].astype(f32) for g in gu_grads]),
        jnp.stack([g[:, ff:].astype(f32) for g in gu_grads]),
        jnp.stack([g.astype(f32).T for g in down_grads]),
    )


def solution(mesh):
    rows = P(("fsdp", "tp"), None)
    gain = P(None, "fsdp")
    column = P(None, "fsdp", "tp")
    row = P(None, "tp", "fsdp")
    weights = (gain, column, column, column, row, gain, column, column, row)
    return jax.shard_map(
        local,
        mesh=mesh,
        in_specs=(rows, rows) + weights,
        out_specs=(rows, rows) + weights,
        check_vma=False,
    )
```

```python
import jax
import jax.numpy as jnp
from jax import lax
from jax.experimental import pallas as pl
from jax.experimental.pallas import tpu as pltpu
from jax.sharding import PartitionSpec as P

HD = 64
SEQ_LEN = 512
epsilon = 1e-05
theta = 10000.0
masked_score = -1e30
f32 = jnp.float32
bf16 = jnp.bfloat16


def norm_rows(residual, scales):
    inverse = lax.rsqrt(jnp.mean(residual * residual, axis=-1, keepdims=True) + epsilon)
    return residual * inverse * scales


def swiglu(gate_lin, up_lin):
    return jax.nn.silu(gate_lin) * up_lin


def angle_tables(positions):
    half_width = HD // 2
    exponent = 2.0 * jnp.arange(half_width).astype(f32) / HD
    frequency = theta ** (-exponent)
    angles = positions.astype(f32)[:, None] * frequency[None, :]
    return jnp.cos(angles), jnp.sin(angles)


def rotate(values, cosine, sine_table):
    half_width = values.shape[-1] // 2
    first_half = values[..., :half_width]
    second_half = values[..., half_width:]
    cos_rows = cosine[:, None, :]
    sin_rows = sine_table[:, None, :]
    return jnp.concatenate(
        [
            first_half * cos_rows - second_half * sin_rows,
            second_half * cos_rows + first_half * sin_rows,
        ],
        axis=-1,
    )


def attend_forward(query_seq, key_seq, value_seq, mask):
    rows, head_count, head_width = query_seq.shape
    group_count = key_seq.shape[1]
    repeat = head_count // group_count
    grouped = query_seq.reshape(rows, group_count, repeat, head_width)
    scores = jnp.einsum("qgrd,kgd->grqk", grouped, key_seq, preferred_element_type=f32)
    scores = jnp.where(mask, scores * head_width ** (-0.5), masked_score)
    largest = jnp.max(scores, axis=-1, keepdims=True)
    exp_scores = jnp.exp(scores - largest)
    totals = jnp.sum(exp_scores, axis=-1, keepdims=True)
    probabilities = exp_scores / totals
    log_total = largest + jnp.log(totals)
    mixed = jnp.einsum(
        "grqk,kgd->qgrd", probabilities.astype(bf16), value_seq, preferred_element_type=f32
    )
    return mixed.reshape(rows, head_count * head_width).astype(bf16), log_total


def attend_backward(query_seq, key_seq, value_seq, log_total, grad_mixed, mask):
    rows, head_count, head_width = query_seq.shape
    group_count = key_seq.shape[1]
    repeat = head_count // group_count
    score_scale = head_width ** (-0.5)
    grouped = query_seq.reshape(rows, group_count, repeat, head_width)
    scores = jnp.einsum("qgrd,kgd->grqk", grouped, key_seq, preferred_element_type=f32)
    scores = jnp.where(mask, scores * score_scale, masked_score)
    probabilities = jnp.exp(scores - log_total)
    grad_grouped = grad_mixed.reshape(rows, group_count, repeat, head_width)
    grad_value = jnp.einsum(
        "grqk,qgrd->kgd", probabilities.astype(bf16), grad_grouped, preferred_element_type=f32
    )
    grad_probs = jnp.einsum(
        "qgrd,kgd->grqk", grad_grouped, value_seq, preferred_element_type=f32
    )
    inner_sum = jnp.sum(probabilities * grad_probs, axis=-1, keepdims=True)
    grad_scores = (probabilities * (grad_probs - inner_sum) * score_scale).astype(bf16)
    grad_query = jnp.einsum("grqk,kgd->qgrd", grad_scores, key_seq, preferred_element_type=f32)
    grad_key = jnp.einsum("grqk,qgrd->kgd", grad_scores, grouped, preferred_element_type=f32)
    return grad_query.reshape(rows, head_count, head_width), grad_key, grad_value


def shift(values):
    size = lax.axis_size("tp")
    return lax.ppermute(values, "tp", [(i, (i + 1) % size) for i in range(size)])


def dot(a, b):
    return jnp.dot(a, b, preferred_element_type=f32)


def dot_t(a, b):
    return lax.dot_general(a, b, (((1,), (1,)), ((), ())), preferred_element_type=f32)


def t_dot(a, b):
    return lax.dot_general(a, b, (((0,), (0,)), ((), ())), preferred_element_type=f32)


def thin_cost():
    return pl.CostEstimate(flops=1, bytes_accessed=1, transcendentals=0)


def run_kernel(body, grid, in_specs, out_specs, out_shape, args, scratch=()):
    return pl.pallas_call(
        body,
        grid=(grid,),
        in_specs=in_specs,
        out_specs=out_specs,
        out_shape=out_shape,
        scratch_shapes=scratch,
        cost_estimate=thin_cost(),
        compiler_params=pltpu.CompilerParams(
            dimension_semantics=("arbitrary",), vmem_limit_bytes=48 * 1024 * 1024
        ),
    )(*args)


TILE = 1024
OUTER_TILE = 512


def swiglu_back(gate, up, grad):
    sig = 1.0 / (1.0 + jnp.exp(-gate))
    return grad * up * (sig * (1.0 + gate * (1.0 - sig))), grad * (gate * sig), gate * sig * up


def pair_forward(xa, xb, weights):
    rows, features = xa.shape
    ff = weights.shape[1] // 3
    n = features // TILE

    def body(xa, xb, wgu, wd, gu, act, pa, pb):
        i = pl.program_id(0)

        @pl.when(i == 0)
        def _():
            gu[...] = jnp.zeros(gu.shape, f32)

        @pl.when(i < n)
        def _():
            gu[...] += dot(jnp.concatenate([xa[...], xb[...]], axis=0), wgu[...])

        @pl.when(i == n - 1)
        def _():
            gate = gu[:, :ff]
            act[...] = (gate / (1.0 + jnp.exp(-gate)) * gu[:, ff:]).astype(bf16)

        @pl.when(i >= n)
        def _():
            part = dot_t(act[...], wd[...])
            pa[...] = part[:rows].astype(bf16)
            pb[...] = part[rows:].astype(bf16)

    early = lambda i: jnp.minimum(i, n - 1)
    late = lambda i: jnp.maximum(i - n, 0)
    return run_kernel(
        body,
        2 * n,
        [
            pl.BlockSpec((rows, TILE), lambda i: (0, early(i))),
            pl.BlockSpec((rows, TILE), lambda i: (0, early(i))),
            pl.BlockSpec((TILE, 2 * ff), lambda i: (early(i), 0)),
            pl.BlockSpec((TILE, ff), lambda i: (late(i), 2)),
        ],
        [
            pl.BlockSpec((2 * rows, 2 * ff), lambda i: (0, 0)),
            pl.BlockSpec((2 * rows, ff), lambda i: (0, 0)),
            pl.BlockSpec((rows, TILE), lambda i: (0, late(i))),
            pl.BlockSpec((rows, TILE), lambda i: (0, late(i))),
        ],
        [
            jax.ShapeDtypeStruct((2 * rows, 2 * ff), f32),
            jax.ShapeDtypeStruct((2 * rows, ff), bf16),
            jax.ShapeDtypeStruct((rows, features), bf16),
            jax.ShapeDtypeStruct((rows, features), bf16),
        ],
        (xa, xb, weights, weights),
    )


def pair_up_back(xa, xb, grad_act, which, weights):
    rows, features = xa.shape
    ff = weights.shape[1] // 3
    n = features // TILE

    def body(xa, xb, ga, w, act, grads, pa, pb, gu):
        i = pl.program_id(0)

        @pl.when(i == 0)
        def _():
            gu[...] = jnp.zeros(gu.shape, f32)

        @pl.when(i < n)
        def _():
            gu[...] += dot(jnp.concatenate([xa[...], xb[...]], axis=0), w[...])

        @pl.when(i == n - 1)
        def _():
            dgate, dup, a = swiglu_back(gu[:, :ff], gu[:, ff:], ga[...])
            grads[:, :ff] = dgate.astype(bf16)
            grads[:, ff:] = dup.astype(bf16)
            act[...] = a.astype(bf16)

        @pl.when(i >= n)
        def _():
            part = dot_t(grads[...], w[...])
            pa[...] = part[:rows].astype(bf16)
            pb[...] = part[rows:].astype(bf16)

    early = lambda i: jnp.minimum(i, n - 1)
    late = lambda i: jnp.maximum(i - n, 0)
    return run_kernel(
        body,
        2 * n,
        [
            pl.BlockSpec((rows, TILE), lambda i: (0, early(i))),
            pl.BlockSpec((rows, TILE), lambda i: (0, early(i))),
            pl.BlockSpec((2 * rows, ff), lambda i: (which, 0)),
            pl.BlockSpec((TILE, 2 * ff), lambda i: (i % n, 0)),
        ],
        [
            pl.BlockSpec((2 * rows, ff), lambda i: (0, 0)),
            pl.BlockSpec((2 * rows, 2 * ff), lambda i: (0, 0)),
            pl.BlockSpec((rows, TILE), lambda i: (0, late(i))),
            pl.BlockSpec((rows, TILE), lambda i: (0, late(i))),
        ],
        [
            jax.ShapeDtypeStruct((2 * rows, ff), bf16),
            jax.ShapeDtypeStruct((2 * rows, 2 * ff), bf16),
            jax.ShapeDtypeStruct((rows, features), bf16),
            jax.ShapeDtypeStruct((rows, features), bf16),
        ],
        (xa, xb, grad_act, weights),
        (pltpu.VMEM((2 * rows, 2 * ff), f32),),
    )


def pair_back(ga, gb, gu, weights):
    rows, features = ga.shape
    ff = weights.shape[1] // 3
    n = features // TILE

    def body(ga, gb, gu, wd, wgu, grads, pa, pb, acc):
        i = pl.program_id(0)

        @pl.when(i == 0)
        def _():
            acc[...] = jnp.zeros(acc.shape, f32)

        @pl.when(i < n)
        def _():
            acc[...] += dot(jnp.concatenate([ga[...], gb[...]], axis=0), wd[...])

        @pl.when(i == n - 1)
        def _():
            dgate, dup, _ = swiglu_back(gu[:, :ff], gu[:, ff:], acc[...])
            grads[:, :ff] = dgate.astype(bf16)
            grads[:, ff:] = dup.astype(bf16)

        @pl.when(i >= n)
        def _():
            part = dot_t(grads[...], wgu[...])
            pa[...] = part[:rows].astype(bf16)
            pb[...] = part[rows:].astype(bf16)

    early = lambda i: jnp.minimum(i, n - 1)
    late = lambda i: jnp.maximum(i - n, 0)
    return run_kernel(
        body,
        2 * n,
        [
            pl.BlockSpec((rows, TILE), lambda i: (0, early(i))),
            pl.BlockSpec((rows, TILE), lambda i: (0, early(i))),
            pl.BlockSpec((2 * rows, 2 * ff), lambda i: (0, 0)),
            pl.BlockSpec((TILE, ff), lambda i: (early(i), 2)),
            pl.BlockSpec((TILE, 2 * ff), lambda i: (late(i), 0)),
        ],
        [
            pl.BlockSpec((2 * rows, 2 * ff), lambda i: (0, 0)),
            pl.BlockSpec((rows, TILE), lambda i: (0, late(i))),
            pl.BlockSpec((rows, TILE), lambda i: (0, late(i))),
        ],
        [
            jax.ShapeDtypeStruct((2 * rows, 2 * ff), bf16),
            jax.ShapeDtypeStruct((rows, features), bf16),
            jax.ShapeDtypeStruct((rows, features), bf16),
        ],
        (ga, gb, gu, weights, weights),
        (pltpu.VMEM((2 * rows, ff), f32),),
    )


def outer(slots, pairs, parts=1):
    rows, features = slots[0].shape
    width = pairs[0].shape[1] // parts

    def body(s0, s1, s2, s3, b0, b1, *outs):
        first = jnp.concatenate([s0[...], s1[...]], axis=0)
        second = jnp.concatenate([s2[...], s3[...]], axis=0)
        for index, out in enumerate(outs):
            at = slice(index * width, (index + 1) * width)
            out[...] = (t_dot(first, b0[:, at]) + t_dot(second, b1[:, at])).astype(bf16)

    return run_kernel(
        body,
        features // OUTER_TILE,
        [pl.BlockSpec((rows, OUTER_TILE), lambda i: (0, i)) for _ in slots]
        + [pl.BlockSpec((2 * rows, parts * width), lambda i: (0, 0)) for _ in pairs],
        [pl.BlockSpec((OUTER_TILE, width), lambda i: (i, 0)) for _ in range(parts)],
        [jax.ShapeDtypeStruct((features, width), bf16) for _ in range(parts)],
        (*slots, *pairs),
    )


def gather_weight(values):
    return lax.all_gather(values, "fsdp", axis=0, tiled=True)


def scatter_weight(values):
    return lax.psum_scatter(values.astype(bf16), "fsdp", scatter_dimension=0, tiled=True)


def step(moving, work=None, inputs=(), launch=(), land=()):
    moving, inputs, sent = lax.optimization_barrier(
        (tuple(moving), tuple(inputs), tuple(a for a, _ in launch))
    )
    moved = tuple(shift(m) for m in moving)
    flying = tuple(exchange(a, bit) for a, (_, bit) in zip(sent, launch))
    results = () if work is None else work(*inputs)
    moved, results, landed = lax.optimization_barrier((moved, results, tuple(land)))
    return moved, results, flying, landed


def exchange(values, bit, axis="fsdp"):
    size = lax.axis_size(axis)
    return lax.ppermute(values, axis, [(i, i ^ (1 << bit)) for i in range(size)])


def fsdp_bits():
    count = lax.axis_size("fsdp").bit_length() - 1
    width = (count - 1) // 2
    return [0], list(range(1, 1 + width)), list(range(1 + width, count))


def my_bit(bit):
    return (lax.axis_index("fsdp") // (1 << bit)) % 2


class Scatter:
    def __init__(self, partial, order):
        bits = [b for phase in order for b in phase]
        self.left = sorted(bits, reverse=True)
        size = lax.axis_size("fsdp")
        rows, width = partial.shape
        self.values = partial.reshape((2,) * len(bits) + (rows // size, width))
        self.order = [b for phase in order for b in phase]

    def half(self, values, other):
        bit = self.order[0]
        which = 1 - my_bit(bit) if other else my_bit(bit)
        return lax.dynamic_index_in_dim(values, which, self.left.index(bit), keepdims=False)

    def send(self):
        return self.half(self.values, True)

    def add(self, values, arrived):
        return (self.half(values, False).astype(f32) + arrived.astype(f32)).astype(bf16)

    def advance(self, values):
        self.left.remove(self.order.pop(0))
        self.values = values

    @property
    def bit(self):
        return self.order[0]


def sum_all(values, axis):
    for bit in range(lax.axis_size(axis).bit_length() - 1):
        values = values + exchange(values, bit, axis)
    return values


def sum_to_owner(values):
    for bit in reversed(range(lax.axis_size("fsdp").bit_length() - 1)):
        low, high = jnp.split(values, 2, axis=-1)
        upper = my_bit(bit) == 1
        values = jnp.where(upper, high, low) + exchange(jnp.where(upper, low, high), bit)
    return values


def local(
    tokens,
    cotangent,
    attention_gain,
    query_weight,
    key_weight,
    value_weight,
    output_weight,
    feed_gain,
    gate_weight,
    up_weight,
    down_weight,
):
    layer_count = query_weight.shape[0]
    local_rows = tokens.shape[0]
    size = lax.axis_size("tp")
    me = lax.axis_index("tp")
    group_rows = local_rows * size
    q_width = query_weight.shape[2]
    k_width = key_weight.shape[2]
    head_local = q_width // HD
    group_local = k_width // HD
    qkv_width = q_width + 2 * k_width
    ff = gate_weight.shape[2]
    assert size == 4 and layer_count == 2

    row_index = (
        ((me - jnp.arange(size)) % size)[:, None] * local_rows + jnp.arange(local_rows)[None, :]
    ).reshape(group_rows)
    cosine, sine = angle_tables(row_index % SEQ_LEN)
    mask = (row_index[:, None] >= row_index[None, :]) & (
        (row_index // SEQ_LEN)[:, None] == (row_index // SEQ_LEN)[None, :]
    )

    core, xs, ys = fsdp_bits()
    me_f = lax.axis_index("fsdp")
    shards = lax.axis_size("fsdp")
    shard_rows = query_weight.shape[1]
    features = shards * shard_rows

    def attention_shard(l):
        return jnp.concatenate(
            [query_weight[l], key_weight[l], value_weight[l], output_weight[l].T], axis=1
        )

    def feed_shard(l):
        return jnp.concatenate([gate_weight[l], up_weight[l], down_weight[l].T], axis=1)

    def slot(values, s):
        return values[s * local_rows : (s + 1) * local_rows]

    def cat(parts):
        return jnp.concatenate(parts, axis=0)

    def norm_low(values, gain):
        return norm_rows(values, gain).astype(bf16)

    def act_of(gu):
        return swiglu(gu[:, :ff], gu[:, ff:]).astype(bf16)

    def grad_gu_of(gu, grad_act):
        pair = jax.vjp(swiglu, gu[:, :ff], gu[:, ff:])[1](grad_act)
        return jnp.concatenate([p.astype(bf16) for p in pair], axis=1)

    def attention(normed, wqkv):
        qkv = dot(normed, wqkv)
        query_used = rotate(
            qkv[:, :q_width].reshape(group_rows, head_local, HD), cosine, sine
        ).astype(bf16)
        key_used = rotate(
            qkv[:, q_width : q_width + k_width].reshape(group_rows, group_local, HD), cosine, sine
        ).astype(bf16)
        value_used = qkv[:, q_width + k_width :].reshape(group_rows, group_local, HD).astype(bf16)
        mixed, log_total = attend_forward(query_used, key_used, value_used, mask)
        return query_used, key_used, value_used, log_total, mixed

    def attention_back(saved, grad_mixed):
        query_used, key_used, value_used, log_total = saved
        grad_query, grad_key, grad_value = attend_backward(
            query_used, key_used, value_used, log_total, grad_mixed, mask
        )
        return jnp.concatenate(
            [
                rotate(grad_query, cosine, -sine).reshape(group_rows, q_width).astype(bf16),
                rotate(grad_key, cosine, -sine).reshape(group_rows, k_width).astype(bf16),
                grad_value.reshape(group_rows, k_width).astype(bf16),
            ],
            axis=1,
        )

    def add_low(moved, part):
        return (moved.astype(f32) + part).astype(bf16)

    weights_a0 = gather_weight(attention_shard(0))
    gains = jnp.zeros((shards, 2 * layer_count, shard_rows), bf16)
    gains = lax.dynamic_update_slice(
        gains, jnp.concatenate([attention_gain, feed_gain], axis=0)[None], (me_f, 0, 0)
    )
    bits = core + xs + ys

    def with_gains(count, work=lambda: ()):
        def found(gains):
            for bit in bits[:count]:
                gains = gains + exchange(gains, bit)
            del bits[:count]
            return (gains, *work())

        return found

    (t1,), (gains, shard_f0), _, _ = step(
        [tokens], with_gains(1, lambda: (feed_shard(0),)), (gains,)
    )
    weights_f = [gather_weight(shard_f0), None]
    (t2,), (gains, shard_a1), _, _ = step(
        [t1], with_gains(1, lambda: (attention_shard(1),)), (gains,)
    )
    (t3,), (gains, shard_f1), _, _ = step(
        [t2], with_gains(len(bits), lambda: (feed_shard(1),)), (gains,)
    )
    weights_a1 = gather_weight(shard_a1)
    gains = jnp.moveaxis(gains.astype(f32), 0, 1).reshape(2 * layer_count, features)
    gain_a, gain_f = gains[:layer_count], gains[layer_count:]
    (c1,), (normed0, wqkv0, wo0), _, _ = step(
        [cotangent],
        lambda g, v, *t: (
            norm_low(cat(t).astype(f32), g), v[:, :qkv_width], v[:, qkv_width:]
        ),
        (gain_a[0], weights_a0, tokens, t1, t2, t3),
    )
    (c2,), att0, _, _ = step([c1], attention, (normed0, wqkv0))
    weights_f[1] = gather_weight(shard_f1)

    residual0 = tokens.astype(f32)

    def attention_out(mixed, wo, residual, work=None, inputs=()):
        _, (p1,), _, _ = step([], lambda m, w: (dot_t(slot(m, 1), w).astype(bf16),), (mixed, wo))
        (r,), (p2, p3, p0), _, _ = step(
            [p1], lambda m, w: tuple(dot_t(slot(m, s), w) for s in (2, 3, 0)), (mixed, wo)
        )
        (r,), extra, _, _ = step([add_low(r, p2)], work, inputs)
        (r,), _, _, _ = step([add_low(r, p3)])
        return residual + (r.astype(f32) + p0), extra

    hidden0, _ = attention_out(att0[-1], wo0, residual0)

    w = weights_f[0]
    x0 = norm_low(hidden0, gain_f[0])
    (x1,), _, _, _ = step([x0])
    (x2,), _, _, _ = step([x1])
    (x3,), _, _, _ = step([x2])
    _, (gu01, act01, p0, p1), _, _ = step([], pair_forward, (x0, x1, w))
    (r,), (gu23, act23, p2, p3), _, _ = step([p1], pair_forward, (x2, x3, w))
    (r,), (wqkv1, wo1), _, _ = step(
        [add_low(r, p2)], lambda v: (v[:, :qkv_width], v[:, qkv_width:]), (weights_a1,)
    )
    (r,), _, _, _ = step([add_low(r, p3)])
    residual1 = hidden0 + (r.astype(f32) + p0)
    feed0, gu0, act0 = [x0, x1, x2, x3], [gu01, gu23], [act01, act23]

    n0 = norm_low(residual1, gain_a[1])
    (n1,), _, _, _ = step([n0])
    (n2,), _, _, _ = step([n1])
    (n3,), _, _, _ = step([n2])
    normed1 = cat([n0, n1, n2, n3])
    (c3,), att1, _, _ = step([c2], attention, (normed1, wqkv1))
    cot_all = cat([cotangent, c1, c2, c3])
    hidden1, (grad_act,) = attention_out(
        att1[-1],
        wo1,
        residual1,
        lambda c, v: (dot(c, v[:, 2 * ff :]),),
        (cot_all, weights_f[1]),
    )

    w = weights_f[1]

    x0 = norm_low(hidden1, gain_f[1])
    (x1,), _, _, _ = step([x0])
    (x2,), (a01, q01, p0, p1), _, _ = step(
        [x1], lambda x, y, g, v: pair_up_back(x, y, g, 0, v), (x0, x1, grad_act, w)
    )
    (x3,), _, _, _ = step([x2])
    (r,), (a23, q23, p2, p3), _, _ = step(
        [p1], lambda x, y, g, v: pair_up_back(x, y, g, 1, v), (x2, x3, grad_act, w)
    )
    cots = [cotangent, c1, c2, c3]
    (r,), (down_part1,), _, _ = step(
        [add_low(r, p2)], lambda *v: outer(v[:4], v[4:]), (*cots, a01, a23)
    )
    down_grad1 = scatter_weight(down_part1)
    (r,), (gu_part1,), _, _ = step(
        [add_low(r, p3)],
        lambda *v: outer(v[:4], v[4:]),
        (x0, x1, x2, x3, q01, q23),
    )
    gu_grad1 = scatter_weight(gu_part1)
    grad_normed = r.astype(f32) + p0
    grad_hidden, feed_gain_part1 = jax.vjp(norm_rows, hidden1, gain_f[1])[1](grad_normed)
    grad_resid = cotangent.astype(f32) + grad_hidden

    def back_parts(saved, m, wo, wqkv):
        g = attention_back(saved, dot(m, wo).astype(bf16))
        return g, dot_t(slot(g, 1), wqkv).astype(bf16)

    def rest_parts(g, wqkv, normed, m, mixed):
        return tuple(dot_t(slot(g, s), wqkv) for s in (2, 3, 0)) + (
            t_dot(normed, g).astype(bf16),
            t_dot(m, mixed).astype(bf16),
        )

    m0 = grad_resid.astype(bf16)
    (m1,), (low,), _, _ = step(
        [m0], lambda a, b, w: (dot_t(cat([a, b]), w[:, 2 * ff :]),), (a01, a23, w)
    )
    low0, low1, low2, low3 = (slot(low, s) for s in range(4))
    (m2,), _, _, _ = step([m1])
    (m3,), _, _, _ = step([m2])
    mid = cat([m0, m1, m2, m3])
    (lowr,), (g, p1), _, _ = step(
        [low1.astype(bf16)], back_parts, (att1[:4], mid, wo1, wqkv1)
    )
    (r,), (p2, p3, p0, qkv_part, out_part), _, (down_grad1,) = step(
        [p1], rest_parts, (g, wqkv1, normed1, mid, att1[4]), land=(down_grad1,)
    )
    attention_grad1 = scatter_weight(jnp.concatenate([qkv_part, out_part], axis=1))
    (r,), _, _, _ = step([add_low(r, p2)])
    (r,), _, _, _ = step([add_low(r, p3)])
    grad_normed = r.astype(f32) + p0
    grad_before, attention_gain_part1 = jax.vjp(norm_rows, residual1, gain_a[1])[1](grad_normed)
    grad_resid = grad_resid + grad_before

    w = weights_f[0]

    g0 = grad_resid.astype(bf16)
    (g1,), _, _, _ = step([g0])
    (g2,), (q01, p0, p1), _, _ = step([g1], pair_back, (g0, g1, gu0[0], w))
    (g3,), _, _, _ = step([g2])
    (r,), (q23, p2, p3), _, (gu_grad1,) = step(
        [p1], pair_back, (g2, g3, gu0[1], w), land=(gu_grad1,)
    )
    (r,), (down_part0,), _, _ = step(
        [add_low(r, p2)], lambda *v: outer(v[:4], v[4:]), (g0, g1, g2, g3, *act0)
    )
    down_grad0 = scatter_weight(down_part0)

    def gate_up(*v):
        found = [
            Scatter(part, order)
            for part, order in zip(
                outer(v[:4], v[4:], 2), ((core, ys, xs), (core, xs, ys))
            )
        ]
        return tuple(s.values for s in found) + tuple(s.send() for s in found)

    (r,), (gate_v, up_v, gate_s, up_s), _, _ = step(
        [add_low(r, p3)], gate_up, (*feed0, q01, q23)
    )
    order_a, order_b = (core, ys, xs), (core, xs, ys)

    def tracker(values, order):
        s = Scatter(jnp.zeros((features, 1), bf16), order)
        s.values = values
        return s

    gate_t, up_t = tracker(gate_v, order_a), tracker(up_v, order_b)

    def turn(track, values, arrived):
        values = track.add(values, arrived)
        track.advance(values)
        return values, track.send() if track.order else values

    def turn_all(tracks):
        def work(*v):
            results = []
            for index, track in enumerate(tracks):
                results += turn(track, v[2 * index], v[2 * index + 1])
            return tuple(results)

        return work

    grad_normed = r.astype(f32) + p0
    grad_hidden, feed_gain_part0 = jax.vjp(norm_rows, hidden0, gain_f[0])[1](grad_normed)
    grad_resid = grad_resid + grad_hidden

    m0 = grad_resid.astype(bf16)
    (m1,), (gate_r, up_r), _, _ = step(
        [m0], lambda a, b: (exchange(a, 0), exchange(b, 0)), (gate_s, up_s)
    )
    (m2,), (gate_v, gate_s, up_v, up_s), _, _ = step(
        [m1], turn_all([gate_t, up_t]), (gate_v, gate_r, up_v, up_r)
    )
    bits = (gate_t.bit, up_t.bit)
    (m3,), _, flying, _ = step([m2], launch=((gate_s, bits[0]), (up_s, bits[1])))
    mid = cat([m0, m1, m2, m3])
    (lowr,), (g, p1), _, (gate_r, up_r) = step(
        [add_low(lowr, low2)], back_parts, (att0[:4], mid, wo0, wqkv0), land=flying
    )

    def parts_and_turn(*v):
        return rest_parts(*v[:5]) + turn_all([gate_t, up_t])(*v[5:])

    (r,), (p2, p3, p0, qkv_part, out_part, gate_v, gate_s, up_v, up_s), _, (attention_grad1,) = (
        step(
            [p1],
            parts_and_turn,
            (g, wqkv0, normed0, mid, att0[4], gate_v, gate_r, up_v, up_r),
            land=(attention_grad1,),
        )
    )

    def run_down(track, values, send):
        while len(track.order) > 1:
            values = track.add(values, exchange(send, track.bit))
            track.advance(values)
            send = track.send()
        return values, send

    gate_v, gate_s = run_down(gate_t, gate_v, gate_s)
    up_v, up_s = run_down(up_t, up_v, up_s)
    qkv_t, out_t = Scatter(qkv_part, order_a), Scatter(out_part, order_b)
    bits = (gate_t.bit, up_t.bit)
    (r,), (qkv_r, out_r), flying, _ = step(
        [add_low(r, p2)],
        lambda a, b: (exchange(a, 0), exchange(b, 0)),
        (qkv_t.send(), out_t.send()),
        launch=((gate_s, bits[0]), (up_s, bits[1])),
    )
    (r,), (qkv_v, qkv_s, out_v, out_s), _, (gate_r, up_r) = step(
        [add_low(r, p3)],
        turn_all([qkv_t, out_t]),
        (qkv_t.values, qkv_r, out_t.values, out_r),
        land=flying,
    )

    bits = (qkv_t.bit, out_t.bit)

    def last_norm(r, p0, grad_resid, gate_v, gate_r, up_v, up_r):
        grad_before, gain_part = jax.vjp(norm_rows, residual0, gain_a[0])[1](r.astype(f32) + p0)
        return (
            grad_resid + grad_before,
            gain_part,
            gate_t.add(gate_v, gate_r),
            up_t.add(up_v, up_r),
        )

    (lowr,), (grad_resid, attention_gain_part0, gate_grad0, up_grad0), _, (qkv_r, out_r) = step(
        [add_low(lowr, low3)],
        lambda *v: last_norm(*v[2:]) ,
        (qkv_s, out_s, r, p0, grad_resid, gate_v, gate_r, up_v, up_r),
        land=(exchange(qkv_s, bits[0]), exchange(out_s, bits[1])),
    )
    block_out = (hidden1 + (lowr.astype(f32) + low0)).astype(bf16)
    qkv_v, qkv_s = turn(qkv_t, qkv_v, qkv_r)
    out_v, out_s = turn(out_t, out_v, out_r)
    qkv_v, qkv_s = run_down(qkv_t, qkv_v, qkv_s)
    out_v, out_s = run_down(out_t, out_v, out_s)
    qkv_grad0 = qkv_t.add(qkv_v, exchange(qkv_s, qkv_t.bit)).astype(f32)
    out_grad0 = out_t.add(out_v, exchange(out_s, out_t.bit)).astype(f32)

    gain_sums = jnp.stack(
        [attention_gain_part0, attention_gain_part1, feed_gain_part0, feed_gain_part1]
    )
    gain_sums = sum_all(sum_to_owner(gain_sums), "tp")
    qkv_grad1 = attention_grad1[:, :qkv_width].astype(f32)
    out_grad1 = attention_grad1[:, qkv_width:].astype(f32)
    qkv_grads = [qkv_grad0, qkv_grad1]
    return (
        block_out,
        grad_resid,
        gain_sums[:layer_count],
        jnp.stack([p[:, :q_width] for p in qkv_grads]),
        jnp.stack([p[:, q_width : q_width + k_width] for p in qkv_grads]),
        jnp.stack([p[:, q_width + k_width :] for p in qkv_grads]),
        jnp.stack([out_grad0.T, out_grad1.T]),
        gain_sums[layer_count:],
        jnp.stack([gate_grad0.astype(f32), gu_grad1[:, :ff].astype(f32)]),
        jnp.stack([up_grad0.astype(f32), gu_grad1[:, ff:].astype(f32)]),
        jnp.stack([g.astype(f32).T for g in (down_grad0, down_grad1)]),
    )


def solution(mesh):
    rows = P(("fsdp", "tp"), None)
    gain = P(None, "fsdp")
    column = P(None, "fsdp", "tp")
    row = P(None, "tp", "fsdp")
    weights = (gain, column, column, column, row, gain, column, column, row)
    return jax.shard_map(
        local,
        mesh=mesh,
        in_specs=(rows, rows) + weights,
        out_specs=(rows, rows) + weights,
        check_vma=False,
    )
```

```python
import jax
import jax.numpy as jnp
from jax import lax
from jax.experimental import pallas as pl
from jax.experimental.pallas import tpu as pltpu
from jax.sharding import PartitionSpec as P

HD = 64
SEQ_LEN = 512
epsilon = 1e-05
theta = 10000.0
masked_score = -1e30
f32 = jnp.float32
bf16 = jnp.bfloat16


def norm_rows(residual, scales):
    inverse = lax.rsqrt(jnp.mean(residual * residual, axis=-1, keepdims=True) + epsilon)
    return residual * inverse * scales


def swiglu(gate_lin, up_lin):
    return jax.nn.silu(gate_lin) * up_lin


def angle_tables(positions):
    half_width = HD // 2
    exponent = 2.0 * jnp.arange(half_width).astype(f32) / HD
    frequency = theta ** (-exponent)
    angles = positions.astype(f32)[:, None] * frequency[None, :]
    return jnp.cos(angles), jnp.sin(angles)


def shift(values):
    size = lax.axis_size("tp")
    return lax.ppermute(values, "tp", [(i, (i + 1) % size) for i in range(size)])


def dot(a, b):
    return jnp.dot(a, b, preferred_element_type=f32)


def dot_t(a, b):
    return lax.dot_general(a, b, (((1,), (1,)), ((), ())), preferred_element_type=f32)


def t_dot(a, b):
    return lax.dot_general(a, b, (((0,), (0,)), ((), ())), preferred_element_type=f32)


def thin_cost():
    return pl.CostEstimate(flops=1, bytes_accessed=1, transcendentals=0)


def run_kernel(body, grid, in_specs, out_specs, out_shape, args, scratch=()):
    return pl.pallas_call(
        body,
        grid=(grid,),
        in_specs=in_specs,
        out_specs=out_specs,
        out_shape=out_shape,
        scratch_shapes=scratch,
        cost_estimate=thin_cost(),
        compiler_params=pltpu.CompilerParams(
            dimension_semantics=("arbitrary",), vmem_limit_bytes=48 * 1024 * 1024
        ),
    )(*args)


TILE = 1024
OUTER_TILE = 512


def swiglu_back(gate, up, grad):
    sig = 1.0 / (1.0 + jnp.exp(-gate))
    return grad * up * (sig * (1.0 + gate * (1.0 - sig))), grad * (gate * sig), gate * sig * up


def pair_forward(xa, xb, weights):
    rows, features = xa.shape
    ff = weights.shape[1] // 3
    n = features // TILE

    def body(xa, xb, wgu, wd, gu, act, pa, pb):
        i = pl.program_id(0)

        @pl.when(i == 0)
        def _():
            gu[...] = jnp.zeros(gu.shape, f32)

        @pl.when(i < n)
        def _():
            gu[...] += dot(jnp.concatenate([xa[...], xb[...]], axis=0), wgu[...])

        @pl.when(i == n - 1)
        def _():
            gate = gu[:, :ff]
            act[...] = (gate / (1.0 + jnp.exp(-gate)) * gu[:, ff:]).astype(bf16)

        @pl.when(i >= n)
        def _():
            part = dot_t(act[...], wd[...])
            pa[...] = part[:rows].astype(bf16)
            pb[...] = part[rows:].astype(bf16)

    early = lambda i: jnp.minimum(i, n - 1)
    late = lambda i: jnp.maximum(i - n, 0)
    return run_kernel(
        body,
        2 * n,
        [
            pl.BlockSpec((rows, TILE), lambda i: (0, early(i))),
            pl.BlockSpec((rows, TILE), lambda i: (0, early(i))),
            pl.BlockSpec((TILE, 2 * ff), lambda i: (early(i), 0)),
            pl.BlockSpec((TILE, ff), lambda i: (late(i), 2)),
        ],
        [
            pl.BlockSpec((2 * rows, 2 * ff), lambda i: (0, 0)),
            pl.BlockSpec((2 * rows, ff), lambda i: (0, 0)),
            pl.BlockSpec((rows, TILE), lambda i: (0, late(i))),
            pl.BlockSpec((rows, TILE), lambda i: (0, late(i))),
        ],
        [
            jax.ShapeDtypeStruct((2 * rows, 2 * ff), f32),
            jax.ShapeDtypeStruct((2 * rows, ff), bf16),
            jax.ShapeDtypeStruct((rows, features), bf16),
            jax.ShapeDtypeStruct((rows, features), bf16),
        ],
        (xa, xb, weights, weights),
    )


def pair_up_back(xa, xb, grad_act, which, weights):
    rows, features = xa.shape
    ff = weights.shape[1] // 3
    n = features // TILE

    def body(xa, xb, ga, w, act, grads, pa, pb, gu):
        i = pl.program_id(0)

        @pl.when(i == 0)
        def _():
            gu[...] = jnp.zeros(gu.shape, f32)

        @pl.when(i < n)
        def _():
            gu[...] += dot(jnp.concatenate([xa[...], xb[...]], axis=0), w[...])

        @pl.when(i == n - 1)
        def _():
            dgate, dup, a = swiglu_back(gu[:, :ff], gu[:, ff:], ga[...])
            grads[:, :ff] = dgate.astype(bf16)
            grads[:, ff:] = dup.astype(bf16)
            act[...] = a.astype(bf16)

        @pl.when(i >= n)
        def _():
            part = dot_t(grads[...], w[...])
            pa[...] = part[:rows].astype(bf16)
            pb[...] = part[rows:].astype(bf16)

    early = lambda i: jnp.minimum(i, n - 1)
    late = lambda i: jnp.maximum(i - n, 0)
    return run_kernel(
        body,
        2 * n,
        [
            pl.BlockSpec((rows, TILE), lambda i: (0, early(i))),
            pl.BlockSpec((rows, TILE), lambda i: (0, early(i))),
            pl.BlockSpec((2 * rows, ff), lambda i: (which, 0)),
            pl.BlockSpec((TILE, 2 * ff), lambda i: (i % n, 0)),
        ],
        [
            pl.BlockSpec((2 * rows, ff), lambda i: (0, 0)),
            pl.BlockSpec((2 * rows, 2 * ff), lambda i: (0, 0)),
            pl.BlockSpec((rows, TILE), lambda i: (0, late(i))),
            pl.BlockSpec((rows, TILE), lambda i: (0, late(i))),
        ],
        [
            jax.ShapeDtypeStruct((2 * rows, ff), bf16),
            jax.ShapeDtypeStruct((2 * rows, 2 * ff), bf16),
            jax.ShapeDtypeStruct((rows, features), bf16),
            jax.ShapeDtypeStruct((rows, features), bf16),
        ],
        (xa, xb, grad_act, weights),
        (pltpu.VMEM((2 * rows, 2 * ff), f32),),
    )


def pair_back(ga, gb, gu, weights):
    rows, features = ga.shape
    ff = weights.shape[1] // 3
    n = features // TILE

    def body(ga, gb, gu, wd, wgu, grads, pa, pb, acc):
        i = pl.program_id(0)

        @pl.when(i == 0)
        def _():
            acc[...] = jnp.zeros(acc.shape, f32)

        @pl.when(i < n)
        def _():
            acc[...] += dot(jnp.concatenate([ga[...], gb[...]], axis=0), wd[...])

        @pl.when(i == n - 1)
        def _():
            dgate, dup, _ = swiglu_back(gu[:, :ff], gu[:, ff:], acc[...])
            grads[:, :ff] = dgate.astype(bf16)
            grads[:, ff:] = dup.astype(bf16)

        @pl.when(i >= n)
        def _():
            part = dot_t(grads[...], wgu[...])
            pa[...] = part[:rows].astype(bf16)
            pb[...] = part[rows:].astype(bf16)

    early = lambda i: jnp.minimum(i, n - 1)
    late = lambda i: jnp.maximum(i - n, 0)
    return run_kernel(
        body,
        2 * n,
        [
            pl.BlockSpec((rows, TILE), lambda i: (0, early(i))),
            pl.BlockSpec((rows, TILE), lambda i: (0, early(i))),
            pl.BlockSpec((2 * rows, 2 * ff), lambda i: (0, 0)),
            pl.BlockSpec((TILE, ff), lambda i: (early(i), 2)),
            pl.BlockSpec((TILE, 2 * ff), lambda i: (late(i), 0)),
        ],
        [
            pl.BlockSpec((2 * rows, 2 * ff), lambda i: (0, 0)),
            pl.BlockSpec((rows, TILE), lambda i: (0, late(i))),
            pl.BlockSpec((rows, TILE), lambda i: (0, late(i))),
        ],
        [
            jax.ShapeDtypeStruct((2 * rows, 2 * ff), bf16),
            jax.ShapeDtypeStruct((rows, features), bf16),
            jax.ShapeDtypeStruct((rows, features), bf16),
        ],
        (ga, gb, gu, weights, weights),
        (pltpu.VMEM((2 * rows, ff), f32),),
    )


def outer(slots, pairs, parts=1):
    rows, features = slots[0].shape
    width = pairs[0].shape[1] // parts

    def body(s0, s1, s2, s3, b0, b1, *outs):
        first = jnp.concatenate([s0[...], s1[...]], axis=0)
        second = jnp.concatenate([s2[...], s3[...]], axis=0)
        for index, out in enumerate(outs):
            at = slice(index * width, (index + 1) * width)
            out[...] = (t_dot(first, b0[:, at]) + t_dot(second, b1[:, at])).astype(bf16)

    return run_kernel(
        body,
        features // OUTER_TILE,
        [pl.BlockSpec((rows, OUTER_TILE), lambda i: (0, i)) for _ in slots]
        + [pl.BlockSpec((2 * rows, parts * width), lambda i: (0, 0)) for _ in pairs],
        [pl.BlockSpec((OUTER_TILE, width), lambda i: (i, 0)) for _ in range(parts)],
        [jax.ShapeDtypeStruct((features, width), bf16) for _ in range(parts)],
        (*slots, *pairs),
    )


def whole_kernel(body, out_shape, args, scratch=()):
    return pl.pallas_call(
        body,
        out_shape=out_shape,
        scratch_shapes=scratch,
        cost_estimate=thin_cost(),
        compiler_params=pltpu.CompilerParams(vmem_limit_bytes=56 * 1024 * 1024),
    )(*args)


def turn_heads(values, cosine, sine):
    half_width = HD // 2
    parts = []
    for at in range(0, values.shape[0], HD):
        first = values[at : at + half_width]
        second = values[at + half_width : at + HD]
        parts += [first * cosine - second * sine, second * cosine + first * sine]
    return jnp.concatenate(parts, axis=0)


def attention_forward(slots, weights, bias, cosine, sine, widths):
    q_width, k_width = widths
    rows, features = slots[0].shape
    total = rows * len(slots)
    heads = q_width // HD
    repeat = heads // (k_width // HD)
    qkv_width = q_width + 2 * k_width
    scale = HD ** (-0.5)

    def body(*refs):
        xs, (w, bias, cosine, sine) = refs[: len(slots)], refs[len(slots) : len(slots) + 4]
        qt, kvt, lse, mixed, *parts = refs[len(slots) + 4 : -2]
        mt, keys = refs[-2:]
        x = jnp.concatenate([r[...] for r in xs], axis=0)
        qkv = dot(x, w[:, :qkv_width]).T
        cos, sin = cosine[...], sine[...]
        qt[...] = turn_heads(qkv[:q_width], cos, sin).astype(bf16)
        kt = turn_heads(qkv[q_width : q_width + k_width], cos, sin).astype(bf16)
        kvt[:k_width] = kt
        kvt[k_width:] = qkv[q_width + k_width :].astype(bf16)
        keys[...] = kt.astype(f32).T.astype(bf16)

        def head(h, carry):
            at = pl.ds(h * HD, HD)
            group = h // repeat
            vt = kvt[pl.ds(k_width + group * HD, HD)]
            k = keys[...] if k_width == HD else keys[:, pl.ds(group * HD, HD)]
            q = qt[at] * jnp.asarray(scale, bf16)
            s = dot(k, q) + bias[...]
            largest = jnp.max(s, axis=0, keepdims=True)
            e = jnp.exp(s - largest)
            t = jnp.sum(e, axis=0, keepdims=True)
            p = (e * (1.0 / t)).astype(bf16)
            mt[at] = dot(vt, p)
            lse[pl.ds(h, 1)] = largest + jnp.log(t)
            return carry

        lax.fori_loop(0, heads, head, 0, unroll=4 if heads % 4 == 0 else 1)
        m = mt[...].T.astype(bf16)
        mixed[...] = m
        out = dot_t(m, w[:, qkv_width:])
        for index, part in enumerate(parts):
            part[...] = out[index * rows : (index + 1) * rows].astype(bf16)

    return whole_kernel(
        body,
        [
            jax.ShapeDtypeStruct((q_width, total), bf16),
            jax.ShapeDtypeStruct((2 * k_width, total), bf16),
            jax.ShapeDtypeStruct((heads, total), f32),
            jax.ShapeDtypeStruct((total, q_width), bf16),
        ]
        + [jax.ShapeDtypeStruct((rows, features), bf16) for _ in slots],
        (*slots, weights, bias, cosine, sine),
        (pltpu.VMEM((q_width, total), f32), pltpu.VMEM((total, k_width), bf16)),
    )


def attention_backward(slots, weights, bias, cosine, sine, qt, kvt, lse, widths):
    q_width, k_width = widths
    rows, features = slots[0].shape
    total = rows * len(slots)
    heads = q_width // HD
    repeat = heads // (k_width // HD)
    qkv_width = q_width + 2 * k_width
    scale = HD ** (-0.5)

    def body(*refs):
        ms, (w, bias, cosine, sine, qt, kvt, lse) = refs[: len(slots)], refs[len(slots) : len(slots) + 7]
        grad, *parts = refs[len(slots) + 7 : -4]
        gt, gq, kv, gkv = refs[-4:]
        m = jnp.concatenate([r[...] for r in ms], axis=0)
        gt[...] = dot(m, w[:, qkv_width:]).T.astype(bf16)
        kv[...] = kvt[...].astype(f32).T.astype(bf16)
        gkv[...] = jnp.zeros(gkv.shape, f32)

        def head(h, carry):
            at = pl.ds(h * HD, HD)
            group = h // repeat
            k_at = 0 if k_width == HD else group * HD
            kt = kvt[pl.ds(k_at, HD)]
            k = kv[:, pl.ds(k_at, HD)]
            v = kv[:, pl.ds(k_width + k_at, HD)]
            q = qt[at]
            g = gt[at]
            s = dot(k, q * jnp.asarray(scale, bf16)) + bias[...]
            p = jnp.exp(s - lse[pl.ds(h, 1)])
            gp = dot(v, g)
            inner = jnp.sum(p * gp, axis=0, keepdims=True)
            gs = (p * (gp - inner) * scale).astype(bf16)
            gq[at] = dot(kt, gs)
            gk = dot_t(gs, q)
            gv = dot_t(p.astype(bf16), g)
            gkv[pl.ds(group, 1)] += jnp.concatenate([gk, gv], axis=1)[None]
            return carry

        lax.fori_loop(0, heads, head, 0, unroll=4 if heads % 4 == 0 else 1)
        cos, sin = cosine[...], -sine[...]
        both = [gkv[index].T for index in range(k_width // HD)]
        gk = jnp.concatenate([b[:HD] for b in both], axis=0)
        gv = jnp.concatenate([b[HD:] for b in both], axis=0)
        found = jnp.concatenate(
            [turn_heads(gq[...], cos, sin), turn_heads(gk, cos, sin), gv], axis=0
        ).T.astype(bf16)
        grad[...] = found
        out = dot_t(found, w[:, :qkv_width])
        for index, part in enumerate(parts):
            part[...] = out[index * rows : (index + 1) * rows].astype(bf16)

    return whole_kernel(
        body,
        [jax.ShapeDtypeStruct((total, qkv_width), bf16)]
        + [jax.ShapeDtypeStruct((rows, features), bf16) for _ in slots],
        (*slots, weights, bias, cosine, sine, qt, kvt, lse),
        (
            pltpu.VMEM((q_width, total), bf16),
            pltpu.VMEM((q_width, total), f32),
            pltpu.VMEM((total, 2 * k_width), bf16),
            pltpu.VMEM((k_width // HD, total, 2 * HD), f32),
        ),
    )


def attention_outer(normed, grad, mids, mixed):
    rows, features = normed[0].shape

    def body(*refs):
        g, m = refs[8:10]
        for slots, wide, out in ((refs[:4], g, refs[10]), (refs[4:8], m, refs[11])):
            left = jnp.concatenate([r[...] for r in slots], axis=0)
            out[...] = t_dot(left, wide[...]).astype(bf16)

    slot_spec = pl.BlockSpec((rows, OUTER_TILE), lambda i: (0, i))
    return run_kernel(
        body,
        features // OUTER_TILE,
        [slot_spec] * 8 + [pl.BlockSpec(v.shape, lambda i: (0, 0)) for v in (grad, mixed)],
        [pl.BlockSpec((OUTER_TILE, v.shape[1]), lambda i: (i, 0)) for v in (grad, mixed)],
        [jax.ShapeDtypeStruct((features, v.shape[1]), bf16) for v in (grad, mixed)],
        (*normed, *mids, grad, mixed),
    )


def gather_weight(values):
    return lax.all_gather(values, "fsdp", axis=0, tiled=True)


def scatter_weight(values):
    return lax.psum_scatter(values.astype(bf16), "fsdp", scatter_dimension=0, tiled=True)


def step(moving, work=None, inputs=(), launch=(), land=()):
    moving, inputs, sent = lax.optimization_barrier(
        (tuple(moving), tuple(inputs), tuple(a for a, _ in launch))
    )
    moved = tuple(shift(m) for m in moving)
    flying = tuple(exchange(a, bit) for a, (_, bit) in zip(sent, launch))
    results = () if work is None else work(*inputs)
    moved, results, landed = lax.optimization_barrier((moved, results, tuple(land)))
    return moved, results, flying, landed


def exchange(values, bit, axis="fsdp"):
    size = lax.axis_size(axis)
    return lax.ppermute(values, axis, [(i, i ^ (1 << bit)) for i in range(size)])


def fsdp_bits():
    count = lax.axis_size("fsdp").bit_length() - 1
    width = (count - 1) // 2
    return [0], list(range(1, 1 + width)), list(range(1 + width, count))


def my_bit(bit):
    return (lax.axis_index("fsdp") // (1 << bit)) % 2


class Scatter:
    def __init__(self, partial, order):
        self.left = sorted(order, reverse=True)
        size = lax.axis_size("fsdp")
        rows, width = partial.shape
        self.values = partial.reshape((2,) * len(order) + (rows // size, width))
        self.order = list(order)

    def half(self, values, other):
        bit = self.order[0]
        which = 1 - my_bit(bit) if other else my_bit(bit)
        return lax.dynamic_index_in_dim(values, which, self.left.index(bit), keepdims=False)

    def send(self):
        return self.half(self.values, True)

    def add(self, values, arrived):
        return (self.half(values, False).astype(f32) + arrived.astype(f32)).astype(bf16)

    def advance(self, values):
        self.left.remove(self.order.pop(0))
        self.values = values

    @property
    def bit(self):
        return self.order[0]


def sum_all(values, axis):
    for bit in range(lax.axis_size(axis).bit_length() - 1):
        values = values + exchange(values, bit, axis)
    return values


def sum_to_owner(values):
    for bit in reversed(range(lax.axis_size("fsdp").bit_length() - 1)):
        low, high = jnp.split(values, 2, axis=-1)
        upper = my_bit(bit) == 1
        values = jnp.where(upper, high, low) + exchange(jnp.where(upper, low, high), bit)
    return values


def local(
    tokens,
    cotangent,
    attention_gain,
    query_weight,
    key_weight,
    value_weight,
    output_weight,
    feed_gain,
    gate_weight,
    up_weight,
    down_weight,
):
    layer_count = query_weight.shape[0]
    local_rows = tokens.shape[0]
    size = lax.axis_size("tp")
    me = lax.axis_index("tp")
    group_rows = local_rows * size
    q_width = query_weight.shape[2]
    k_width = key_weight.shape[2]
    qkv_width = q_width + 2 * k_width
    ff = gate_weight.shape[2]
    assert size == 4 and layer_count == 2

    row_index = (
        ((me - jnp.arange(size)) % size)[:, None] * local_rows + jnp.arange(local_rows)[None, :]
    ).reshape(group_rows)
    cosine, sine = (table.T for table in angle_tables(row_index % SEQ_LEN))
    seen = (row_index[:, None] <= row_index[None, :]) & (
        (row_index // SEQ_LEN)[:, None] == (row_index // SEQ_LEN)[None, :]
    )
    bias = jnp.where(seen, 0.0, masked_score).astype(f32)
    core, xs, ys = fsdp_bits()
    me_f = lax.axis_index("fsdp")
    shards = lax.axis_size("fsdp")
    shard_rows = query_weight.shape[1]
    features = shards * shard_rows

    def attention_shard(l):
        return jnp.concatenate(
            [query_weight[l], key_weight[l], value_weight[l], output_weight[l].T], axis=1
        )

    def feed_shard(l):
        return jnp.concatenate([gate_weight[l], up_weight[l], down_weight[l].T], axis=1)

    def slot(values, s):
        return values[s * local_rows : (s + 1) * local_rows]

    def cat(parts):
        return jnp.concatenate(parts, axis=0)

    def norm_low(values, gain):
        return norm_rows(values, gain).astype(bf16)

    def attention(x0, x1, x2, x3, w, bias, cosine, sine):
        return tuple(
            attention_forward([x0, x1, x2, x3], w, bias, cosine, sine, (q_width, k_width))
        )

    def attention_back(m0, m1, m2, m3, w, bias, cosine, sine, qt, kvt, lse):
        return tuple(
            attention_backward(
                [m0, m1, m2, m3], w, bias, cosine, sine, qt, kvt, lse, (q_width, k_width)
            )
        )

    def add_low(moved, part):
        return (moved.astype(f32) + part).astype(bf16)

    weights_a0 = gather_weight(attention_shard(0))
    gains = jnp.zeros((shards, 2 * layer_count, shard_rows), bf16)
    gains = lax.dynamic_update_slice(
        gains, jnp.concatenate([attention_gain, feed_gain], axis=0)[None], (me_f, 0, 0)
    )
    bits = core + xs + ys

    def gather_gains(gains):
        for bit in bits:
            gains = gains + exchange(gains, bit)
        return gains, feed_shard(0)

    (t1,), (gains, shard_f0), _, _ = step([tokens], gather_gains, (gains,))
    weights_f = [gather_weight(shard_f0), None]
    gains = jnp.moveaxis(gains.astype(f32), 0, 1).reshape(2 * layer_count, features)
    gain_a, gain_f = gains[:layer_count], gains[layer_count:]

    def norm_slot(values, gain):
        return norm_low(values.astype(f32), gain)

    (t2,), (x0, x1, shard_a1), _, _ = step(
        [t1],
        lambda a, b, g: (norm_slot(a, g), norm_slot(b, g), attention_shard(1)),
        (tokens, t1, gain_a[0]),
    )
    (t3,), (x2, shard_f1), _, _ = step(
        [t2], lambda a, g: (norm_slot(a, g), feed_shard(1)), (t2, gain_a[0])
    )
    weights_a1 = gather_weight(shard_a1)
    tables = (bias, cosine, sine)
    normed0 = [x0, x1, x2, norm_slot(t3, gain_a[0])]
    (c1,), (*saved0, mixed0, p0, p1, p2, p3), _, _ = step(
        [cotangent], attention, (*normed0, weights_a0, *tables)
    )
    weights_f[1] = gather_weight(shard_f1)

    residual0 = tokens.astype(f32)

    def ring_sum(p0, p1, p2, p3):
        (r,), _, _, _ = step([p1])
        (r,), _, _, _ = step([add_low(r, p2)])
        (r,), _, _, _ = step([add_low(r, p3)])
        return r.astype(f32) + p0

    hidden0 = residual0 + ring_sum(p0, p1, p2, p3)

    w = weights_f[0]
    x0 = norm_low(hidden0, gain_f[0])
    (x1,), _, _, _ = step([x0])
    (x2,), _, _, _ = step([x1])
    (x3,), _, _, _ = step([x2])
    (c2,), (gu01, act01, p0, p1), _, _ = step([c1], pair_forward, (x0, x1, w))
    (r,), (gu23, act23, p2, p3), _, _ = step([p1], pair_forward, (x2, x3, w))
    (r,), _, _, _ = step([add_low(r, p2)])
    (r,), _, _, _ = step([add_low(r, p3)])
    residual1 = hidden0 + (r.astype(f32) + p0)
    feed0, gu0, act0 = [x0, x1, x2, x3], [gu01, gu23], [act01, act23]

    n0 = norm_low(residual1, gain_a[1])
    (n1,), _, _, _ = step([n0])
    (n2,), _, _, _ = step([n1])
    (n3,), _, _, _ = step([n2])
    normed1 = [n0, n1, n2, n3]
    (c3,), (*saved1, mixed1, p0, p1, p2, p3), _, _ = step(
        [c2], attention, (*normed1, weights_a1, *tables)
    )
    cots = [cotangent, c1, c2, c3]
    (r,), (grad_act,), _, _ = step(
        [p1], lambda v, *c: (dot(cat(c), v[:, 2 * ff :]),), (weights_f[1], *cots)
    )
    (r,), _, _, _ = step([add_low(r, p2)])
    (r,), _, _, _ = step([add_low(r, p3)])
    hidden1 = residual1 + (r.astype(f32) + p0)

    w = weights_f[1]

    x0 = norm_low(hidden1, gain_f[1])
    (x1,), _, _, _ = step([x0])
    (x2,), (a01, q01, p0, p1), _, _ = step(
        [x1], lambda x, y, g, v: pair_up_back(x, y, g, 0, v), (x0, x1, grad_act, w)
    )
    (x3,), _, _, _ = step([x2])
    (r,), (a23, q23, p2, p3), _, _ = step(
        [p1], lambda x, y, g, v: pair_up_back(x, y, g, 1, v), (x2, x3, grad_act, w)
    )
    (r,), (down_part1,), _, _ = step(
        [add_low(r, p2)], lambda *v: outer(v[:4], v[4:]), (*cots, a01, a23)
    )
    down_grad1 = scatter_weight(down_part1)
    (r,), (gu_part1,), _, _ = step(
        [add_low(r, p3)],
        lambda *v: outer(v[:4], v[4:]),
        (x0, x1, x2, x3, q01, q23),
    )
    gu_grad1 = scatter_weight(gu_part1)
    grad_normed = r.astype(f32) + p0
    grad_hidden, feed_gain_part1 = jax.vjp(norm_rows, hidden1, gain_f[1])[1](grad_normed)
    grad_resid = cotangent.astype(f32) + grad_hidden

    m0 = grad_resid.astype(bf16)
    (m1,), (low,), _, _ = step(
        [m0], lambda a, b, w: (dot_t(cat([a, b]), w[:, 2 * ff :]),), (a01, a23, w)
    )
    low0, low1, low2, low3 = (slot(low, s) for s in range(4))
    (m2,), _, _, _ = step([m1])
    (m3,), _, _, _ = step([m2])
    (lowr,), (g, p0, p1, p2, p3), _, _ = step(
        [low1.astype(bf16)],
        attention_back,
        (m0, m1, m2, m3, weights_a1, *tables, *saved1),
    )

    order_a, order_b = core + ys + xs, core + xs + ys

    def outer_attention(n0, n1, n2, n3, g, m0, m1, m2, m3, mixed):
        pair = attention_outer([n0, n1, n2, n3], g, [m0, m1, m2, m3], mixed)
        tracks = [Scatter(v, o) for v, o in zip(pair, (order_a, order_b))]
        return tuple(t.values for t in tracks) + tuple(t.send() for t in tracks)

    def turn(track, values, arrived):
        values = track.add(values, arrived)
        track.advance(values)
        return [values, track.send()] if track.order else [values]

    def turns(*tracks):
        def work(*v):
            results = []
            for index, track in enumerate(tracks):
                results += turn(track, v[2 * index], v[2 * index + 1])
            return tuple(results)

        return work

    def core_turns(*tracks):
        return lambda a, send_a, b, send_b: turns(*tracks)(
            a, exchange(send_a, 0), b, exchange(send_b, 0)
        )

    def run_down(track, values, send):
        while len(track.order) > 1:
            values, send = turn(track, values, exchange(send, track.bit))
        return values, send

    def tracker(order):
        return Scatter(jnp.zeros((features, 1), bf16), order)

    (r,), (qkv_v, out_v, qkv_s, out_s), _, (down_grad1,) = step(
        [p1],
        outer_attention,
        (*normed1, g, m0, m1, m2, m3, mixed1),
        land=(down_grad1,),
    )
    qkv_t, out_t = tracker(order_a), tracker(order_b)
    (r,), (qkv_v, qkv_s, out_v, out_s), _, _ = step(
        [add_low(r, p2)], core_turns(qkv_t, out_t), (qkv_v, qkv_s, out_v, out_s)
    )
    (r,), _, flying, _ = step(
        [add_low(r, p3)], launch=((qkv_s, qkv_t.bit), (out_s, out_t.bit))
    )
    grad_normed = r.astype(f32) + p0
    grad_before, attention_gain_part1 = jax.vjp(norm_rows, residual1, gain_a[1])[1](grad_normed)
    grad_resid = grad_resid + grad_before

    w = weights_f[0]

    g0 = grad_resid.astype(bf16)
    (g1,), _, _, (qkv_r, out_r) = step([g0], land=flying)
    (g2,), (q01, p0, p1), _, _ = step([g1], pair_back, (g0, g1, gu0[0], w))
    (g3,), (qkv_v, qkv_s, out_v, out_s), _, _ = step(
        [g2], turns(qkv_t, out_t), (qkv_v, qkv_r, out_v, out_r)
    )
    qkv_v, qkv_s = run_down(qkv_t, qkv_v, qkv_s)
    out_v, out_s = run_down(out_t, out_v, out_s)
    (r,), (q23, p2, p3), flying, (gu_grad1,) = step(
        [p1],
        pair_back,
        (g2, g3, gu0[1], w),
        launch=((qkv_s, qkv_t.bit), (out_s, out_t.bit)),
        land=(gu_grad1,),
    )

    def gate_up(*v):
        pair = outer(v[:4], v[4:], 2)
        tracks = [Scatter(t, o) for t, o in zip(pair, (order_a, order_b))]
        return tuple(t.values for t in tracks) + tuple(t.send() for t in tracks)

    (r,), (gate_v, up_v, gate_s, up_s), _, (qkv_r, out_r) = step(
        [add_low(r, p2)], gate_up, (*feed0, q01, q23), land=flying
    )
    qkv_grad1 = qkv_t.add(qkv_v, qkv_r).astype(f32)
    out_grad1 = out_t.add(out_v, out_r).astype(f32)
    (r,), (gate_r, up_r, down_part0), _, _ = step(
        [add_low(r, p3)],
        lambda a, b, *v: (exchange(a, 0), exchange(b, 0), *outer(v[:4], v[4:])),
        (gate_s, up_s, g0, g1, g2, g3, *act0),
    )
    down_grad0 = scatter_weight(down_part0)
    gate_t, up_t = tracker(order_a), tracker(order_b)
    grad_normed = r.astype(f32) + p0
    grad_hidden, feed_gain_part0 = jax.vjp(norm_rows, hidden0, gain_f[0])[1](grad_normed)
    grad_resid = grad_resid + grad_hidden

    m0 = grad_resid.astype(bf16)
    (m1,), (gate_v, gate_s, up_v, up_s), _, _ = step(
        [m0], turns(gate_t, up_t), (gate_v, gate_r, up_v, up_r)
    )
    (m2,), _, flying, _ = step([m1], launch=((gate_s, gate_t.bit), (up_s, up_t.bit)))
    (m3,), _, _, _ = step([m2])
    (lowr,), (g, p0, p1, p2, p3), _, (gate_r, up_r) = step(
        [add_low(lowr, low2)],
        attention_back,
        (m0, m1, m2, m3, weights_a0, *tables, *saved0),
        land=flying,
    )
    (r,), (qkv_v, out_v, qkv_s, out_s, gate_v, gate_s, up_v, up_s), _, _ = step(
        [p1],
        lambda *v: (*outer_attention(*v[:10]), *turns(gate_t, up_t)(*v[10:])),
        (*normed0, g, m0, m1, m2, m3, mixed0, gate_v, gate_r, up_v, up_r),
    )
    gate_v, gate_s = run_down(gate_t, gate_v, gate_s)
    up_v, up_s = run_down(up_t, up_v, up_s)
    qkv_t, out_t = tracker(order_a), tracker(order_b)
    (r,), (qkv_v, qkv_s, out_v, out_s), flying, _ = step(
        [add_low(r, p2)],
        core_turns(qkv_t, out_t),
        (qkv_v, qkv_s, out_v, out_s),
        launch=((gate_s, gate_t.bit), (up_s, up_t.bit)),
    )
    (r,), _, att_flying, (gate_r, up_r) = step(
        [add_low(r, p3)],
        launch=((qkv_s, qkv_t.bit), (out_s, out_t.bit)),
        land=flying,
    )

    def last_norm(r, p0, grad_resid, gate_v, gate_r, up_v, up_r):
        grad_before, gain_part = jax.vjp(norm_rows, residual0, gain_a[0])[1](r.astype(f32) + p0)
        return (
            grad_resid + grad_before,
            gain_part,
            gate_t.add(gate_v, gate_r),
            up_t.add(up_v, up_r),
        )

    (lowr,), (grad_resid, attention_gain_part0, gate_grad0, up_grad0), _, _ = step(
        [add_low(lowr, low3)],
        last_norm,
        (r, p0, grad_resid, gate_v, gate_r, up_v, up_r),
    )
    qkv_r, out_r = att_flying
    qkv_v, qkv_s = run_down(qkv_t, *turn(qkv_t, qkv_v, qkv_r))
    out_v, out_s = run_down(out_t, *turn(out_t, out_v, out_r))
    qkv_grad0 = qkv_t.add(qkv_v, exchange(qkv_s, qkv_t.bit)).astype(f32)
    out_grad0 = out_t.add(out_v, exchange(out_s, out_t.bit)).astype(f32)
    block_out = (hidden1 + (lowr.astype(f32) + low0)).astype(bf16)

    gain_sums = jnp.stack(
        [attention_gain_part0, attention_gain_part1, feed_gain_part0, feed_gain_part1]
    )
    gain_sums = sum_all(sum_to_owner(gain_sums), "tp")
    qkv_grads = [qkv_grad0, qkv_grad1]
    return (
        block_out,
        grad_resid,
        gain_sums[:layer_count],
        jnp.stack([p[:, :q_width] for p in qkv_grads]),
        jnp.stack([p[:, q_width : q_width + k_width] for p in qkv_grads]),
        jnp.stack([p[:, q_width + k_width :] for p in qkv_grads]),
        jnp.stack([out_grad0.T, out_grad1.T]),
        gain_sums[layer_count:],
        jnp.stack([gate_grad0.astype(f32), gu_grad1[:, :ff].astype(f32)]),
        jnp.stack([up_grad0.astype(f32), gu_grad1[:, ff:].astype(f32)]),
        jnp.stack([g.astype(f32).T for g in (down_grad0, down_grad1)]),
    )


def solution(mesh):
    rows = P(("fsdp", "tp"), None)
    gain = P(None, "fsdp")
    column = P(None, "fsdp", "tp")
    row = P(None, "tp", "fsdp")
    weights = (gain, column, column, column, row, gain, column, column, row)
    return jax.shard_map(
        local,
        mesh=mesh,
        in_specs=(rows, rows) + weights,
        out_specs=(rows, rows) + weights,
        check_vma=False,
    )
```

```python
import jax
import jax.numpy as jnp
from jax import lax
from jax.experimental import pallas as pl
from jax.experimental.pallas import tpu as pltpu
from jax.sharding import PartitionSpec as P

HD = 64
SEQ_LEN = 512
epsilon = 1e-05
theta = 10000.0
masked_score = -1e30
f32 = jnp.float32
bf16 = jnp.bfloat16


def norm_rows(residual, scales):
    inverse = lax.rsqrt(jnp.mean(residual * residual, axis=-1, keepdims=True) + epsilon)
    return residual * inverse * scales


def swiglu(gate_lin, up_lin):
    return jax.nn.silu(gate_lin) * up_lin


def angle_tables(positions):
    half_width = HD // 2
    exponent = 2.0 * jnp.arange(half_width).astype(f32) / HD
    frequency = theta ** (-exponent)
    angles = positions.astype(f32)[:, None] * frequency[None, :]
    return jnp.cos(angles), jnp.sin(angles)


def shift(values):
    size = lax.axis_size("tp")
    return lax.ppermute(values, "tp", [(i, (i + 1) % size) for i in range(size)])


def dot(a, b):
    return jnp.dot(a, b, preferred_element_type=f32)


def dot_t(a, b):
    return lax.dot_general(a, b, (((1,), (1,)), ((), ())), preferred_element_type=f32)


def t_dot(a, b):
    return lax.dot_general(a, b, (((0,), (0,)), ((), ())), preferred_element_type=f32)


def thin_cost():
    return pl.CostEstimate(flops=1, bytes_accessed=1, transcendentals=0)


def run_kernel(body, grid, in_specs, out_specs, out_shape, args, scratch=(), room=36):
    return pl.pallas_call(
        body,
        grid=(grid,),
        in_specs=in_specs,
        out_specs=out_specs,
        out_shape=out_shape,
        scratch_shapes=scratch,
        cost_estimate=thin_cost(),
        compiler_params=pltpu.CompilerParams(
            dimension_semantics=("arbitrary",), vmem_limit_bytes=room * 1024 * 1024
        ),
    )(*args)


TILE = 1024
OUTER_TILE = 512


def swiglu_back(gate, up, grad):
    sig = 1.0 / (1.0 + jnp.exp(-gate))
    return grad * up * (sig * (1.0 + gate * (1.0 - sig))), grad * (gate * sig), gate * sig * up


def pair_forward(xa, xb, weights):
    rows, features = xa.shape
    ff = weights.shape[1] // 3
    n = features // TILE

    def body(xa, xb, wgu, wd, gu, act, pa, pb):
        i = pl.program_id(0)

        @pl.when(i == 0)
        def _():
            gu[...] = jnp.zeros(gu.shape, f32)

        @pl.when(i < n)
        def _():
            gu[...] += dot(jnp.concatenate([xa[...], xb[...]], axis=0), wgu[...])

        @pl.when(i == n - 1)
        def _():
            gate = gu[:, :ff]
            act[...] = (gate / (1.0 + jnp.exp(-gate)) * gu[:, ff:]).astype(bf16)

        @pl.when(i >= n)
        def _():
            part = dot_t(act[...], wd[...])
            pa[...] = part[:rows].astype(bf16)
            pb[...] = part[rows:].astype(bf16)

    early = lambda i: jnp.minimum(i, n - 1)
    late = lambda i: jnp.maximum(i - n, 0)
    return run_kernel(
        body,
        2 * n,
        [
            pl.BlockSpec((rows, TILE), lambda i: (0, early(i))),
            pl.BlockSpec((rows, TILE), lambda i: (0, early(i))),
            pl.BlockSpec((TILE, 2 * ff), lambda i: (early(i), 0)),
            pl.BlockSpec((TILE, ff), lambda i: (late(i), 2)),
        ],
        [
            pl.BlockSpec((2 * rows, 2 * ff), lambda i: (0, 0)),
            pl.BlockSpec((2 * rows, ff), lambda i: (0, 0)),
            pl.BlockSpec((rows, TILE), lambda i: (0, late(i))),
            pl.BlockSpec((rows, TILE), lambda i: (0, late(i))),
        ],
        [
            jax.ShapeDtypeStruct((2 * rows, 2 * ff), f32),
            jax.ShapeDtypeStruct((2 * rows, ff), bf16),
            jax.ShapeDtypeStruct((rows, features), bf16),
            jax.ShapeDtypeStruct((rows, features), bf16),
        ],
        (xa, xb, weights, weights),
    )


def pair_up_back(xa, xb, grad_act, which, weights):
    rows, features = xa.shape
    ff = weights.shape[1] // 3
    n = features // TILE

    def body(xa, xb, ga, w, act, grads, pa, pb, gu):
        i = pl.program_id(0)

        @pl.when(i == 0)
        def _():
            gu[...] = jnp.zeros(gu.shape, f32)

        @pl.when(i < n)
        def _():
            gu[...] += dot(jnp.concatenate([xa[...], xb[...]], axis=0), w[...])

        @pl.when(i == n - 1)
        def _():
            dgate, dup, a = swiglu_back(gu[:, :ff], gu[:, ff:], ga[...])
            grads[:, :ff] = dgate.astype(bf16)
            grads[:, ff:] = dup.astype(bf16)
            act[...] = a.astype(bf16)

        @pl.when(i >= n)
        def _():
            part = dot_t(grads[...], w[...])
            pa[...] = part[:rows].astype(bf16)
            pb[...] = part[rows:].astype(bf16)

    early = lambda i: jnp.minimum(i, n - 1)
    late = lambda i: jnp.maximum(i - n, 0)
    return run_kernel(
        body,
        2 * n,
        [
            pl.BlockSpec((rows, TILE), lambda i: (0, early(i))),
            pl.BlockSpec((rows, TILE), lambda i: (0, early(i))),
            pl.BlockSpec((2 * rows, ff), lambda i: (which, 0)),
            pl.BlockSpec((TILE, 2 * ff), lambda i: (i % n, 0)),
        ],
        [
            pl.BlockSpec((2 * rows, ff), lambda i: (0, 0)),
            pl.BlockSpec((2 * rows, 2 * ff), lambda i: (0, 0)),
            pl.BlockSpec((rows, TILE), lambda i: (0, late(i))),
            pl.BlockSpec((rows, TILE), lambda i: (0, late(i))),
        ],
        [
            jax.ShapeDtypeStruct((2 * rows, ff), bf16),
            jax.ShapeDtypeStruct((2 * rows, 2 * ff), bf16),
            jax.ShapeDtypeStruct((rows, features), bf16),
            jax.ShapeDtypeStruct((rows, features), bf16),
        ],
        (xa, xb, grad_act, weights),
        (pltpu.VMEM((2 * rows, 2 * ff), f32),),
    )


def pair_back(ga, gb, gu, weights):
    rows, features = ga.shape
    ff = weights.shape[1] // 3
    n = features // TILE

    def body(ga, gb, gu, wd, wgu, grads, pa, pb, acc):
        i = pl.program_id(0)

        @pl.when(i == 0)
        def _():
            acc[...] = jnp.zeros(acc.shape, f32)

        @pl.when(i < n)
        def _():
            acc[...] += dot(jnp.concatenate([ga[...], gb[...]], axis=0), wd[...])

        @pl.when(i == n - 1)
        def _():
            dgate, dup, _ = swiglu_back(gu[:, :ff], gu[:, ff:], acc[...])
            grads[:, :ff] = dgate.astype(bf16)
            grads[:, ff:] = dup.astype(bf16)

        @pl.when(i >= n)
        def _():
            part = dot_t(grads[...], wgu[...])
            pa[...] = part[:rows].astype(bf16)
            pb[...] = part[rows:].astype(bf16)

    early = lambda i: jnp.minimum(i, n - 1)
    late = lambda i: jnp.maximum(i - n, 0)
    return run_kernel(
        body,
        2 * n,
        [
            pl.BlockSpec((rows, TILE), lambda i: (0, early(i))),
            pl.BlockSpec((rows, TILE), lambda i: (0, early(i))),
            pl.BlockSpec((2 * rows, 2 * ff), lambda i: (0, 0)),
            pl.BlockSpec((TILE, ff), lambda i: (early(i), 2)),
            pl.BlockSpec((TILE, 2 * ff), lambda i: (late(i), 0)),
        ],
        [
            pl.BlockSpec((2 * rows, 2 * ff), lambda i: (0, 0)),
            pl.BlockSpec((rows, TILE), lambda i: (0, late(i))),
            pl.BlockSpec((rows, TILE), lambda i: (0, late(i))),
        ],
        [
            jax.ShapeDtypeStruct((2 * rows, 2 * ff), bf16),
            jax.ShapeDtypeStruct((rows, features), bf16),
            jax.ShapeDtypeStruct((rows, features), bf16),
        ],
        (ga, gb, gu, weights, weights),
        (pltpu.VMEM((2 * rows, ff), f32),),
    )


def outer(slots, pairs, parts=1):
    rows, features = slots[0].shape
    width = pairs[0].shape[1] // parts

    def body(s0, s1, s2, s3, b0, b1, *outs):
        first = jnp.concatenate([s0[...], s1[...]], axis=0)
        second = jnp.concatenate([s2[...], s3[...]], axis=0)
        for index, out in enumerate(outs):
            at = slice(index * width, (index + 1) * width)
            out[...] = (t_dot(first, b0[:, at]) + t_dot(second, b1[:, at])).astype(bf16)

    return run_kernel(
        body,
        features // OUTER_TILE,
        [pl.BlockSpec((rows, OUTER_TILE), lambda i: (0, i)) for _ in slots]
        + [pl.BlockSpec((2 * rows, parts * width), lambda i: (0, 0)) for _ in pairs],
        [pl.BlockSpec((OUTER_TILE, width), lambda i: (i, 0)) for _ in range(parts)],
        [jax.ShapeDtypeStruct((features, width), bf16) for _ in range(parts)],
        (*slots, *pairs),
        room=24,
    )


def whole_kernel(body, out_shape, args, scratch=()):
    return pl.pallas_call(
        body,
        out_shape=out_shape,
        scratch_shapes=scratch,
        cost_estimate=thin_cost(),
        compiler_params=pltpu.CompilerParams(vmem_limit_bytes=32 * 1024 * 1024),
    )(*args)


def turn_heads(values, cosine, sine):
    half_width = HD // 2
    parts = []
    for at in range(0, values.shape[0], HD):
        first = values[at : at + half_width]
        second = values[at + half_width : at + HD]
        parts += [first * cosine - second * sine, second * cosine + first * sine]
    return jnp.concatenate(parts, axis=0)


def attention_forward(slots, weights, bias, cosine, sine, widths):
    q_width, k_width = widths
    rows, features = slots[0].shape
    total = rows * len(slots)
    heads = q_width // HD
    repeat = heads // (k_width // HD)
    qkv_width = q_width + 2 * k_width
    scale = HD ** (-0.5)

    def body(*refs):
        xs, (w, bias, cosine, sine) = refs[: len(slots)], refs[len(slots) : len(slots) + 4]
        qt, kvt, lse, mixed, *parts = refs[len(slots) + 4 : -2]
        mt, keys = refs[-2:]
        x = jnp.concatenate([r[...] for r in xs], axis=0)
        qkv = dot(x, w[:, :qkv_width]).T
        cos, sin = cosine[...], sine[...]
        qt[...] = turn_heads(qkv[:q_width], cos, sin).astype(bf16)
        kt = turn_heads(qkv[q_width : q_width + k_width], cos, sin).astype(bf16)
        kvt[:k_width] = kt
        kvt[k_width:] = qkv[q_width + k_width :].astype(bf16)
        keys[...] = kt.astype(f32).T.astype(bf16)

        def head(h, carry):
            at = pl.ds(h * HD, HD)
            group = h // repeat
            vt = kvt[pl.ds(k_width + group * HD, HD)]
            k = keys[...] if k_width == HD else keys[:, pl.ds(group * HD, HD)]
            q = qt[at] * jnp.asarray(scale, bf16)
            s = dot(k, q) + bias[...]
            largest = jnp.max(s, axis=0, keepdims=True)
            e = jnp.exp(s - largest)
            t = jnp.sum(e, axis=0, keepdims=True)
            p = (e * (1.0 / t)).astype(bf16)
            mt[at] = dot(vt, p)
            lse[pl.ds(h, 1)] = largest + jnp.log(t)
            return carry

        lax.fori_loop(0, heads, head, 0, unroll=4 if heads % 4 == 0 else 1)
        m = mt[...].T.astype(bf16)
        mixed[...] = m
        out = dot_t(m, w[:, qkv_width:])
        for index, part in enumerate(parts):
            part[...] = out[index * rows : (index + 1) * rows].astype(bf16)

    return whole_kernel(
        body,
        [
            jax.ShapeDtypeStruct((q_width, total), bf16),
            jax.ShapeDtypeStruct((2 * k_width, total), bf16),
            jax.ShapeDtypeStruct((heads, total), f32),
            jax.ShapeDtypeStruct((total, q_width), bf16),
        ]
        + [jax.ShapeDtypeStruct((rows, features), bf16) for _ in slots],
        (*slots, weights, bias, cosine, sine),
        (pltpu.VMEM((q_width, total), f32), pltpu.VMEM((total, k_width), bf16)),
    )


def attention_backward(slots, weights, bias, cosine, sine, qt, kvt, lse, widths):
    q_width, k_width = widths
    rows, features = slots[0].shape
    total = rows * len(slots)
    heads = q_width // HD
    repeat = heads // (k_width // HD)
    qkv_width = q_width + 2 * k_width
    scale = HD ** (-0.5)

    def body(*refs):
        ms, (w, bias, cosine, sine, qt, kvt, lse) = refs[: len(slots)], refs[len(slots) : len(slots) + 7]
        grad, *parts = refs[len(slots) + 7 : -4]
        gt, gq, kv, gkv = refs[-4:]
        m = jnp.concatenate([r[...] for r in ms], axis=0)
        gt[...] = dot(m, w[:, qkv_width:]).T.astype(bf16)
        kv[...] = kvt[...].astype(f32).T.astype(bf16)
        gkv[...] = jnp.zeros(gkv.shape, f32)

        def head(h, carry):
            at = pl.ds(h * HD, HD)
            group = h // repeat
            k_at = 0 if k_width == HD else group * HD
            kt = kvt[pl.ds(k_at, HD)]
            k = kv[:, pl.ds(k_at, HD)]
            v = kv[:, pl.ds(k_width + k_at, HD)]
            q = qt[at]
            g = gt[at]
            s = dot(k, q * jnp.asarray(scale, bf16)) + bias[...]
            p = jnp.exp(s - lse[pl.ds(h, 1)])
            gp = dot(v, g)
            inner = jnp.sum(p * gp, axis=0, keepdims=True)
            gs = (p * (gp - inner) * scale).astype(bf16)
            gq[at] = dot(kt, gs)
            gk = dot_t(gs, q)
            gv = dot_t(p.astype(bf16), g)
            gkv[pl.ds(group, 1)] += jnp.concatenate([gk, gv], axis=1)[None]
            return carry

        lax.fori_loop(0, heads, head, 0, unroll=4 if heads % 4 == 0 else 1)
        cos, sin = cosine[...], -sine[...]
        both = [gkv[index].T for index in range(k_width // HD)]
        gk = jnp.concatenate([b[:HD] for b in both], axis=0)
        gv = jnp.concatenate([b[HD:] for b in both], axis=0)
        found = jnp.concatenate(
            [turn_heads(gq[...], cos, sin), turn_heads(gk, cos, sin), gv], axis=0
        ).T.astype(bf16)
        grad[...] = found
        out = dot_t(found, w[:, :qkv_width])
        for index, part in enumerate(parts):
            part[...] = out[index * rows : (index + 1) * rows].astype(bf16)

    return whole_kernel(
        body,
        [jax.ShapeDtypeStruct((total, qkv_width), bf16)]
        + [jax.ShapeDtypeStruct((rows, features), bf16) for _ in slots],
        (*slots, weights, bias, cosine, sine, qt, kvt, lse),
        (
            pltpu.VMEM((q_width, total), bf16),
            pltpu.VMEM((q_width, total), f32),
            pltpu.VMEM((total, 2 * k_width), bf16),
            pltpu.VMEM((k_width // HD, total, 2 * HD), f32),
        ),
    )


def attention_outer(normed, grad, mids, mixed):
    rows, features = normed[0].shape

    def body(*refs):
        g, m = refs[8:10]
        for slots, wide, out in ((refs[:4], g, refs[10]), (refs[4:8], m, refs[11])):
            left = jnp.concatenate([r[...] for r in slots], axis=0)
            out[...] = t_dot(left, wide[...]).astype(bf16)

    slot_spec = pl.BlockSpec((rows, OUTER_TILE), lambda i: (0, i))
    return run_kernel(
        body,
        features // OUTER_TILE,
        [slot_spec] * 8 + [pl.BlockSpec(v.shape, lambda i: (0, 0)) for v in (grad, mixed)],
        [pl.BlockSpec((OUTER_TILE, v.shape[1]), lambda i: (i, 0)) for v in (grad, mixed)],
        [jax.ShapeDtypeStruct((features, v.shape[1]), bf16) for v in (grad, mixed)],
        (*normed, *mids, grad, mixed),
        room=16,
    )


def slots_by_down(slots, weights):
    rows, features = slots[0].shape
    ff = weights.shape[1] // 3
    total = rows * len(slots)

    def body(*refs):
        i = pl.program_id(0)
        out = refs[-1]
        part = dot(jnp.concatenate([r[...] for r in refs[:-2]], axis=0), refs[-2][...])

        @pl.when(i == 0)
        def _():
            out[...] = part

        @pl.when(i > 0)
        def _():
            out[...] += part

    return run_kernel(
        body,
        features // OUTER_TILE,
        [pl.BlockSpec((rows, OUTER_TILE), lambda i: (0, i)) for _ in slots]
        + [pl.BlockSpec((OUTER_TILE, ff), lambda i: (i, 2))],
        pl.BlockSpec((total, ff), lambda i: (0, 0)),
        jax.ShapeDtypeStruct((total, ff), f32),
        (*slots, weights),
        room=24,
    )


def down_of(pairs, weights):
    both, ff = pairs[0].shape
    rows = both // 2
    features = weights.shape[0]

    def body(*refs):
        acts, w, outs = refs[:2], refs[2], refs[3:]
        part = dot_t(jnp.concatenate([r[...] for r in acts], axis=0), w[...])
        for index, out in enumerate(outs):
            out[...] = part[index * rows : (index + 1) * rows].astype(bf16)

    return run_kernel(
        body,
        features // OUTER_TILE,
        [pl.BlockSpec((both, ff), lambda i: (0, 0)) for _ in pairs]
        + [pl.BlockSpec((OUTER_TILE, ff), lambda i: (i, 2))],
        [pl.BlockSpec((rows, OUTER_TILE), lambda i: (0, i)) for _ in range(4)],
        [jax.ShapeDtypeStruct((rows, features), bf16) for _ in range(4)],
        (*pairs, weights),
        room=24,
    )


def gather_weight(values):
    return lax.all_gather(values, "fsdp", axis=0, tiled=True)


def scatter_weight(values):
    return lax.psum_scatter(values.astype(bf16), "fsdp", scatter_dimension=0, tiled=True)


def step(moving, work=None, inputs=(), launch=(), land=()):
    moving, inputs, sent = lax.optimization_barrier(
        (tuple(moving), tuple(inputs), tuple(a for a, _ in launch))
    )
    moved = tuple(shift(m) for m in moving)
    flying = tuple(exchange(a, bit) for a, (_, bit) in zip(sent, launch))
    results = () if work is None else work(*inputs)
    moved, results, landed = lax.optimization_barrier((moved, results, tuple(land)))
    return moved, results, flying, landed


def exchange(values, bit, axis="fsdp"):
    size = lax.axis_size(axis)
    return lax.ppermute(values, axis, [(i, i ^ (1 << bit)) for i in range(size)])


def fsdp_bits():
    count = lax.axis_size("fsdp").bit_length() - 1
    width = (count - 1) // 2
    return [0], list(range(1, 1 + width)), list(range(1 + width, count))


def my_bit(bit):
    return (lax.axis_index("fsdp") // (1 << bit)) % 2


class Scatter:
    def __init__(self, partial, order):
        self.left = sorted(order, reverse=True)
        self.rows = partial.shape[0] // lax.axis_size("fsdp")
        self.values = partial
        self.order = list(order)

    def half(self, values, other):
        bit = self.order[0]
        which = 1 - my_bit(bit) if other else my_bit(bit)
        at = self.left.index(bit)
        width = values.shape[1]
        low = self.rows << (len(self.left) - 1 - at)
        values = values.reshape(1 << at, 2, low, width)
        return lax.dynamic_index_in_dim(values, which, 1, keepdims=False).reshape(-1, width)

    def send(self):
        return self.half(self.values, True)

    def add(self, values, arrived):
        return (self.half(values, False).astype(f32) + arrived.astype(f32)).astype(bf16)

    def advance(self, values):
        self.left.remove(self.order.pop(0))
        self.values = values

    @property
    def bit(self):
        return self.order[0]


def sum_all(values, axis):
    for bit in range(lax.axis_size(axis).bit_length() - 1):
        values = values + exchange(values, bit, axis)
    return values


def sum_to_owner(values):
    for bit in reversed(range(lax.axis_size("fsdp").bit_length() - 1)):
        low, high = jnp.split(values, 2, axis=-1)
        upper = my_bit(bit) == 1
        values = jnp.where(upper, high, low) + exchange(jnp.where(upper, low, high), bit)
    return values


def local(
    tokens,
    cotangent,
    attention_gain,
    query_weight,
    key_weight,
    value_weight,
    output_weight,
    feed_gain,
    gate_weight,
    up_weight,
    down_weight,
):
    layer_count = query_weight.shape[0]
    local_rows = tokens.shape[0]
    size = lax.axis_size("tp")
    me = lax.axis_index("tp")
    group_rows = local_rows * size
    q_width = query_weight.shape[2]
    k_width = key_weight.shape[2]
    qkv_width = q_width + 2 * k_width
    ff = gate_weight.shape[2]
    assert size == 4 and layer_count == 2

    row_index = (
        ((me - jnp.arange(size)) % size)[:, None] * local_rows + jnp.arange(local_rows)[None, :]
    ).reshape(group_rows)
    cosine, sine = (table.T for table in angle_tables(row_index % SEQ_LEN))
    seen = (row_index[:, None] <= row_index[None, :]) & (
        (row_index // SEQ_LEN)[:, None] == (row_index // SEQ_LEN)[None, :]
    )
    bias = jnp.where(seen, 0.0, masked_score).astype(f32)
    core, xs, ys = fsdp_bits()
    me_f = lax.axis_index("fsdp")
    shards = lax.axis_size("fsdp")
    shard_rows = query_weight.shape[1]
    features = shards * shard_rows

    def attention_shard(l):
        return jnp.concatenate(
            [query_weight[l], key_weight[l], value_weight[l], output_weight[l].T], axis=1
        )

    def feed_shard(l):
        return jnp.concatenate([gate_weight[l], up_weight[l], down_weight[l].T], axis=1)

    def cat(parts):
        return jnp.concatenate(parts, axis=0)

    def norm_low(values, gain):
        return norm_rows(values, gain).astype(bf16)

    def attention(x0, x1, x2, x3, w, bias, cosine, sine):
        return tuple(
            attention_forward([x0, x1, x2, x3], w, bias, cosine, sine, (q_width, k_width))
        )

    def attention_back(m0, m1, m2, m3, w, bias, cosine, sine, qt, kvt, lse):
        return tuple(
            attention_backward(
                [m0, m1, m2, m3], w, bias, cosine, sine, qt, kvt, lse, (q_width, k_width)
            )
        )

    def add_low(moved, part):
        return (moved.astype(f32) + part).astype(bf16)

    weights_a0 = gather_weight(attention_shard(0))
    gains = jnp.zeros((shards, 2 * layer_count, shard_rows), bf16)
    gains = lax.dynamic_update_slice(
        gains, jnp.concatenate([attention_gain, feed_gain], axis=0)[None], (me_f, 0, 0)
    )
    bits = core + xs + ys

    (t1,), (gains, shard_f0), _, _ = step(
        [tokens], lambda g: (g + exchange(g, bits[0]), feed_shard(0)), (gains,)
    )
    weights_f = [gather_weight(shard_f0), None]

    def gather_gains(gains):
        for bit in bits[1:]:
            gains = gains + exchange(gains, bit)
        return (gains,)

    (t2,), (gains,), _, _ = step([t1], gather_gains, (gains,))
    gains = jnp.moveaxis(gains.astype(f32), 0, 1).reshape(2 * layer_count, features)
    gain_a, gain_f = gains[:layer_count], gains[layer_count:]

    def norm_slots(gain, *slots):
        return tuple(norm_low(v.astype(f32), gain) for v in slots)

    (t3,), (x0, x1, x2), _, _ = step([t2], norm_slots, (gain_a[0], tokens, t1, t2))
    tables = (bias, cosine, sine)
    normed0 = [x0, x1, x2, *norm_slots(gain_a[0], t3)]
    (c1,), (*saved0, mixed0, p0, p1, p2, p3), _, _ = step(
        [cotangent], attention, (*normed0, weights_a0, *tables)
    )
    residual0 = tokens.astype(f32)

    (r,), (shard_a1,), _, _ = step([p1], lambda: (attention_shard(1),))
    weights_a1 = gather_weight(shard_a1)
    (r,), (shard_f1,), _, _ = step([add_low(r, p2)], lambda: (feed_shard(1),))
    weights_f[1] = gather_weight(shard_f1)
    (r,), _, _, _ = step([add_low(r, p3)])
    hidden0 = residual0 + (r.astype(f32) + p0)

    w = weights_f[0]
    x0 = norm_low(hidden0, gain_f[0])
    (x1,), _, _, _ = step([x0])
    (x2,), _, _, _ = step([x1])
    (x3,), _, _, _ = step([x2])
    (c2,), (gu01, act01, p0, p1), _, _ = step([c1], pair_forward, (x0, x1, w))
    (r,), (gu23, act23, p2, p3), _, _ = step([p1], pair_forward, (x2, x3, w))
    (r,), _, _, _ = step([add_low(r, p2)])
    (r,), _, _, _ = step([add_low(r, p3)])
    residual1 = hidden0 + (r.astype(f32) + p0)
    feed0, gu0, act0 = [x0, x1, x2, x3], [gu01, gu23], [act01, act23]

    n0 = norm_low(residual1, gain_a[1])
    (n1,), _, _, _ = step([n0])
    (n2,), _, _, _ = step([n1])
    (n3,), _, _, _ = step([n2])
    normed1 = [n0, n1, n2, n3]
    (c3,), (*saved1, mixed1, p0, p1, p2, p3), _, _ = step(
        [c2], attention, (*normed1, weights_a1, *tables)
    )
    cots = [cotangent, c1, c2, c3]
    (r,), _, _, _ = step([p1])
    (r,), _, _, _ = step([add_low(r, p2)])
    (r,), _, _, _ = step([add_low(r, p3)])
    hidden1 = residual1 + (r.astype(f32) + p0)

    w = weights_f[1]

    x0 = norm_low(hidden1, gain_f[1])
    (x1,), (grad_act,), _, _ = step(
        [x0], lambda v, *c: (slots_by_down(c, v),), (w, *cots)
    )
    (x2,), (a01, q01, p0, p1), _, _ = step(
        [x1], lambda x, y, g, v: pair_up_back(x, y, g, 0, v), (x0, x1, grad_act, w)
    )
    (x3,), _, _, _ = step([x2])
    (r,), (a23, q23, p2, p3), _, _ = step(
        [p1], lambda x, y, g, v: pair_up_back(x, y, g, 1, v), (x2, x3, grad_act, w)
    )
    (r,), (down_part1,), _, _ = step(
        [add_low(r, p2)], lambda *v: outer(v[:4], v[4:]), (*cots, a01, a23)
    )
    down_grad1 = scatter_weight(down_part1)
    (r,), (gu_part1,), _, _ = step(
        [add_low(r, p3)],
        lambda *v: outer(v[:4], v[4:]),
        (x0, x1, x2, x3, q01, q23),
    )
    gu_grad1 = scatter_weight(gu_part1)
    grad_normed = r.astype(f32) + p0
    grad_hidden, feed_gain_part1 = jax.vjp(norm_rows, hidden1, gain_f[1])[1](grad_normed)
    grad_resid = cotangent.astype(f32) + grad_hidden

    m0 = grad_resid.astype(bf16)
    (m1,), (low0, low1, low2, low3), _, _ = step(
        [m0], lambda a, b, v: tuple(down_of([a, b], v)), (a01, a23, w)
    )
    (m2,), _, _, _ = step([m1])
    (m3,), _, _, _ = step([m2])
    (lowr,), (g, p0, p1, p2, p3), _, _ = step(
        [low1],
        attention_back,
        (m0, m1, m2, m3, weights_a1, *tables, *saved1),
    )

    order_a, order_b = core + ys + xs, core + xs + ys

    def outer_attention(n0, n1, n2, n3, g, m0, m1, m2, m3, mixed):
        pair = attention_outer([n0, n1, n2, n3], g, [m0, m1, m2, m3], mixed)
        tracks = [Scatter(v, o) for v, o in zip(pair, (order_a, order_b))]
        return tuple(t.values for t in tracks) + tuple(t.send() for t in tracks)

    def turn(track, values, arrived):
        values = track.add(values, arrived)
        track.advance(values)
        return [values, track.send()] if track.order else [values]

    def turns(*tracks):
        def work(*v):
            results = []
            for index, track in enumerate(tracks):
                results += turn(track, v[2 * index], v[2 * index + 1])
            return tuple(results)

        return work

    def core_turns(*tracks):
        return lambda a, send_a, b, send_b: turns(*tracks)(
            a, exchange(send_a, 0), b, exchange(send_b, 0)
        )

    def run_down(track, values, send):
        while len(track.order) > 1:
            values, send = turn(track, values, exchange(send, track.bit))
        return values, send

    def tracker(order):
        return Scatter(jnp.zeros((features, 1), bf16), order)

    (r,), (qkv_v, out_v, qkv_s, out_s), _, (down_grad1,) = step(
        [p1],
        outer_attention,
        (*normed1, g, m0, m1, m2, m3, mixed1),
        land=(down_grad1,),
    )
    qkv_t, out_t = tracker(order_a), tracker(order_b)
    (r,), (qkv_v, qkv_s, out_v, out_s), _, _ = step(
        [add_low(r, p2)], core_turns(qkv_t, out_t), (qkv_v, qkv_s, out_v, out_s)
    )
    (r,), _, flying, _ = step(
        [add_low(r, p3)], launch=((qkv_s, qkv_t.bit), (out_s, out_t.bit))
    )
    grad_normed = r.astype(f32) + p0
    grad_before, attention_gain_part1 = jax.vjp(norm_rows, residual1, gain_a[1])[1](grad_normed)
    grad_resid = grad_resid + grad_before

    w = weights_f[0]

    g0 = grad_resid.astype(bf16)
    (g1,), _, _, (qkv_r, out_r) = step([g0], land=flying)
    (g2,), (q01, p0, p1), _, _ = step([g1], pair_back, (g0, g1, gu0[0], w))
    (g3,), (qkv_v, qkv_s, out_v, out_s), _, _ = step(
        [g2], turns(qkv_t, out_t), (qkv_v, qkv_r, out_v, out_r)
    )
    qkv_v, qkv_s = run_down(qkv_t, qkv_v, qkv_s)
    out_v, out_s = run_down(out_t, out_v, out_s)
    (r,), (q23, p2, p3), flying, (gu_grad1,) = step(
        [p1],
        pair_back,
        (g2, g3, gu0[1], w),
        launch=((qkv_s, qkv_t.bit), (out_s, out_t.bit)),
        land=(gu_grad1,),
    )

    def gate_up(*v):
        pair = outer(v[:4], v[4:], 2)
        tracks = [Scatter(t, o) for t, o in zip(pair, (order_a, order_b))]
        return tuple(t.values for t in tracks) + tuple(t.send() for t in tracks)

    (r,), (gate_v, up_v, gate_s, up_s), _, (qkv_r, out_r) = step(
        [add_low(r, p2)], gate_up, (*feed0, q01, q23), land=flying
    )
    qkv_grad1 = qkv_t.add(qkv_v, qkv_r).astype(f32)
    out_grad1 = out_t.add(out_v, out_r).astype(f32)
    (r,), (gate_r, up_r, down_part0), _, _ = step(
        [add_low(r, p3)],
        lambda a, b, *v: (exchange(a, 0), exchange(b, 0), *outer(v[:4], v[4:])),
        (gate_s, up_s, g0, g1, g2, g3, *act0),
    )
    down_grad0 = scatter_weight(down_part0)
    gate_t, up_t = tracker(order_a), tracker(order_b)
    grad_normed = r.astype(f32) + p0
    grad_hidden, feed_gain_part0 = jax.vjp(norm_rows, hidden0, gain_f[0])[1](grad_normed)
    grad_resid = grad_resid + grad_hidden

    m0 = grad_resid.astype(bf16)
    (m1,), (gate_v, gate_s, up_v, up_s), _, _ = step(
        [m0], turns(gate_t, up_t), (gate_v, gate_r, up_v, up_r)
    )
    (m2,), _, flying, _ = step([m1], launch=((gate_s, gate_t.bit), (up_s, up_t.bit)))
    (m3,), _, _, _ = step([m2])
    (lowr,), (g, p0, p1, p2, p3), _, (gate_r, up_r) = step(
        [add_low(lowr, low2)],
        attention_back,
        (m0, m1, m2, m3, weights_a0, *tables, *saved0),
        land=flying,
    )
    (r,), (qkv_v, out_v, qkv_s, out_s, gate_v, gate_s, up_v, up_s), _, (down_grad0,) = step(
        [p1],
        lambda *v: (*outer_attention(*v[:10]), *turns(gate_t, up_t)(*v[10:])),
        (*normed0, g, m0, m1, m2, m3, mixed0, gate_v, gate_r, up_v, up_r),
        land=(down_grad0,),
    )
    gate_v, gate_s = run_down(gate_t, gate_v, gate_s)
    up_v, up_s = run_down(up_t, up_v, up_s)
    qkv_t, out_t = tracker(order_a), tracker(order_b)
    (r,), (qkv_v, qkv_s, out_v, out_s), flying, _ = step(
        [add_low(r, p2)],
        core_turns(qkv_t, out_t),
        (qkv_v, qkv_s, out_v, out_s),
        launch=((gate_s, gate_t.bit), (up_s, up_t.bit)),
    )
    (r,), _, att_flying, (gate_r, up_r) = step(
        [add_low(r, p3)],
        launch=((qkv_s, qkv_t.bit), (out_s, out_t.bit)),
        land=flying,
    )

    def last_norm(r, p0, grad_resid, gate_v, gate_r, up_v, up_r):
        grad_before, gain_part = jax.vjp(norm_rows, residual0, gain_a[0])[1](r.astype(f32) + p0)
        return (
            grad_resid + grad_before,
            gain_part,
            gate_t.add(gate_v, gate_r),
            up_t.add(up_v, up_r),
        )

    (lowr,), (grad_resid, attention_gain_part0, gate_grad0, up_grad0), _, _ = step(
        [add_low(lowr, low3)],
        last_norm,
        (r, p0, grad_resid, gate_v, gate_r, up_v, up_r),
    )
    qkv_r, out_r = att_flying
    qkv_v, qkv_s = run_down(qkv_t, *turn(qkv_t, qkv_v, qkv_r))
    out_v, out_s = run_down(out_t, *turn(out_t, out_v, out_r))
    qkv_grad0 = qkv_t.add(qkv_v, exchange(qkv_s, qkv_t.bit)).astype(f32)
    out_grad0 = out_t.add(out_v, exchange(out_s, out_t.bit)).astype(f32)
    block_out = (hidden1 + (lowr.astype(f32) + low0)).astype(bf16)

    gain_sums = jnp.stack(
        [attention_gain_part0, attention_gain_part1, feed_gain_part0, feed_gain_part1]
    )
    gain_sums = sum_all(sum_to_owner(gain_sums), "tp")
    qkv_grads = [qkv_grad0, qkv_grad1]
    return (
        block_out,
        grad_resid,
        gain_sums[:layer_count],
        jnp.stack([p[:, :q_width] for p in qkv_grads]),
        jnp.stack([p[:, q_width : q_width + k_width] for p in qkv_grads]),
        jnp.stack([p[:, q_width + k_width :] for p in qkv_grads]),
        jnp.stack([out_grad0.T, out_grad1.T]),
        gain_sums[layer_count:],
        jnp.stack([gate_grad0.astype(f32), gu_grad1[:, :ff].astype(f32)]),
        jnp.stack([up_grad0.astype(f32), gu_grad1[:, ff:].astype(f32)]),
        jnp.stack([g.astype(f32).T for g in (down_grad0, down_grad1)]),
    )


def solution(mesh):
    rows = P(("fsdp", "tp"), None)
    gain = P(None, "fsdp")
    column = P(None, "fsdp", "tp")
    row = P(None, "tp", "fsdp")
    weights = (gain, column, column, column, row, gain, column, column, row)
    return jax.shard_map(
        local,
        mesh=mesh,
        in_specs=(rows, rows) + weights,
        out_specs=(rows, rows) + weights,
        check_vma=False,
    )
```

```python
import jax
import jax.numpy as jnp
from jax import lax
from jax.experimental import pallas as pl
from jax.experimental.pallas import tpu as pltpu
from jax.sharding import PartitionSpec as P

HD = 64
SEQ_LEN = 512
epsilon = 1e-05
theta = 10000.0
masked_score = -1e30
f32 = jnp.float32
bf16 = jnp.bfloat16


def norm_rows(residual, scales):
    inverse = lax.rsqrt(jnp.mean(residual * residual, axis=-1, keepdims=True) + epsilon)
    return residual * inverse * scales


def swiglu(gate_lin, up_lin):
    return jax.nn.silu(gate_lin) * up_lin


def angle_tables(positions):
    half_width = HD // 2
    exponent = 2.0 * jnp.arange(half_width).astype(f32) / HD
    frequency = theta ** (-exponent)
    angles = positions.astype(f32)[:, None] * frequency[None, :]
    return jnp.cos(angles), jnp.sin(angles)


def shift(values):
    size = lax.axis_size("tp")
    return lax.ppermute(values, "tp", [(i, (i + 1) % size) for i in range(size)])


def dot(a, b):
    return jnp.dot(a, b, preferred_element_type=f32)


def dot_t(a, b):
    return lax.dot_general(a, b, (((1,), (1,)), ((), ())), preferred_element_type=f32)


def t_dot(a, b):
    return lax.dot_general(a, b, (((0,), (0,)), ((), ())), preferred_element_type=f32)


def thin_cost():
    return pl.CostEstimate(flops=1, bytes_accessed=1, transcendentals=0)


def pinned(args):
    return [pltpu.with_memory_space_constraint(a, pltpu.HBM) for a in args]


def run_kernel(body, grid, in_specs, out_specs, out_shape, args, scratch=(), room=36):
    return pl.pallas_call(
        body,
        grid=(grid,),
        in_specs=in_specs,
        out_specs=out_specs,
        out_shape=out_shape,
        scratch_shapes=scratch,
        cost_estimate=thin_cost(),
        compiler_params=pltpu.CompilerParams(
            dimension_semantics=("arbitrary",), vmem_limit_bytes=room * 1024 * 1024
        ),
    )(*pinned(args))


TILE = 1024
OUTER_TILE = 512


def swiglu_back(gate, up, grad):
    sig = 1.0 / (1.0 + jnp.exp(-gate))
    return grad * up * (sig * (1.0 + gate * (1.0 - sig))), grad * (gate * sig), gate * sig * up


def pair_forward(xa, xb, weights):
    rows, features = xa.shape
    ff = weights.shape[1] // 3
    n = features // TILE

    def body(xa, xb, wgu, wd, gu, act, pa, pb):
        i = pl.program_id(0)

        @pl.when(i == 0)
        def _():
            gu[...] = jnp.zeros(gu.shape, f32)

        @pl.when(i < n)
        def _():
            gu[...] += dot(jnp.concatenate([xa[...], xb[...]], axis=0), wgu[...])

        @pl.when(i == n - 1)
        def _():
            gate = gu[:, :ff]
            act[...] = (gate / (1.0 + jnp.exp(-gate)) * gu[:, ff:]).astype(bf16)

        @pl.when(i >= n)
        def _():
            part = dot_t(act[...], wd[...])
            pa[...] = part[:rows].astype(bf16)
            pb[...] = part[rows:].astype(bf16)

    early = lambda i: jnp.minimum(i, n - 1)
    late = lambda i: jnp.maximum(i - n, 0)
    return run_kernel(
        body,
        2 * n,
        [
            pl.BlockSpec((rows, TILE), lambda i: (0, early(i))),
            pl.BlockSpec((rows, TILE), lambda i: (0, early(i))),
            pl.BlockSpec((TILE, 2 * ff), lambda i: (early(i), 0)),
            pl.BlockSpec((TILE, ff), lambda i: (late(i), 2)),
        ],
        [
            pl.BlockSpec((2 * rows, 2 * ff), lambda i: (0, 0)),
            pl.BlockSpec((2 * rows, ff), lambda i: (0, 0)),
            pl.BlockSpec((rows, TILE), lambda i: (0, late(i))),
            pl.BlockSpec((rows, TILE), lambda i: (0, late(i))),
        ],
        [
            jax.ShapeDtypeStruct((2 * rows, 2 * ff), f32),
            jax.ShapeDtypeStruct((2 * rows, ff), bf16),
            jax.ShapeDtypeStruct((rows, features), bf16),
            jax.ShapeDtypeStruct((rows, features), bf16),
        ],
        (xa, xb, weights, weights),
    )


def pair_up_back(xa, xb, grad_act, which, weights):
    rows, features = xa.shape
    ff = weights.shape[1] // 3
    n = features // TILE

    def body(xa, xb, ga, w, act, grads, pa, pb, gu):
        i = pl.program_id(0)

        @pl.when(i == 0)
        def _():
            gu[...] = jnp.zeros(gu.shape, f32)

        @pl.when(i < n)
        def _():
            gu[...] += dot(jnp.concatenate([xa[...], xb[...]], axis=0), w[...])

        @pl.when(i == n - 1)
        def _():
            dgate, dup, a = swiglu_back(gu[:, :ff], gu[:, ff:], ga[...])
            grads[:, :ff] = dgate.astype(bf16)
            grads[:, ff:] = dup.astype(bf16)
            act[...] = a.astype(bf16)

        @pl.when(i >= n)
        def _():
            part = dot_t(grads[...], w[...])
            pa[...] = part[:rows].astype(bf16)
            pb[...] = part[rows:].astype(bf16)

    early = lambda i: jnp.minimum(i, n - 1)
    late = lambda i: jnp.maximum(i - n, 0)
    return run_kernel(
        body,
        2 * n,
        [
            pl.BlockSpec((rows, TILE), lambda i: (0, early(i))),
            pl.BlockSpec((rows, TILE), lambda i: (0, early(i))),
            pl.BlockSpec((2 * rows, ff), lambda i: (which, 0)),
            pl.BlockSpec((TILE, 2 * ff), lambda i: (i % n, 0)),
        ],
        [
            pl.BlockSpec((2 * rows, ff), lambda i: (0, 0)),
            pl.BlockSpec((2 * rows, 2 * ff), lambda i: (0, 0)),
            pl.BlockSpec((rows, TILE), lambda i: (0, late(i))),
            pl.BlockSpec((rows, TILE), lambda i: (0, late(i))),
        ],
        [
            jax.ShapeDtypeStruct((2 * rows, ff), bf16),
            jax.ShapeDtypeStruct((2 * rows, 2 * ff), bf16),
            jax.ShapeDtypeStruct((rows, features), bf16),
            jax.ShapeDtypeStruct((rows, features), bf16),
        ],
        (xa, xb, grad_act, weights),
        (pltpu.VMEM((2 * rows, 2 * ff), f32),),
    )


def pair_back(ga, gb, gu, weights):
    rows, features = ga.shape
    ff = weights.shape[1] // 3
    n = features // TILE

    def body(ga, gb, gu, wd, wgu, grads, pa, pb, acc):
        i = pl.program_id(0)

        @pl.when(i == 0)
        def _():
            acc[...] = jnp.zeros(acc.shape, f32)

        @pl.when(i < n)
        def _():
            acc[...] += dot(jnp.concatenate([ga[...], gb[...]], axis=0), wd[...])

        @pl.when(i == n - 1)
        def _():
            dgate, dup, _ = swiglu_back(gu[:, :ff], gu[:, ff:], acc[...])
            grads[:, :ff] = dgate.astype(bf16)
            grads[:, ff:] = dup.astype(bf16)

        @pl.when(i >= n)
        def _():
            part = dot_t(grads[...], wgu[...])
            pa[...] = part[:rows].astype(bf16)
            pb[...] = part[rows:].astype(bf16)

    early = lambda i: jnp.minimum(i, n - 1)
    late = lambda i: jnp.maximum(i - n, 0)
    return run_kernel(
        body,
        2 * n,
        [
            pl.BlockSpec((rows, TILE), lambda i: (0, early(i))),
            pl.BlockSpec((rows, TILE), lambda i: (0, early(i))),
            pl.BlockSpec((2 * rows, 2 * ff), lambda i: (0, 0)),
            pl.BlockSpec((TILE, ff), lambda i: (early(i), 2)),
            pl.BlockSpec((TILE, 2 * ff), lambda i: (late(i), 0)),
        ],
        [
            pl.BlockSpec((2 * rows, 2 * ff), lambda i: (0, 0)),
            pl.BlockSpec((rows, TILE), lambda i: (0, late(i))),
            pl.BlockSpec((rows, TILE), lambda i: (0, late(i))),
        ],
        [
            jax.ShapeDtypeStruct((2 * rows, 2 * ff), bf16),
            jax.ShapeDtypeStruct((rows, features), bf16),
            jax.ShapeDtypeStruct((rows, features), bf16),
        ],
        (ga, gb, gu, weights, weights),
        (pltpu.VMEM((2 * rows, ff), f32),),
    )


def outer(slots, pairs, parts=1):
    rows, features = slots[0].shape
    width = pairs[0].shape[1] // parts

    def body(s0, s1, s2, s3, b0, b1, *outs):
        first = jnp.concatenate([s0[...], s1[...]], axis=0)
        second = jnp.concatenate([s2[...], s3[...]], axis=0)
        for index, out in enumerate(outs):
            at = slice(index * width, (index + 1) * width)
            out[...] = (t_dot(first, b0[:, at]) + t_dot(second, b1[:, at])).astype(bf16)

    return run_kernel(
        body,
        features // OUTER_TILE,
        [pl.BlockSpec((rows, OUTER_TILE), lambda i: (0, i)) for _ in slots]
        + [pl.BlockSpec((2 * rows, parts * width), lambda i: (0, 0)) for _ in pairs],
        [pl.BlockSpec((OUTER_TILE, width), lambda i: (i, 0)) for _ in range(parts)],
        [jax.ShapeDtypeStruct((features, width), bf16) for _ in range(parts)],
        (*slots, *pairs),
        room=24,
    )


def whole_kernel(body, out_shape, args, scratch=()):
    return pl.pallas_call(
        body,
        out_shape=out_shape,
        scratch_shapes=scratch,
        cost_estimate=thin_cost(),
        compiler_params=pltpu.CompilerParams(vmem_limit_bytes=40 * 1024 * 1024),
    )(*pinned(args))


def turn_heads(values, cosine, sine):
    half_width = HD // 2
    parts = []
    for at in range(0, values.shape[0], HD):
        first = values[at : at + half_width]
        second = values[at + half_width : at + HD]
        parts += [first * cosine - second * sine, second * cosine + first * sine]
    return jnp.concatenate(parts, axis=0)


def attention_forward(slots, weights, bias, cosine, sine, widths):
    q_width, k_width = widths
    rows, features = slots[0].shape
    total = rows * len(slots)
    heads = q_width // HD
    repeat = heads // (k_width // HD)
    qkv_width = q_width + 2 * k_width
    scale = HD ** (-0.5)

    def body(*refs):
        xs, (w, bias, cosine, sine) = refs[: len(slots)], refs[len(slots) : len(slots) + 4]
        qt, kvt, lse, mixed, *parts = refs[len(slots) + 4 : -2]
        mt, keys = refs[-2:]
        x = jnp.concatenate([r[...] for r in xs], axis=0)
        qkv = dot(x, w[:, :qkv_width]).T
        cos, sin = cosine[...], sine[...]
        qt[...] = turn_heads(qkv[:q_width], cos, sin).astype(bf16)
        kt = turn_heads(qkv[q_width : q_width + k_width], cos, sin).astype(bf16)
        kvt[:k_width] = kt
        kvt[k_width:] = qkv[q_width + k_width :].astype(bf16)
        keys[...] = kt.astype(f32).T.astype(bf16)

        def head(h, carry):
            at = pl.ds(h * HD, HD)
            group = h // repeat
            vt = kvt[pl.ds(k_width + group * HD, HD)]
            k = keys[...] if k_width == HD else keys[:, pl.ds(group * HD, HD)]
            q = qt[at] * jnp.asarray(scale, bf16)
            s = dot(k, q) + bias[...]
            largest = jnp.max(s, axis=0, keepdims=True)
            e = jnp.exp(s - largest)
            t = jnp.sum(e, axis=0, keepdims=True)
            p = (e * (1.0 / t)).astype(bf16)
            mt[at] = dot(vt, p)
            lse[pl.ds(h, 1)] = largest + jnp.log(t)
            return carry

        lax.fori_loop(0, heads, head, 0, unroll=4 if heads % 4 == 0 else 1)
        m = mt[...].T.astype(bf16)
        mixed[...] = m
        out = dot_t(m, w[:, qkv_width:])
        for index, part in enumerate(parts):
            part[...] = out[index * rows : (index + 1) * rows].astype(bf16)

    return whole_kernel(
        body,
        [
            jax.ShapeDtypeStruct((q_width, total), bf16),
            jax.ShapeDtypeStruct((2 * k_width, total), bf16),
            jax.ShapeDtypeStruct((heads, total), f32),
            jax.ShapeDtypeStruct((total, q_width), bf16),
        ]
        + [jax.ShapeDtypeStruct((rows, features), bf16) for _ in slots],
        (*slots, weights, bias, cosine, sine),
        (pltpu.VMEM((q_width, total), f32), pltpu.VMEM((total, k_width), bf16)),
    )


def attention_backward(slots, weights, bias, cosine, sine, qt, kvt, lse, widths):
    q_width, k_width = widths
    rows, features = slots[0].shape
    total = rows * len(slots)
    heads = q_width // HD
    repeat = heads // (k_width // HD)
    qkv_width = q_width + 2 * k_width
    scale = HD ** (-0.5)

    def body(*refs):
        ms, (w, bias, cosine, sine, qt, kvt, lse) = refs[: len(slots)], refs[len(slots) : len(slots) + 7]
        grad, *parts = refs[len(slots) + 7 : -4]
        gt, gq, kv, gkv = refs[-4:]
        m = jnp.concatenate([r[...] for r in ms], axis=0)
        gt[...] = dot(m, w[:, qkv_width:]).T.astype(bf16)
        kv[...] = kvt[...].astype(f32).T.astype(bf16)
        gkv[...] = jnp.zeros(gkv.shape, f32)

        def head(h, carry):
            at = pl.ds(h * HD, HD)
            group = h // repeat
            k_at = 0 if k_width == HD else group * HD
            kt = kvt[pl.ds(k_at, HD)]
            k = kv[:, pl.ds(k_at, HD)]
            v = kv[:, pl.ds(k_width + k_at, HD)]
            q = qt[at]
            g = gt[at]
            s = dot(k, q * jnp.asarray(scale, bf16)) + bias[...]
            p = jnp.exp(s - lse[pl.ds(h, 1)])
            gp = dot(v, g)
            inner = jnp.sum(p * gp, axis=0, keepdims=True)
            gs = (p * (gp - inner) * scale).astype(bf16)
            gq[at] = dot(kt, gs)
            gk = dot_t(gs, q)
            gv = dot_t(p.astype(bf16), g)
            gkv[pl.ds(group, 1)] += jnp.concatenate([gk, gv], axis=1)[None]
            return carry

        lax.fori_loop(0, heads, head, 0, unroll=4 if heads % 4 == 0 else 1)
        cos, sin = cosine[...], -sine[...]
        both = [gkv[index].T for index in range(k_width // HD)]
        gk = jnp.concatenate([b[:HD] for b in both], axis=0)
        gv = jnp.concatenate([b[HD:] for b in both], axis=0)
        found = jnp.concatenate(
            [turn_heads(gq[...], cos, sin), turn_heads(gk, cos, sin), gv], axis=0
        ).T.astype(bf16)
        grad[...] = found
        out = dot_t(found, w[:, :qkv_width])
        for index, part in enumerate(parts):
            part[...] = out[index * rows : (index + 1) * rows].astype(bf16)

    return whole_kernel(
        body,
        [jax.ShapeDtypeStruct((total, qkv_width), bf16)]
        + [jax.ShapeDtypeStruct((rows, features), bf16) for _ in slots],
        (*slots, weights, bias, cosine, sine, qt, kvt, lse),
        (
            pltpu.VMEM((q_width, total), bf16),
            pltpu.VMEM((q_width, total), f32),
            pltpu.VMEM((total, 2 * k_width), bf16),
            pltpu.VMEM((k_width // HD, total, 2 * HD), f32),
        ),
    )


def attention_outer(normed, grad, mids, mixed):
    rows, features = normed[0].shape

    def body(*refs):
        g, m = refs[8:10]
        for slots, wide, out in ((refs[:4], g, refs[10]), (refs[4:8], m, refs[11])):
            left = jnp.concatenate([r[...] for r in slots], axis=0)
            out[...] = t_dot(left, wide[...]).astype(bf16)

    slot_spec = pl.BlockSpec((rows, OUTER_TILE), lambda i: (0, i))
    return run_kernel(
        body,
        features // OUTER_TILE,
        [slot_spec] * 8 + [pl.BlockSpec(v.shape, lambda i: (0, 0)) for v in (grad, mixed)],
        [pl.BlockSpec((OUTER_TILE, v.shape[1]), lambda i: (i, 0)) for v in (grad, mixed)],
        [jax.ShapeDtypeStruct((features, v.shape[1]), bf16) for v in (grad, mixed)],
        (*normed, *mids, grad, mixed),
        room=16,
    )


def slots_by_down(slots, weights):
    rows, features = slots[0].shape
    ff = weights.shape[1] // 3
    total = rows * len(slots)

    def body(*refs):
        i = pl.program_id(0)
        out = refs[-1]
        part = dot(jnp.concatenate([r[...] for r in refs[:-2]], axis=0), refs[-2][...])

        @pl.when(i == 0)
        def _():
            out[...] = part

        @pl.when(i > 0)
        def _():
            out[...] += part

    return run_kernel(
        body,
        features // OUTER_TILE,
        [pl.BlockSpec((rows, OUTER_TILE), lambda i: (0, i)) for _ in slots]
        + [pl.BlockSpec((OUTER_TILE, ff), lambda i: (i, 2))],
        pl.BlockSpec((total, ff), lambda i: (0, 0)),
        jax.ShapeDtypeStruct((total, ff), f32),
        (*slots, weights),
        room=24,
    )


def down_of(pairs, weights):
    both, ff = pairs[0].shape
    rows = both // 2
    features = weights.shape[0]

    def body(*refs):
        acts, w, outs = refs[:2], refs[2], refs[3:]
        part = dot_t(jnp.concatenate([r[...] for r in acts], axis=0), w[...])
        for index, out in enumerate(outs):
            out[...] = part[index * rows : (index + 1) * rows].astype(bf16)

    return run_kernel(
        body,
        features // OUTER_TILE,
        [pl.BlockSpec((both, ff), lambda i: (0, 0)) for _ in pairs]
        + [pl.BlockSpec((OUTER_TILE, ff), lambda i: (i, 2))],
        [pl.BlockSpec((rows, OUTER_TILE), lambda i: (0, i)) for _ in range(4)],
        [jax.ShapeDtypeStruct((rows, features), bf16) for _ in range(4)],
        (*pairs, weights),
        room=24,
    )


def gather_weight(values):
    return lax.all_gather(values, "fsdp", axis=0, tiled=True)


def scatter_weight(values):
    return lax.psum_scatter(values.astype(bf16), "fsdp", scatter_dimension=0, tiled=True)


def step(moving, work=None, inputs=(), launch=(), land=()):
    moving, inputs, sent = lax.optimization_barrier(
        (tuple(moving), tuple(inputs), tuple(a for a, _ in launch))
    )
    moved = tuple(shift(m) for m in moving)
    flying = tuple(exchange(a, bit) for a, (_, bit) in zip(sent, launch))
    results = () if work is None else work(*inputs)
    moved, results, landed = lax.optimization_barrier((moved, results, tuple(land)))
    return moved, results, flying, landed


def exchange(values, bit, axis="fsdp"):
    size = lax.axis_size(axis)
    return lax.ppermute(values, axis, [(i, i ^ (1 << bit)) for i in range(size)])


def fsdp_bits():
    count = lax.axis_size("fsdp").bit_length() - 1
    width = (count - 1) // 2
    return [0], list(range(1, 1 + width)), list(range(1 + width, count))


def my_bit(bit):
    return (lax.axis_index("fsdp") // (1 << bit)) % 2


def sends(*tracks):
    def work(*values):
        values, found = list(values), []
        for track in tracks:
            held, track.terms = track.terms, [values.pop(0) for _ in track.terms]
            found.append(track.send())
            track.terms = held
        return tuple(found)

    return work


def held(*tracks):
    return tuple(t for track in tracks for t in track.terms)


def flights(tracks, arrays):
    return tuple((a, t.bit) for t, a in zip(tracks, arrays))


def arrive(tracks, arrays):
    for track, values in zip(tracks, arrays):
        track.arrived(values)


def run_down(tracks, arrays, left):
    arrays = list(arrays)
    for index, track in enumerate(tracks):
        while len(track.order) - track.stage > left:
            track.arrived(exchange(arrays[index], track.bit))
            arrays[index] = track.send()
    return arrays


class Scatter:
    def __init__(self, partial, order):
        self.size = lax.axis_size("fsdp")
        self.me = lax.axis_index("fsdp")
        self.rows = partial.shape[0] // self.size
        self.order = list(order)
        self.stage = 0
        self.terms = [partial]
        self.free = [sorted(order, reverse=True)]

    @property
    def bit(self):
        return self.order[self.stage]

    @property
    def last(self):
        return self.stage == len(self.order) - 1

    def sum_blocks(self, blocks, dtype):
        ids = jnp.stack(
            [
                sum(
                    (((blocks >> b) & 1) << (len(free) - 1 - k) for k, b in enumerate(free)),
                    jnp.zeros_like(blocks),
                )
                for free in self.free
            ]
        ).astype(jnp.int32)
        width = self.terms[0].shape[1]
        rows, count = self.rows, blocks.shape[0]

        def body(ids, *refs):
            refs[-1][...] = sum(r[...].astype(f32) for r in refs[:-1]).astype(dtype)

        return pl.pallas_call(
            body,
            grid_spec=pltpu.PrefetchScalarGridSpec(
                num_scalar_prefetch=1,
                grid=(count,),
                in_specs=[
                    pl.BlockSpec((rows, width), lambda i, ids, term=term: (ids[term, i], 0))
                    for term in range(len(self.terms))
                ],
                out_specs=pl.BlockSpec((rows, width), lambda i, ids: (i, 0)),
            ),
            out_shape=jax.ShapeDtypeStruct((count * rows, width), dtype),
            cost_estimate=thin_cost(),
            compiler_params=pltpu.CompilerParams(
                dimension_semantics=("arbitrary",), vmem_limit_bytes=16 * 1024 * 1024
            ),
        )(ids, *pinned(self.terms))

    def send(self):
        free = self.free[self.stage]
        left = [b for b in free if b != self.bit]
        each = jnp.arange(1 << len(left))
        blocks = (self.me ^ (1 << self.bit)) + jnp.zeros_like(each)
        for k, b in enumerate(left):
            blocks = (blocks & ~(1 << b)) | (((each >> (len(left) - 1 - k)) & 1) << b)
        return self.sum_blocks(blocks, bf16)

    def arrived(self, values):
        self.terms.append(values)
        self.free.append([b for b in self.free[-1] if b != self.bit])
        self.stage += 1

    def finish(self):
        return self.sum_blocks(self.me[None], f32)


def sum_all(values, axis):
    for bit in range(lax.axis_size(axis).bit_length() - 1):
        values = values + exchange(values, bit, axis)
    return values


def sum_to_owner(values):
    for bit in reversed(range(lax.axis_size("fsdp").bit_length() - 1)):
        low, high = jnp.split(values, 2, axis=-1)
        upper = my_bit(bit) == 1
        values = jnp.where(upper, high, low) + exchange(jnp.where(upper, low, high), bit)
    return values


def local(
    tokens,
    cotangent,
    attention_gain,
    query_weight,
    key_weight,
    value_weight,
    output_weight,
    feed_gain,
    gate_weight,
    up_weight,
    down_weight,
):
    layer_count = query_weight.shape[0]
    local_rows = tokens.shape[0]
    size = lax.axis_size("tp")
    me = lax.axis_index("tp")
    group_rows = local_rows * size
    q_width = query_weight.shape[2]
    k_width = key_weight.shape[2]
    qkv_width = q_width + 2 * k_width
    ff = gate_weight.shape[2]
    assert size == 4 and layer_count == 2

    row_index = (
        ((me - jnp.arange(size)) % size)[:, None] * local_rows + jnp.arange(local_rows)[None, :]
    ).reshape(group_rows)
    cosine, sine = (table.T for table in angle_tables(row_index % SEQ_LEN))
    seen = (row_index[:, None] <= row_index[None, :]) & (
        (row_index // SEQ_LEN)[:, None] == (row_index // SEQ_LEN)[None, :]
    )
    bias = jnp.where(seen, 0.0, masked_score).astype(f32)
    core, xs, ys = fsdp_bits()
    me_f = lax.axis_index("fsdp")
    shards = lax.axis_size("fsdp")
    shard_rows = query_weight.shape[1]
    features = shards * shard_rows

    def attention_shard(l):
        return jnp.concatenate(
            [query_weight[l], key_weight[l], value_weight[l], output_weight[l].T], axis=1
        )

    def feed_shard(l):
        return jnp.concatenate([gate_weight[l], up_weight[l], down_weight[l].T], axis=1)

    def cat(parts):
        return jnp.concatenate(parts, axis=0)

    def norm_low(values, gain):
        return norm_rows(values, gain).astype(bf16)

    def attention(x0, x1, x2, x3, w, bias, cosine, sine):
        return tuple(
            attention_forward([x0, x1, x2, x3], w, bias, cosine, sine, (q_width, k_width))
        )

    def attention_back(m0, m1, m2, m3, w, bias, cosine, sine, qt, kvt, lse):
        return tuple(
            attention_backward(
                [m0, m1, m2, m3], w, bias, cosine, sine, qt, kvt, lse, (q_width, k_width)
            )
        )

    def add_low(moved, part):
        return (moved.astype(f32) + part).astype(bf16)

    weights_a0 = gather_weight(attention_shard(0))
    gains = jnp.zeros((shards, 2 * layer_count, shard_rows), bf16)
    gains = lax.dynamic_update_slice(
        gains, jnp.concatenate([attention_gain, feed_gain], axis=0)[None], (me_f, 0, 0)
    )
    bits = core + xs + ys

    (t1,), (gains, shard_f0), _, _ = step(
        [tokens], lambda g: (g + exchange(g, bits[0]), feed_shard(0)), (gains,)
    )
    weights_f = [gather_weight(shard_f0), None]

    def gather_gains(gains):
        for bit in bits[1:]:
            gains = gains + exchange(gains, bit)
        return (gains,)

    (t2,), (gains,), _, _ = step([t1], gather_gains, (gains,))
    gains = jnp.moveaxis(gains.astype(f32), 0, 1).reshape(2 * layer_count, features)
    gain_a, gain_f = gains[:layer_count], gains[layer_count:]

    def norm_slots(gain, *slots):
        return tuple(norm_low(v.astype(f32), gain) for v in slots)

    (t3,), (x0, x1, x2), _, _ = step([t2], norm_slots, (gain_a[0], tokens, t1, t2))
    tables = (bias, cosine, sine)
    normed0 = [x0, x1, x2, *norm_slots(gain_a[0], t3)]
    (c1,), (*saved0, mixed0, p0, p1, p2, p3), _, _ = step(
        [cotangent], attention, (*normed0, weights_a0, *tables)
    )
    residual0 = tokens.astype(f32)

    (r,), (shard_a1,), _, _ = step([p1], lambda: (attention_shard(1),))
    weights_a1 = gather_weight(shard_a1)
    (r,), (shard_f1,), _, _ = step([add_low(r, p2)], lambda: (feed_shard(1),))
    weights_f[1] = gather_weight(shard_f1)
    (r,), _, _, _ = step([add_low(r, p3)])
    hidden0 = residual0 + (r.astype(f32) + p0)

    w = weights_f[0]
    x0 = norm_low(hidden0, gain_f[0])
    (x1,), _, _, _ = step([x0])
    (x2,), _, _, _ = step([x1])
    (x3,), _, _, _ = step([x2])
    (c2,), (gu01, act01, p0, p1), _, _ = step([c1], pair_forward, (x0, x1, w))
    (r,), (gu23, act23, p2, p3), _, _ = step([p1], pair_forward, (x2, x3, w))
    (r,), _, _, _ = step([add_low(r, p2)])
    (r,), _, _, _ = step([add_low(r, p3)])
    residual1 = hidden0 + (r.astype(f32) + p0)
    feed0, gu0, act0 = [x0, x1, x2, x3], [gu01, gu23], [act01, act23]

    n0 = norm_low(residual1, gain_a[1])
    (n1,), _, _, _ = step([n0])
    (n2,), _, _, _ = step([n1])
    (n3,), _, _, _ = step([n2])
    normed1 = [n0, n1, n2, n3]
    (c3,), (*saved1, mixed1, p0, p1, p2, p3), _, _ = step(
        [c2], attention, (*normed1, weights_a1, *tables)
    )
    cots = [cotangent, c1, c2, c3]
    (r,), _, _, _ = step([p1])
    (r,), _, _, _ = step([add_low(r, p2)])
    (r,), _, _, _ = step([add_low(r, p3)])
    hidden1 = residual1 + (r.astype(f32) + p0)

    w = weights_f[1]

    x0 = norm_low(hidden1, gain_f[1])
    (x1,), (grad_act,), _, _ = step(
        [x0], lambda v, *c: (slots_by_down(c, v),), (w, *cots)
    )
    (x2,), (a01, q01, p0, p1), _, _ = step(
        [x1], lambda x, y, g, v: pair_up_back(x, y, g, 0, v), (x0, x1, grad_act, w)
    )
    (x3,), _, _, _ = step([x2])
    (r,), (a23, q23, p2, p3), _, _ = step(
        [p1], lambda x, y, g, v: pair_up_back(x, y, g, 1, v), (x2, x3, grad_act, w)
    )
    (r,), (down_part1,), _, _ = step(
        [add_low(r, p2)], lambda *v: outer(v[:4], v[4:]), (*cots, a01, a23)
    )
    down_grad1 = scatter_weight(down_part1)
    (r,), (gu_part1,), _, _ = step(
        [add_low(r, p3)],
        lambda *v: outer(v[:4], v[4:]),
        (x0, x1, x2, x3, q01, q23),
    )
    gu_grad1 = scatter_weight(gu_part1)
    grad_normed = r.astype(f32) + p0
    grad_hidden, feed_gain_part1 = jax.vjp(norm_rows, hidden1, gain_f[1])[1](grad_normed)
    grad_resid = cotangent.astype(f32) + grad_hidden

    m0 = grad_resid.astype(bf16)
    (m1,), (low0, low1, low2, low3), _, _ = step(
        [m0], lambda a, b, v: tuple(down_of([a, b], v)), (a01, a23, w)
    )
    (m2,), _, _, _ = step([m1])
    (m3,), _, _, _ = step([m2])
    (lowr,), (g, p0, p1, p2, p3), _, _ = step(
        [low1],
        attention_back,
        (m0, m1, m2, m3, weights_a1, *tables, *saved1),
    )

    order_a, order_b = core + ys + xs, core + xs + ys

    second_axis = len(ys)
    assert len(xs) == second_axis

    def outer_attention(n0, n1, n2, n3, g, m0, m1, m2, m3, mixed):
        pair = attention_outer([n0, n1, n2, n3], g, [m0, m1, m2, m3], mixed)
        return (*pair, *(Scatter(v, o).send() for v, o in zip(pair, (order_a, order_b))))

    (r,), (qkv, out, qkv_s, out_s), _, (down_grad1,) = step(
        [p1],
        outer_attention,
        (*normed1, g, m0, m1, m2, m3, mixed1),
        land=(down_grad1,),
    )
    att_1 = (Scatter(qkv, order_a), Scatter(out, order_b))

    def core_then_send(*tracks):
        def work(*values):
            values = list(values)
            got = [exchange(values.pop(0), 0) for _ in tracks]
            fresh = [Scatter(v, t.order) for t, v in zip(tracks, values)]
            arrive(fresh, got)
            return (*got, *(t.send() for t in fresh))

        return work

    (r,), (qkv_r, out_r, *arrays), _, _ = step(
        [add_low(r, p2)], core_then_send(*att_1), (qkv_s, out_s, qkv, out)
    )
    arrive(att_1, (qkv_r, out_r))
    arrays = run_down(att_1, arrays, 1 + second_axis)
    (r,), _, flying, _ = step([add_low(r, p3)], launch=flights(att_1, arrays))
    grad_normed = r.astype(f32) + p0
    grad_before, attention_gain_part1 = jax.vjp(norm_rows, residual1, gain_a[1])[1](grad_normed)
    grad_resid = grad_resid + grad_before

    w = weights_f[0]

    g0 = grad_resid.astype(bf16)
    (g1,), _, _, landed = step([g0], land=flying)
    arrive(att_1, landed)
    (g2,), (q01, p0, p1), _, _ = step([g1], pair_back, (g0, g1, gu0[0], w))
    (g3,), arrays, _, _ = step([g2], sends(*att_1), held(*att_1))
    arrays = run_down(att_1, arrays, 1)
    (r,), (q23, p2, p3), flying, (gu_grad1,) = step(
        [p1],
        pair_back,
        (g2, g3, gu0[1], w),
        launch=flights(att_1, arrays),
        land=(gu_grad1,),
    )

    def gate_up(*v):
        pair = outer(v[:4], v[4:], 2)
        return (*pair, *(Scatter(t, o).send() for t, o in zip(pair, (order_a, order_b))))

    (r,), (gate, up, gate_s, up_s), _, landed = step(
        [add_low(r, p2)], gate_up, (*feed0, q01, q23), land=flying
    )
    arrive(att_1, landed)
    (r,), (gate_r, up_r, down_part0), _, _ = step(
        [add_low(r, p3)],
        lambda a, b, *v: (exchange(a, 0), exchange(b, 0), *outer(v[:4], v[4:])),
        (gate_s, up_s, g0, g1, g2, g3, *act0),
    )
    down_grad0 = scatter_weight(down_part0)
    gu_0 = (Scatter(gate, order_a), Scatter(up, order_b))
    arrive(gu_0, (gate_r, up_r))
    grad_normed = r.astype(f32) + p0
    grad_hidden, feed_gain_part0 = jax.vjp(norm_rows, hidden0, gain_f[0])[1](grad_normed)
    grad_resid = grad_resid + grad_hidden

    m0 = grad_resid.astype(bf16)
    (m1,), arrays, _, _ = step([m0], sends(*gu_0), held(*gu_0))
    arrays = run_down(gu_0, arrays, 1 + second_axis)
    (m2,), _, flying, _ = step([m1], launch=flights(gu_0, arrays))
    (m3,), _, _, _ = step([m2])
    (lowr,), (g, p0, p1, p2, p3), _, _ = step(
        [add_low(lowr, low2)],
        attention_back,
        (m0, m1, m2, m3, weights_a0, *tables, *saved0),
    )
    (r,), (qkv, out, qkv_s, out_s), _, (down_grad0, *landed) = step(
        [p1],
        outer_attention,
        (*normed0, g, m0, m1, m2, m3, mixed0),
        land=(down_grad0, *flying),
    )
    arrive(gu_0, landed)
    att_0 = (Scatter(qkv, order_a), Scatter(out, order_b))
    (r,), (qkv_r, out_r, *arrays), _, _ = step(
        [add_low(r, p2)],
        lambda *v: (*core_then_send(*att_0)(*v[:4]), *sends(*gu_0)(*v[4:])),
        (qkv_s, out_s, qkv, out, *held(*gu_0)),
    )
    arrive(att_0, (qkv_r, out_r))
    att_arrays = run_down(att_0, arrays[:2], 1 + second_axis)
    gu_arrays = run_down(gu_0, arrays[2:], 1)
    done_1 = (*att_1[0].terms, *att_1[1].terms, gu_grad1, down_grad0, down_grad1)
    (r,), _, flying, done_1 = step(
        [add_low(r, p3)],
        launch=flights(gu_0, gu_arrays) + flights(att_0, att_arrays),
        land=done_1,
    )
    count = len(att_1[0].terms)
    att_1[0].terms, att_1[1].terms = list(done_1[:count]), list(done_1[count : 2 * count])
    gu_grad1, down_grad0, down_grad1 = done_1[2 * count :]

    def last_norm(r, p0, grad_resid):
        grad_before, gain_part = jax.vjp(norm_rows, residual0, gain_a[0])[1](r.astype(f32) + p0)
        return grad_resid + grad_before, gain_part

    (lowr,), (grad_resid, attention_gain_part0), _, landed = step(
        [add_low(lowr, low3)], last_norm, (r, p0, grad_resid), land=flying
    )
    arrive(gu_0, landed[:2])
    arrive(att_0, landed[2:])
    arrays = run_down(att_0, [t.send() for t in att_0], 1)
    arrive(att_0, [exchange(a, t.bit) for a, t in zip(arrays, att_0)])
    gate_grad0, up_grad0 = (t.finish() for t in gu_0)
    qkv_grads = [t[0].finish() for t in (att_0, att_1)]
    out_grads = [t[1].finish() for t in (att_0, att_1)]
    block_out = (hidden1 + (lowr.astype(f32) + low0)).astype(bf16)

    gain_sums = jnp.stack(
        [attention_gain_part0, attention_gain_part1, feed_gain_part0, feed_gain_part1]
    )
    gain_sums = sum_all(sum_to_owner(gain_sums), "tp")
    return (
        block_out,
        grad_resid,
        gain_sums[:layer_count],
        jnp.stack([p[:, :q_width] for p in qkv_grads]),
        jnp.stack([p[:, q_width : q_width + k_width] for p in qkv_grads]),
        jnp.stack([p[:, q_width + k_width :] for p in qkv_grads]),
        jnp.stack([p.T for p in out_grads]),
        gain_sums[layer_count:],
        jnp.stack([gate_grad0, gu_grad1[:, :ff].astype(f32)]),
        jnp.stack([up_grad0, gu_grad1[:, ff:].astype(f32)]),
        jnp.stack([g.astype(f32).T for g in (down_grad0, down_grad1)]),
    )


def solution(mesh):
    rows = P(("fsdp", "tp"), None)
    gain = P(None, "fsdp")
    column = P(None, "fsdp", "tp")
    row = P(None, "tp", "fsdp")
    weights = (gain, column, column, column, row, gain, column, column, row)
    return jax.shard_map(
        local,
        mesh=mesh,
        in_specs=(rows, rows) + weights,
        out_specs=(rows, rows) + weights,
        check_vma=False,
    )
```

```python
import jax
import jax.numpy as jnp
from jax import lax
from jax.experimental import pallas as pl
from jax.experimental.pallas import tpu as pltpu
from jax.sharding import PartitionSpec as P

HD = 64
SEQ_LEN = 512
epsilon = 1e-05
theta = 10000.0
masked_score = -1e30
f32 = jnp.float32
bf16 = jnp.bfloat16


def norm_rows(residual, scales):
    inverse = lax.rsqrt(jnp.mean(residual * residual, axis=-1, keepdims=True) + epsilon)
    return residual * inverse * scales


def swiglu(gate_lin, up_lin):
    return jax.nn.silu(gate_lin) * up_lin


def angle_tables(positions):
    half_width = HD // 2
    exponent = 2.0 * jnp.arange(half_width).astype(f32) / HD
    frequency = theta ** (-exponent)
    angles = positions.astype(f32)[:, None] * frequency[None, :]
    return jnp.cos(angles), jnp.sin(angles)


def shift(values):
    size = lax.axis_size("tp")
    return lax.ppermute(values, "tp", [(i, (i + 1) % size) for i in range(size)])


def dot(a, b):
    return jnp.dot(a, b, preferred_element_type=f32)


def dot_t(a, b):
    return lax.dot_general(a, b, (((1,), (1,)), ((), ())), preferred_element_type=f32)


def t_dot(a, b):
    return lax.dot_general(a, b, (((0,), (0,)), ((), ())), preferred_element_type=f32)


def thin_cost():
    return pl.CostEstimate(flops=1, bytes_accessed=1, transcendentals=0)


def pinned(args, free=0):
    return [
        a if index < free else pltpu.with_memory_space_constraint(a, pltpu.HBM)
        for index, a in enumerate(args)
    ]


def run_kernel(body, grid, in_specs, out_specs, out_shape, args, scratch=(), room=36, free=0):
    return pl.pallas_call(
        body,
        grid=(grid,),
        in_specs=in_specs,
        out_specs=out_specs,
        out_shape=out_shape,
        scratch_shapes=scratch,
        cost_estimate=thin_cost(),
        compiler_params=pltpu.CompilerParams(
            dimension_semantics=("arbitrary",), vmem_limit_bytes=room * 1024 * 1024
        ),
    )(*pinned(args, free))


TILE = 1024
OUTER_TILE = 512


def swiglu_back(gate, up, grad):
    sig = 1.0 / (1.0 + jnp.exp(-gate))
    return grad * up * (sig * (1.0 + gate * (1.0 - sig))), grad * (gate * sig), gate * sig * up


def pair_forward(xa, xb, weights):
    rows, features = xa.shape
    ff = weights.shape[1] // 3
    n = features // TILE

    def body(xa, xb, wgu, wd, gu, act, pa, pb):
        i = pl.program_id(0)

        @pl.when(i == 0)
        def _():
            gu[...] = jnp.zeros(gu.shape, f32)

        @pl.when(i < n)
        def _():
            gu[...] += dot(jnp.concatenate([xa[...], xb[...]], axis=0), wgu[...])

        @pl.when(i == n - 1)
        def _():
            gate = gu[:, :ff]
            act[...] = (gate / (1.0 + jnp.exp(-gate)) * gu[:, ff:]).astype(bf16)

        @pl.when(i >= n)
        def _():
            part = dot_t(act[...], wd[...])
            pa[...] = part[:rows].astype(bf16)
            pb[...] = part[rows:].astype(bf16)

    early = lambda i: jnp.minimum(i, n - 1)
    late = lambda i: jnp.maximum(i - n, 0)
    return run_kernel(
        body,
        2 * n,
        [
            pl.BlockSpec((rows, TILE), lambda i: (0, early(i))),
            pl.BlockSpec((rows, TILE), lambda i: (0, early(i))),
            pl.BlockSpec((TILE, 2 * ff), lambda i: (early(i), 0)),
            pl.BlockSpec((TILE, ff), lambda i: (late(i), 2)),
        ],
        [
            pl.BlockSpec((2 * rows, 2 * ff), lambda i: (0, 0)),
            pl.BlockSpec((2 * rows, ff), lambda i: (0, 0)),
            pl.BlockSpec((rows, TILE), lambda i: (0, late(i))),
            pl.BlockSpec((rows, TILE), lambda i: (0, late(i))),
        ],
        [
            pltpu.HBM((2 * rows, 2 * ff), f32),
            pltpu.HBM((2 * rows, ff), bf16),
            jax.ShapeDtypeStruct((rows, features), bf16),
            jax.ShapeDtypeStruct((rows, features), bf16),
        ],
        (xa, xb, weights, weights),
        free=2,
    )


def pair_up_back(xa, xb, grad_act, which, weights):
    rows, features = xa.shape
    ff = weights.shape[1] // 3
    n = features // TILE

    def body(xa, xb, ga, w, act, grads, pa, pb, gu):
        i = pl.program_id(0)

        @pl.when(i == 0)
        def _():
            gu[...] = jnp.zeros(gu.shape, f32)

        @pl.when(i < n)
        def _():
            gu[...] += dot(jnp.concatenate([xa[...], xb[...]], axis=0), w[...])

        @pl.when(i == n - 1)
        def _():
            dgate, dup, a = swiglu_back(gu[:, :ff], gu[:, ff:], ga[...])
            grads[:, :ff] = dgate.astype(bf16)
            grads[:, ff:] = dup.astype(bf16)
            act[...] = a.astype(bf16)

        @pl.when(i >= n)
        def _():
            part = dot_t(grads[...], w[...])
            pa[...] = part[:rows].astype(bf16)
            pb[...] = part[rows:].astype(bf16)

    early = lambda i: jnp.minimum(i, n - 1)
    late = lambda i: jnp.maximum(i - n, 0)
    return run_kernel(
        body,
        2 * n,
        [
            pl.BlockSpec((rows, TILE), lambda i: (0, early(i))),
            pl.BlockSpec((rows, TILE), lambda i: (0, early(i))),
            pl.BlockSpec((2 * rows, ff), lambda i: (which, 0)),
            pl.BlockSpec((TILE, 2 * ff), lambda i: (i % n, 0)),
        ],
        [
            pl.BlockSpec((2 * rows, ff), lambda i: (0, 0)),
            pl.BlockSpec((2 * rows, 2 * ff), lambda i: (0, 0)),
            pl.BlockSpec((rows, TILE), lambda i: (0, late(i))),
            pl.BlockSpec((rows, TILE), lambda i: (0, late(i))),
        ],
        [
            pltpu.HBM((2 * rows, ff), bf16),
            pltpu.HBM((2 * rows, 2 * ff), bf16),
            jax.ShapeDtypeStruct((rows, features), bf16),
            jax.ShapeDtypeStruct((rows, features), bf16),
        ],
        (xa, xb, grad_act, weights),
        (pltpu.VMEM((2 * rows, 2 * ff), f32),),
        free=2,
    )


def pair_back(ga, gb, gu, weights):
    rows, features = ga.shape
    ff = weights.shape[1] // 3
    n = features // TILE

    def body(ga, gb, gu, wd, wgu, grads, pa, pb, acc):
        i = pl.program_id(0)

        @pl.when(i == 0)
        def _():
            acc[...] = jnp.zeros(acc.shape, f32)

        @pl.when(i < n)
        def _():
            acc[...] += dot(jnp.concatenate([ga[...], gb[...]], axis=0), wd[...])

        @pl.when(i == n - 1)
        def _():
            dgate, dup, _ = swiglu_back(gu[:, :ff], gu[:, ff:], acc[...])
            grads[:, :ff] = dgate.astype(bf16)
            grads[:, ff:] = dup.astype(bf16)

        @pl.when(i >= n)
        def _():
            part = dot_t(grads[...], wgu[...])
            pa[...] = part[:rows].astype(bf16)
            pb[...] = part[rows:].astype(bf16)

    early = lambda i: jnp.minimum(i, n - 1)
    late = lambda i: jnp.maximum(i - n, 0)
    return run_kernel(
        body,
        2 * n,
        [
            pl.BlockSpec((rows, TILE), lambda i: (0, early(i))),
            pl.BlockSpec((rows, TILE), lambda i: (0, early(i))),
            pl.BlockSpec((2 * rows, 2 * ff), lambda i: (0, 0)),
            pl.BlockSpec((TILE, ff), lambda i: (early(i), 2)),
            pl.BlockSpec((TILE, 2 * ff), lambda i: (late(i), 0)),
        ],
        [
            pl.BlockSpec((2 * rows, 2 * ff), lambda i: (0, 0)),
            pl.BlockSpec((rows, TILE), lambda i: (0, late(i))),
            pl.BlockSpec((rows, TILE), lambda i: (0, late(i))),
        ],
        [
            pltpu.HBM((2 * rows, 2 * ff), bf16),
            jax.ShapeDtypeStruct((rows, features), bf16),
            jax.ShapeDtypeStruct((rows, features), bf16),
        ],
        (ga, gb, gu, weights, weights),
        (pltpu.VMEM((2 * rows, ff), f32),),
        free=2,
    )


def outer(slots, pairs, parts=1):
    rows, features = slots[0].shape
    width = pairs[0].shape[1] // parts

    def body(s0, s1, s2, s3, b0, b1, *outs):
        first = jnp.concatenate([s0[...], s1[...]], axis=0)
        second = jnp.concatenate([s2[...], s3[...]], axis=0)
        for index, out in enumerate(outs):
            at = slice(index * width, (index + 1) * width)
            out[...] = (t_dot(first, b0[:, at]) + t_dot(second, b1[:, at])).astype(bf16)

    return run_kernel(
        body,
        features // OUTER_TILE,
        [pl.BlockSpec((rows, OUTER_TILE), lambda i: (0, i)) for _ in slots]
        + [pl.BlockSpec((2 * rows, parts * width), lambda i: (0, 0)) for _ in pairs],
        [pl.BlockSpec((OUTER_TILE, width), lambda i: (i, 0)) for _ in range(parts)],
        [pltpu.HBM((features, width), bf16) for _ in range(parts)],
        (*slots, *pairs),
        room=24,
    )


def whole_kernel(body, out_shape, args, scratch=(), free=0):
    return pl.pallas_call(
        body,
        out_shape=out_shape,
        scratch_shapes=scratch,
        cost_estimate=thin_cost(),
        compiler_params=pltpu.CompilerParams(vmem_limit_bytes=40 * 1024 * 1024),
    )(*pinned(args, free))


def turn_heads(values, cosine, sine):
    half_width = HD // 2
    parts = []
    for at in range(0, values.shape[0], HD):
        first = values[at : at + half_width]
        second = values[at + half_width : at + HD]
        parts += [first * cosine - second * sine, second * cosine + first * sine]
    return jnp.concatenate(parts, axis=0)


def attention_forward(slots, weights, bias, cosine, sine, widths):
    q_width, k_width = widths
    rows, features = slots[0].shape
    total = rows * len(slots)
    heads = q_width // HD
    repeat = heads // (k_width // HD)
    qkv_width = q_width + 2 * k_width
    scale = HD ** (-0.5)

    def body(*refs):
        xs, (w, bias, cosine, sine) = refs[: len(slots)], refs[len(slots) : len(slots) + 4]
        qt, kvt, lse, mixed, *parts = refs[len(slots) + 4 : -2]
        mt, keys = refs[-2:]
        x = jnp.concatenate([r[...] for r in xs], axis=0)
        qkv = dot(x, w[:, :qkv_width]).T
        cos, sin = cosine[...], sine[...]
        qt[...] = turn_heads(qkv[:q_width], cos, sin).astype(bf16)
        kt = turn_heads(qkv[q_width : q_width + k_width], cos, sin).astype(bf16)
        kvt[:k_width] = kt
        kvt[k_width:] = qkv[q_width + k_width :].astype(bf16)
        keys[...] = kt.astype(f32).T.astype(bf16)

        def head(h, carry):
            at = pl.ds(h * HD, HD)
            group = h // repeat
            vt = kvt[pl.ds(k_width + group * HD, HD)]
            k = keys[...] if k_width == HD else keys[:, pl.ds(group * HD, HD)]
            q = qt[at] * jnp.asarray(scale, bf16)
            s = dot(k, q) + bias[...]
            largest = jnp.max(s, axis=0, keepdims=True)
            e = jnp.exp(s - largest)
            t = jnp.sum(e, axis=0, keepdims=True)
            p = (e * (1.0 / t)).astype(bf16)
            mt[at] = dot(vt, p)
            lse[pl.ds(h, 1)] = largest + jnp.log(t)
            return carry

        lax.fori_loop(0, heads, head, 0, unroll=4 if heads % 4 == 0 else 1)
        m = mt[...].T.astype(bf16)
        mixed[...] = m
        out = dot_t(m, w[:, qkv_width:])
        for index, part in enumerate(parts):
            part[...] = out[index * rows : (index + 1) * rows].astype(bf16)

    return whole_kernel(
        body,
        [
            pltpu.HBM((q_width, total), bf16),
            pltpu.HBM((2 * k_width, total), bf16),
            pltpu.HBM((heads, total), f32),
            pltpu.HBM((total, q_width), bf16),
        ]
        + [jax.ShapeDtypeStruct((rows, features), bf16) for _ in slots],
        (*slots, weights, bias, cosine, sine),
        (pltpu.VMEM((q_width, total), f32), pltpu.VMEM((total, k_width), bf16)),
        free=4,
    )


def attention_backward(slots, weights, bias, cosine, sine, qt, kvt, lse, widths):
    q_width, k_width = widths
    rows, features = slots[0].shape
    total = rows * len(slots)
    heads = q_width // HD
    repeat = heads // (k_width // HD)
    qkv_width = q_width + 2 * k_width
    scale = HD ** (-0.5)

    def body(*refs):
        ms, (w, bias, cosine, sine, qt, kvt, lse) = refs[: len(slots)], refs[len(slots) : len(slots) + 7]
        grad, *parts = refs[len(slots) + 7 : -4]
        gt, gq, kv, gkv = refs[-4:]
        m = jnp.concatenate([r[...] for r in ms], axis=0)
        gt[...] = dot(m, w[:, qkv_width:]).T.astype(bf16)
        kv[...] = kvt[...].astype(f32).T.astype(bf16)
        gkv[...] = jnp.zeros(gkv.shape, f32)

        def head(h, carry):
            at = pl.ds(h * HD, HD)
            group = h // repeat
            k_at = 0 if k_width == HD else group * HD
            kt = kvt[pl.ds(k_at, HD)]
            k = kv[:, pl.ds(k_at, HD)]
            v = kv[:, pl.ds(k_width + k_at, HD)]
            q = qt[at]
            g = gt[at]
            s = dot(k, q * jnp.asarray(scale, bf16)) + bias[...]
            p = jnp.exp(s - lse[pl.ds(h, 1)])
            gp = dot(v, g)
            inner = jnp.sum(p * gp, axis=0, keepdims=True)
            gs = (p * (gp - inner) * scale).astype(bf16)
            gq[at] = dot(kt, gs)
            gk = dot_t(gs, q)
            gv = dot_t(p.astype(bf16), g)
            gkv[pl.ds(group, 1)] += jnp.concatenate([gk, gv], axis=1)[None]
            return carry

        lax.fori_loop(0, heads, head, 0, unroll=4 if heads % 4 == 0 else 1)
        cos, sin = cosine[...], -sine[...]
        both = [gkv[index].T for index in range(k_width // HD)]
        gk = jnp.concatenate([b[:HD] for b in both], axis=0)
        gv = jnp.concatenate([b[HD:] for b in both], axis=0)
        found = jnp.concatenate(
            [turn_heads(gq[...], cos, sin), turn_heads(gk, cos, sin), gv], axis=0
        ).T.astype(bf16)
        grad[...] = found
        out = dot_t(found, w[:, :qkv_width])
        for index, part in enumerate(parts):
            part[...] = out[index * rows : (index + 1) * rows].astype(bf16)

    return whole_kernel(
        body,
        [pltpu.HBM((total, qkv_width), bf16)]
        + [jax.ShapeDtypeStruct((rows, features), bf16) for _ in slots],
        (*slots, weights, bias, cosine, sine, qt, kvt, lse),
        (
            pltpu.VMEM((q_width, total), bf16),
            pltpu.VMEM((q_width, total), f32),
            pltpu.VMEM((total, 2 * k_width), bf16),
            pltpu.VMEM((k_width // HD, total, 2 * HD), f32),
        ),
        free=4,
    )


def shard_of(layer, columns, row):
    depth, rows, _ = columns[0].shape
    widths = [c.shape[2] for c in columns] + [row.shape[1]]

    def body(*refs):
        out = refs[-1]
        at, pending = 0, []
        for ref, width in zip(refs[:-2], widths):
            pending.append(ref[...])
            if sum(p.shape[1] for p in pending) % 128 == 0:
                part = pending[0] if len(pending) == 1 else jnp.concatenate(pending, axis=1)
                out[:, at : at + part.shape[1]] = part
                at, pending = at + part.shape[1], []
        assert not pending
        out[:, at:] = refs[-2][...].astype(f32).T.astype(bf16)

    return pl.pallas_call(
        body,
        grid=(1,),
        in_specs=[
            pl.BlockSpec((None, *v.shape[1:]), lambda i: (layer, 0, 0)) for v in (*columns, row)
        ],
        out_specs=pl.BlockSpec((rows, sum(widths)), lambda i: (0, 0)),
        out_shape=pltpu.HBM((rows, sum(widths)), bf16),
        cost_estimate=thin_cost(),
        compiler_params=pltpu.CompilerParams(vmem_limit_bytes=32 * 1024 * 1024),
    )(*pinned((*columns, row)))


def split_outer(groups, order_pair):
    size = lax.axis_size("fsdp")
    rows, features = groups[0][0][0].shape
    block = features // size
    if block % 128:
        whole = []
        for slots, wide, parts in groups:
            whole += outer(slots, halves(wide, rows), parts)
        return whole, [Scatter(v, o).send() for v, o in zip(whole, order_pair)]
    operands, specs, plan = [], [], []
    for slots, wide, parts in groups:
        plan.append((len(operands), len(wide), wide[0].shape[1] // parts, parts))
        for other in (1, 0):
            operands += slots
            specs += [
                pl.BlockSpec((rows, block), lambda i, c, o=other: (0, 2 * i + (c[0] + o) % 2))
                for _ in slots
            ]
        operands += wide
        specs += [pl.BlockSpec(v.shape, lambda i, c: (0, 0)) for v in wide]
    widths = [width for _, _, width, parts in plan for _ in range(parts)]

    def body(c, *refs):
        outs = list(refs[len(operands) :])
        for start, count, width, parts in plan:
            wides = refs[start + 8 : start + 8 + count]
            lefts = [
                jnp.concatenate([r[...] for r in refs[at : at + 4]], axis=0)
                for at in (start, start + 4)
            ]
            each = 4 * rows // count
            for part in range(parts):
                columns = slice(part * width, (part + 1) * width)
                for left in lefts:
                    found = sum(
                        t_dot(left[k * each : (k + 1) * each], w[:, columns])
                        for k, w in enumerate(wides)
                    )
                    outs.pop(0)[...] = found.astype(bf16)

    core = (lax.axis_index("fsdp") % 2).astype(jnp.int32)[None]
    found = pl.pallas_call(
        body,
        grid_spec=pltpu.PrefetchScalarGridSpec(
            num_scalar_prefetch=1,
            grid=(size // 2,),
            in_specs=specs,
            out_specs=[pl.BlockSpec((block, w), lambda i, c: (i, 0)) for w in widths for _ in (0, 1)],
        ),
        out_shape=[pltpu.HBM((features // 2, w), bf16) for w in widths for _ in (0, 1)],
        cost_estimate=thin_cost(),
        compiler_params=pltpu.CompilerParams(
            dimension_semantics=("arbitrary",), vmem_limit_bytes=32 * 1024 * 1024
        ),
    )(core, *pinned(operands))
    return found[1::2], found[0::2]


def halves(wide, rows):
    return wide if len(wide) == 2 else [wide[0][: 2 * rows], wide[0][2 * rows :]]


def slots_by_down(slots, weights):
    rows, features = slots[0].shape
    ff = weights.shape[1] // 3
    total = rows * len(slots)

    def body(*refs):
        i = pl.program_id(0)
        out = refs[-1]
        part = dot(jnp.concatenate([r[...] for r in refs[:-2]], axis=0), refs[-2][...])

        @pl.when(i == 0)
        def _():
            out[...] = part

        @pl.when(i > 0)
        def _():
            out[...] += part

    return run_kernel(
        body,
        features // OUTER_TILE,
        [pl.BlockSpec((rows, OUTER_TILE), lambda i: (0, i)) for _ in slots]
        + [pl.BlockSpec((OUTER_TILE, ff), lambda i: (i, 2))],
        pl.BlockSpec((total, ff), lambda i: (0, 0)),
        jax.ShapeDtypeStruct((total, ff), f32),
        (*slots, weights),
        room=24,
    )


def down_of(pairs, weights):
    both, ff = pairs[0].shape
    rows = both // 2
    features = weights.shape[0]

    def body(*refs):
        acts, w, outs = refs[:2], refs[2], refs[3:]
        part = dot_t(jnp.concatenate([r[...] for r in acts], axis=0), w[...])
        for index, out in enumerate(outs):
            out[...] = part[index * rows : (index + 1) * rows].astype(bf16)

    return run_kernel(
        body,
        features // OUTER_TILE,
        [pl.BlockSpec((both, ff), lambda i: (0, 0)) for _ in pairs]
        + [pl.BlockSpec((OUTER_TILE, ff), lambda i: (i, 2))],
        [pl.BlockSpec((rows, OUTER_TILE), lambda i: (0, i)) for _ in range(4)],
        [jax.ShapeDtypeStruct((rows, features), bf16) for _ in range(4)],
        (*pairs, weights),
        room=24,
    )


def gather_weight(values):
    return lax.all_gather(values, "fsdp", axis=0, tiled=True)


def scatter_weight(values):
    return lax.psum_scatter(values.astype(bf16), "fsdp", scatter_dimension=0, tiled=True)


def step(moving, work=None, inputs=(), launch=(), land=()):
    moving, inputs, sent = lax.optimization_barrier(
        (tuple(moving), tuple(inputs), tuple(a for a, _ in launch))
    )
    moved = tuple(shift(m) for m in moving)
    flying = tuple(exchange(a, bit) for a, (_, bit) in zip(sent, launch))
    results = () if work is None else work(*inputs)
    moved, results, landed = lax.optimization_barrier((moved, results, tuple(land)))
    return moved, results, flying, landed


def exchange(values, bit, axis="fsdp"):
    size = lax.axis_size(axis)
    return lax.ppermute(values, axis, [(i, i ^ (1 << bit)) for i in range(size)])


def fsdp_bits():
    count = lax.axis_size("fsdp").bit_length() - 1
    width = (count - 1) // 2
    return [0], list(range(1, 1 + width)), list(range(1 + width, count))


def my_bit(bit):
    return (lax.axis_index("fsdp") // (1 << bit)) % 2


def sends(*tracks):
    def work(*values):
        values, found = list(values), []
        for track in tracks:
            held, track.terms = track.terms, [values.pop(0) for _ in track.terms]
            found.append(track.send())
            track.terms = held
        return tuple(found)

    return work


def held(*tracks):
    return tuple(t for track in tracks for t in track.terms)


def flights(tracks, arrays):
    return tuple((a, t.bit) for t, a in zip(tracks, arrays))


def arrive(tracks, arrays):
    for track, values in zip(tracks, arrays):
        track.arrived(values)


def run_down(tracks, arrays, left):
    arrays = list(arrays)
    for index, track in enumerate(tracks):
        while len(track.order) - track.stage > left:
            track.arrived(exchange(arrays[index], track.bit))
            arrays[index] = track.send()
    return arrays


class Scatter:
    def __init__(self, partial, order, features=None):
        self.size = lax.axis_size("fsdp")
        self.me = lax.axis_index("fsdp")
        self.order = list(order)
        self.stage = 0
        self.terms = [partial]
        bits = sorted(order, reverse=True)
        if features is not None and partial.shape[0] < features:
            bits = bits[:-1]
        self.rows = partial.shape[0] >> len(bits)
        self.free = [bits]

    @property
    def bit(self):
        return self.order[self.stage]

    @property
    def last(self):
        return self.stage == len(self.order) - 1

    def sum_blocks(self, blocks, dtype):
        ids = jnp.stack(
            [
                sum(
                    (((blocks >> b) & 1) << (len(free) - 1 - k) for k, b in enumerate(free)),
                    jnp.zeros_like(blocks),
                )
                for free in self.free
            ]
        ).astype(jnp.int32)
        width = self.terms[0].shape[1]
        rows, count = self.rows, blocks.shape[0]

        def body(ids, *refs):
            refs[-1][...] = sum(r[...].astype(f32) for r in refs[:-1]).astype(dtype)

        return pl.pallas_call(
            body,
            grid_spec=pltpu.PrefetchScalarGridSpec(
                num_scalar_prefetch=1,
                grid=(count,),
                in_specs=[
                    pl.BlockSpec((rows, width), lambda i, ids, term=term: (ids[term, i], 0))
                    for term in range(len(self.terms))
                ],
                out_specs=pl.BlockSpec((rows, width), lambda i, ids: (i, 0)),
            ),
            out_shape=jax.ShapeDtypeStruct((count * rows, width), dtype),
            cost_estimate=thin_cost(),
            compiler_params=pltpu.CompilerParams(
                dimension_semantics=("arbitrary",), vmem_limit_bytes=16 * 1024 * 1024
            ),
        )(ids, *pinned(self.terms))

    def send(self):
        free = self.free[self.stage]
        left = [b for b in free if b != self.bit]
        each = jnp.arange(1 << len(left))
        blocks = (self.me ^ (1 << self.bit)) + jnp.zeros_like(each)
        for k, b in enumerate(left):
            blocks = (blocks & ~(1 << b)) | (((each >> (len(left) - 1 - k)) & 1) << b)
        return self.sum_blocks(blocks, bf16)

    def arrived(self, values):
        self.terms.append(values)
        self.free.append([b for b in self.free[-1] if b != self.bit])
        self.stage += 1

    def finish(self):
        total = 0.0
        for values, free in zip(self.terms, self.free):
            at = sum((((self.me >> b) & 1) << (len(free) - 1 - k) for k, b in enumerate(free)), 0)
            blocks = values.reshape(-1, self.rows, values.shape[1])
            total += lax.dynamic_index_in_dim(blocks, at, 0, keepdims=False).astype(f32)
        return total


def sum_all(values, axis):
    for bit in range(lax.axis_size(axis).bit_length() - 1):
        values = values + exchange(values, bit, axis)
    return values


def sum_to_owner(values):
    for bit in reversed(range(lax.axis_size("fsdp").bit_length() - 1)):
        low, high = jnp.split(values, 2, axis=-1)
        upper = my_bit(bit) == 1
        values = jnp.where(upper, high, low) + exchange(jnp.where(upper, low, high), bit)
    return values


def local(
    tokens,
    cotangent,
    attention_gain,
    query_weight,
    key_weight,
    value_weight,
    output_weight,
    feed_gain,
    gate_weight,
    up_weight,
    down_weight,
):
    layer_count = query_weight.shape[0]
    local_rows = tokens.shape[0]
    size = lax.axis_size("tp")
    me = lax.axis_index("tp")
    group_rows = local_rows * size
    q_width = query_weight.shape[2]
    k_width = key_weight.shape[2]
    qkv_width = q_width + 2 * k_width
    ff = gate_weight.shape[2]
    assert size == 4 and layer_count == 2

    row_index = (
        ((me - jnp.arange(size)) % size)[:, None] * local_rows + jnp.arange(local_rows)[None, :]
    ).reshape(group_rows)
    cosine, sine = (table.T for table in angle_tables(row_index % SEQ_LEN))
    seen = (row_index[:, None] <= row_index[None, :]) & (
        (row_index // SEQ_LEN)[:, None] == (row_index // SEQ_LEN)[None, :]
    )
    bias = jnp.where(seen, 0.0, masked_score).astype(f32)
    core, xs, ys = fsdp_bits()
    me_f = lax.axis_index("fsdp")
    shards = lax.axis_size("fsdp")
    shard_rows = query_weight.shape[1]
    features = shards * shard_rows

    def attention_shard(l):
        return shard_of(l, [query_weight, key_weight, value_weight], output_weight)

    def feed_shard(l):
        return shard_of(l, [gate_weight, up_weight], down_weight)

    def cat(parts):
        return jnp.concatenate(parts, axis=0)

    def norm_low(values, gain):
        return norm_rows(values, gain).astype(bf16)

    def attention(x0, x1, x2, x3, w, bias, cosine, sine):
        return tuple(
            attention_forward([x0, x1, x2, x3], w, bias, cosine, sine, (q_width, k_width))
        )

    def attention_back(m0, m1, m2, m3, w, bias, cosine, sine, qt, kvt, lse):
        return tuple(
            attention_backward(
                [m0, m1, m2, m3], w, bias, cosine, sine, qt, kvt, lse, (q_width, k_width)
            )
        )

    def add_low(moved, part):
        return (moved.astype(f32) + part).astype(bf16)

    weights_a0 = gather_weight(attention_shard(0))
    gains = jnp.zeros((shards, 2 * layer_count, shard_rows), bf16)
    gains = lax.dynamic_update_slice(
        gains, jnp.concatenate([attention_gain, feed_gain], axis=0)[None], (me_f, 0, 0)
    )
    bits = core + xs + ys

    (t1,), (gains, shard_f0), _, _ = step(
        [tokens], lambda g: (g + exchange(g, bits[0]), feed_shard(0)), (gains,)
    )
    weights_f = [gather_weight(shard_f0), None]

    def gather_gains(gains):
        for bit in bits[1:]:
            gains = gains + exchange(gains, bit)
        return (gains,)

    (t2,), (gains,), _, _ = step([t1], gather_gains, (gains,))
    gains = jnp.moveaxis(gains.astype(f32), 0, 1).reshape(2 * layer_count, features)
    gain_a, gain_f = gains[:layer_count], gains[layer_count:]

    def norm_slots(gain, *slots):
        return tuple(norm_low(v.astype(f32), gain) for v in slots)

    (t3,), (x0, x1, x2), _, _ = step([t2], norm_slots, (gain_a[0], tokens, t1, t2))
    tables = (bias, cosine, sine)
    normed0 = [x0, x1, x2, *norm_slots(gain_a[0], t3)]
    (c1,), (*saved0, mixed0, p0, p1, p2, p3), _, _ = step(
        [cotangent], attention, (*normed0, weights_a0, *tables)
    )
    residual0 = tokens.astype(f32)

    (r,), (shard_a1,), _, _ = step([p1], lambda: (attention_shard(1),))
    (r,), (shard_f1,), _, _ = step([add_low(r, p2)], lambda: (feed_shard(1),))
    weights_a1 = gather_weight(shard_a1)
    weights_f[1] = gather_weight(shard_f1)
    (r,), _, _, _ = step([add_low(r, p3)])
    hidden0 = residual0 + (r.astype(f32) + p0)

    w = weights_f[0]
    x0 = norm_low(hidden0, gain_f[0])
    (x1,), _, _, _ = step([x0])
    (x2,), _, _, _ = step([x1])
    (x3,), _, _, _ = step([x2])
    (c2,), (gu01, act01, p0, p1), _, _ = step([c1], pair_forward, (x0, x1, w))
    (r,), (gu23, act23, p2, p3), _, _ = step([p1], pair_forward, (x2, x3, w))
    (r,), _, _, _ = step([add_low(r, p2)])
    (r,), _, _, _ = step([add_low(r, p3)])
    residual1 = hidden0 + (r.astype(f32) + p0)
    feed0, gu0, act0 = [x0, x1, x2, x3], [gu01, gu23], [act01, act23]

    n0 = norm_low(residual1, gain_a[1])
    (n1,), _, _, _ = step([n0])
    (n2,), _, _, _ = step([n1])
    (n3,), _, _, _ = step([n2])
    normed1 = [n0, n1, n2, n3]
    (c3,), (*saved1, mixed1, p0, p1, p2, p3), _, _ = step(
        [c2], attention, (*normed1, weights_a1, *tables)
    )
    cots = [cotangent, c1, c2, c3]
    (r,), _, _, _ = step([p1])
    (r,), _, _, _ = step([add_low(r, p2)])
    (r,), _, _, _ = step([add_low(r, p3)])
    hidden1 = residual1 + (r.astype(f32) + p0)

    w = weights_f[1]

    x0 = norm_low(hidden1, gain_f[1])
    (x1,), (grad_act,), _, _ = step(
        [x0], lambda v, *c: (slots_by_down(c, v),), (w, *cots)
    )
    (x2,), (a01, q01, p0, p1), _, _ = step(
        [x1], lambda x, y, g, v: pair_up_back(x, y, g, 0, v), (x0, x1, grad_act, w)
    )
    (x3,), _, _, _ = step([x2])
    (r,), (a23, q23, p2, p3), _, _ = step(
        [p1], lambda x, y, g, v: pair_up_back(x, y, g, 1, v), (x2, x3, grad_act, w)
    )
    (r,), (down_part1,), _, _ = step(
        [add_low(r, p2)], lambda *v: outer(v[:4], v[4:]), (*cots, a01, a23)
    )
    down_grad1 = scatter_weight(down_part1)
    (r,), (gu_part1,), _, _ = step(
        [add_low(r, p3)],
        lambda *v: outer(v[:4], v[4:]),
        (x0, x1, x2, x3, q01, q23),
    )
    gu_grad1 = scatter_weight(gu_part1)
    grad_normed = r.astype(f32) + p0
    grad_hidden, feed_gain_part1 = jax.vjp(norm_rows, hidden1, gain_f[1])[1](grad_normed)
    grad_resid = cotangent.astype(f32) + grad_hidden

    m0 = grad_resid.astype(bf16)
    (m1,), (low0, low1, low2, low3), _, _ = step(
        [m0], lambda a, b, v: tuple(down_of([a, b], v)), (a01, a23, w)
    )
    (m2,), _, _, _ = step([m1])
    (m3,), _, _, _ = step([m2])
    (lowr,), (g, p0, p1, p2, p3), _, _ = step(
        [low1],
        attention_back,
        (m0, m1, m2, m3, weights_a1, *tables, *saved1),
    )

    order_a, order_b = core + ys + xs, core + xs + ys

    second_axis = len(ys)
    assert len(xs) == second_axis

    def outer_attention(n0, n1, n2, n3, g, m0, m1, m2, m3, mixed):
        kept, sent = split_outer(
            [([n0, n1, n2, n3], [g], 1), ([m0, m1, m2, m3], [mixed], 1)], (order_a, order_b)
        )
        return (*kept, *sent)

    (r,), (qkv, out, qkv_s, out_s), _, (down_grad1,) = step(
        [p1],
        outer_attention,
        (*normed1, g, m0, m1, m2, m3, mixed1),
        land=(down_grad1,),
    )
    att_1 = (Scatter(qkv, order_a, features), Scatter(out, order_b, features))

    def core_then_send(*tracks):
        def work(*values):
            values = list(values)
            got = [exchange(values.pop(0), 0) for _ in tracks]
            fresh = [Scatter(v, t.order, features) for t, v in zip(tracks, values)]
            arrive(fresh, got)
            return (*got, *(t.send() for t in fresh))

        return work

    (r,), landed, _, _ = step(
        [add_low(r, p2)], lambda a, b: (exchange(a, 0), exchange(b, 0)), (qkv_s, out_s)
    )
    arrive(att_1, landed)
    (r,), arrays, _, _ = step([add_low(r, p3)], sends(*att_1), held(*att_1))
    arrays = run_down(att_1, arrays, 1 + second_axis)
    grad_normed = r.astype(f32) + p0
    grad_before, attention_gain_part1 = jax.vjp(norm_rows, residual1, gain_a[1])[1](grad_normed)
    grad_resid = grad_resid + grad_before

    w = weights_f[0]

    g0 = grad_resid.astype(bf16)
    (g1,), _, flying, _ = step([g0], launch=flights(att_1, arrays))
    (g2,), (q01, p0, p1), _, landed = step(
        [g1], pair_back, (g0, g1, gu0[0], w), land=flying
    )
    arrive(att_1, landed)
    (g3,), arrays, _, _ = step([g2], sends(*att_1), held(*att_1))
    arrays = run_down(att_1, arrays, 1)
    (r,), (q23, p2, p3), flying, (gu_grad1,) = step(
        [p1],
        pair_back,
        (g2, g3, gu0[1], w),
        launch=flights(att_1, arrays),
        land=(gu_grad1,),
    )

    def gate_up(*v):
        kept, sent = split_outer([(list(v[:4]), list(v[4:]), 2)], (order_a, order_b))
        return (*kept, *sent)

    (r,), (gate, up, gate_s, up_s), _, landed = step(
        [add_low(r, p2)], gate_up, (*feed0, q01, q23), land=flying
    )
    arrive(att_1, landed)
    (r,), (gate_r, up_r, down_part0), _, _ = step(
        [add_low(r, p3)],
        lambda a, b, *v: (exchange(a, 0), exchange(b, 0), *outer(v[:4], v[4:])),
        (gate_s, up_s, g0, g1, g2, g3, *act0),
    )
    down_grad0 = scatter_weight(down_part0)
    gu_0 = (Scatter(gate, order_a, features), Scatter(up, order_b, features))
    arrive(gu_0, (gate_r, up_r))
    grad_normed = r.astype(f32) + p0
    grad_hidden, feed_gain_part0 = jax.vjp(norm_rows, hidden0, gain_f[0])[1](grad_normed)
    grad_resid = grad_resid + grad_hidden

    m0 = grad_resid.astype(bf16)
    (m1,), arrays, _, _ = step([m0], sends(*gu_0), held(*gu_0))
    arrays = run_down(gu_0, arrays, 1 + second_axis)
    (m2,), _, flying, _ = step([m1], launch=flights(gu_0, arrays))
    (m3,), _, _, _ = step([m2])
    (lowr,), (g, p0, p1, p2, p3), _, _ = step(
        [add_low(lowr, low2)],
        attention_back,
        (m0, m1, m2, m3, weights_a0, *tables, *saved0),
    )
    (r,), (qkv, out, qkv_s, out_s), _, (down_grad0, *landed) = step(
        [p1],
        outer_attention,
        (*normed0, g, m0, m1, m2, m3, mixed0),
        land=(down_grad0, *flying),
    )
    arrive(gu_0, landed)
    att_0 = (Scatter(qkv, order_a, features), Scatter(out, order_b, features))
    (r,), (qkv_r, out_r, *arrays), _, _ = step(
        [add_low(r, p2)],
        lambda *v: (*core_then_send(*att_0)(*v[:4]), *sends(*gu_0)(*v[4:])),
        (qkv_s, out_s, qkv, out, *held(*gu_0)),
    )
    arrive(att_0, (qkv_r, out_r))
    att_arrays = run_down(att_0, arrays[:2], 1 + second_axis)
    gu_arrays = run_down(gu_0, arrays[2:], 1)
    done_1 = (*att_1[0].terms, *att_1[1].terms, gu_grad1, down_grad0, down_grad1)
    (r,), _, flying, done_1 = step(
        [add_low(r, p3)],
        launch=flights(gu_0, gu_arrays) + flights(att_0, att_arrays),
        land=done_1,
    )
    count = len(att_1[0].terms)
    att_1[0].terms, att_1[1].terms = list(done_1[:count]), list(done_1[count : 2 * count])
    gu_grad1, down_grad0, down_grad1 = done_1[2 * count :]

    def last_norm(r, p0, grad_resid):
        grad_before, gain_part = jax.vjp(norm_rows, residual0, gain_a[0])[1](r.astype(f32) + p0)
        return grad_resid + grad_before, gain_part

    (lowr,), (grad_resid, attention_gain_part0), _, landed = step(
        [add_low(lowr, low3)], last_norm, (r, p0, grad_resid), land=flying
    )
    arrive(gu_0, landed[:2])
    arrive(att_0, landed[2:])
    gain_sums = jnp.stack(
        [attention_gain_part0, attention_gain_part1, feed_gain_part0, feed_gain_part1]
    )
    _, arrays, _, _ = step([], sends(*att_0), held(*att_0))
    arrays = run_down(att_0, arrays, 1)

    arrive(att_0, [exchange(a, t.bit) for a, t in zip(arrays, att_0)])
    gate_grad0, up_grad0 = (t.finish() for t in gu_0)
    qkv_grads = [t[0].finish() for t in (att_0, att_1)]
    out_grads = [t[1].finish() for t in (att_0, att_1)]
    block_out = (hidden1 + (lowr.astype(f32) + low0)).astype(bf16)

    gain_sums = sum_all(sum_to_owner(gain_sums), "tp")
    return (
        block_out,
        grad_resid,
        gain_sums[:layer_count],
        jnp.stack([p[:, :q_width] for p in qkv_grads]),
        jnp.stack([p[:, q_width : q_width + k_width] for p in qkv_grads]),
        jnp.stack([p[:, q_width + k_width :] for p in qkv_grads]),
        jnp.stack([p.T for p in out_grads]),
        gain_sums[layer_count:],
        jnp.stack([gate_grad0, gu_grad1[:, :ff].astype(f32)]),
        jnp.stack([up_grad0, gu_grad1[:, ff:].astype(f32)]),
        jnp.stack([g.astype(f32).T for g in (down_grad0, down_grad1)]),
    )


def solution(mesh):
    rows = P(("fsdp", "tp"), None)
    gain = P(None, "fsdp")
    column = P(None, "fsdp", "tp")
    row = P(None, "tp", "fsdp")
    weights = (gain, column, column, column, row, gain, column, column, row)
    return jax.shard_map(
        local,
        mesh=mesh,
        in_specs=(rows, rows) + weights,
        out_specs=(rows, rows) + weights,
        check_vma=False,
    )
```

```python
import jax
import jax.numpy as jnp
from jax import lax
from jax.experimental import pallas as pl
from jax.experimental.pallas import tpu as pltpu
from jax.sharding import PartitionSpec as P

HD = 64
SEQ_LEN = 512
epsilon = 1e-05
theta = 10000.0
masked_score = -1e30
f32 = jnp.float32
bf16 = jnp.bfloat16


def norm_rows(residual, scales):
    inverse = lax.rsqrt(jnp.mean(residual * residual, axis=-1, keepdims=True) + epsilon)
    return residual * inverse * scales


def swiglu(gate_lin, up_lin):
    return jax.nn.silu(gate_lin) * up_lin


def angle_tables(positions):
    half_width = HD // 2
    exponent = 2.0 * jnp.arange(half_width).astype(f32) / HD
    frequency = theta ** (-exponent)
    angles = positions.astype(f32)[:, None] * frequency[None, :]
    return jnp.cos(angles), jnp.sin(angles)


def shift(values):
    size = lax.axis_size("tp")
    return lax.ppermute(values, "tp", [(i, (i + 1) % size) for i in range(size)])


def dot(a, b):
    return jnp.dot(a, b, preferred_element_type=f32)


def dot_t(a, b):
    return lax.dot_general(a, b, (((1,), (1,)), ((), ())), preferred_element_type=f32)


def t_dot(a, b):
    return lax.dot_general(a, b, (((0,), (0,)), ((), ())), preferred_element_type=f32)


def thin_cost():
    return pl.CostEstimate(flops=1, bytes_accessed=1, transcendentals=0)


def pinned(args, free=0):
    return [
        a if index < free else pltpu.with_memory_space_constraint(a, pltpu.HBM)
        for index, a in enumerate(args)
    ]


def run_kernel(body, grid, in_specs, out_specs, out_shape, args, scratch=(), room=36, free=0):
    return pl.pallas_call(
        body,
        grid=(grid,),
        in_specs=in_specs,
        out_specs=out_specs,
        out_shape=out_shape,
        scratch_shapes=scratch,
        cost_estimate=thin_cost(),
        compiler_params=pltpu.CompilerParams(
            dimension_semantics=("arbitrary",), vmem_limit_bytes=room * 1024 * 1024
        ),
    )(*pinned(args, free))


TILE = 1024
OUTER_TILE = 512


def swiglu_back(gate, up, grad):
    sig = 1.0 / (1.0 + jnp.exp(-gate))
    return grad * up * (sig * (1.0 + gate * (1.0 - sig))), grad * (gate * sig), gate * sig * up


def pair_forward(xa, xb, weights):
    rows, features = xa.shape
    ff = weights.shape[1] // 3
    n = features // TILE

    def body(xa, xb, wgu, wd, gu, act, pa, pb):
        i = pl.program_id(0)

        @pl.when(i == 0)
        def _():
            gu[...] = jnp.zeros(gu.shape, f32)

        @pl.when(i < n)
        def _():
            gu[...] += dot(jnp.concatenate([xa[...], xb[...]], axis=0), wgu[...])

        @pl.when(i == n - 1)
        def _():
            gate = gu[:, :ff]
            act[...] = (gate / (1.0 + jnp.exp(-gate)) * gu[:, ff:]).astype(bf16)

        @pl.when(i >= n)
        def _():
            part = dot_t(act[...], wd[...])
            pa[...] = part[:rows].astype(bf16)
            pb[...] = part[rows:].astype(bf16)

    early = lambda i: jnp.minimum(i, n - 1)
    late = lambda i: jnp.maximum(i - n, 0)
    return run_kernel(
        body,
        2 * n,
        [
            pl.BlockSpec((rows, TILE), lambda i: (0, early(i))),
            pl.BlockSpec((rows, TILE), lambda i: (0, early(i))),
            pl.BlockSpec((TILE, 2 * ff), lambda i: (early(i), 0)),
            pl.BlockSpec((TILE, ff), lambda i: (late(i), 2)),
        ],
        [
            pl.BlockSpec((2 * rows, 2 * ff), lambda i: (0, 0)),
            pl.BlockSpec((2 * rows, ff), lambda i: (0, 0)),
            pl.BlockSpec((rows, TILE), lambda i: (0, late(i))),
            pl.BlockSpec((rows, TILE), lambda i: (0, late(i))),
        ],
        [
            pltpu.HBM((2 * rows, 2 * ff), f32),
            pltpu.HBM((2 * rows, ff), bf16),
            jax.ShapeDtypeStruct((rows, features), bf16),
            jax.ShapeDtypeStruct((rows, features), bf16),
        ],
        (xa, xb, weights, weights),
        free=2,
    )


def pair_up_back(xa, xb, grad_act, which, weights):
    rows, features = xa.shape
    ff = weights.shape[1] // 3
    n = features // TILE

    def body(xa, xb, ga, w, act, grads, pa, pb, gu):
        i = pl.program_id(0)

        @pl.when(i == 0)
        def _():
            gu[...] = jnp.zeros(gu.shape, f32)

        @pl.when(i < n)
        def _():
            gu[...] += dot(jnp.concatenate([xa[...], xb[...]], axis=0), w[...])

        @pl.when(i == n - 1)
        def _():
            dgate, dup, a = swiglu_back(gu[:, :ff], gu[:, ff:], ga[...])
            grads[:, :ff] = dgate.astype(bf16)
            grads[:, ff:] = dup.astype(bf16)
            act[...] = a.astype(bf16)

        @pl.when(i >= n)
        def _():
            part = dot_t(grads[...], w[...])
            pa[...] = part[:rows].astype(bf16)
            pb[...] = part[rows:].astype(bf16)

    early = lambda i: jnp.minimum(i, n - 1)
    late = lambda i: jnp.maximum(i - n, 0)
    return run_kernel(
        body,
        2 * n,
        [
            pl.BlockSpec((rows, TILE), lambda i: (0, early(i))),
            pl.BlockSpec((rows, TILE), lambda i: (0, early(i))),
            pl.BlockSpec((2 * rows, ff), lambda i: (which, 0)),
            pl.BlockSpec((TILE, 2 * ff), lambda i: (i % n, 0)),
        ],
        [
            pl.BlockSpec((2 * rows, ff), lambda i: (0, 0)),
            pl.BlockSpec((2 * rows, 2 * ff), lambda i: (0, 0)),
            pl.BlockSpec((rows, TILE), lambda i: (0, late(i))),
            pl.BlockSpec((rows, TILE), lambda i: (0, late(i))),
        ],
        [
            pltpu.HBM((2 * rows, ff), bf16),
            pltpu.HBM((2 * rows, 2 * ff), bf16),
            jax.ShapeDtypeStruct((rows, features), bf16),
            jax.ShapeDtypeStruct((rows, features), bf16),
        ],
        (xa, xb, grad_act, weights),
        (pltpu.VMEM((2 * rows, 2 * ff), f32),),
        free=2,
    )


def pair_back(ga, gb, gu, weights):
    rows, features = ga.shape
    ff = weights.shape[1] // 3
    n = features // TILE

    def body(ga, gb, gu, wd, wgu, grads, pa, pb, acc):
        i = pl.program_id(0)

        @pl.when(i == 0)
        def _():
            acc[...] = jnp.zeros(acc.shape, f32)

        @pl.when(i < n)
        def _():
            acc[...] += dot(jnp.concatenate([ga[...], gb[...]], axis=0), wd[...])

        @pl.when(i == n - 1)
        def _():
            dgate, dup, _ = swiglu_back(gu[:, :ff], gu[:, ff:], acc[...])
            grads[:, :ff] = dgate.astype(bf16)
            grads[:, ff:] = dup.astype(bf16)

        @pl.when(i >= n)
        def _():
            part = dot_t(grads[...], wgu[...])
            pa[...] = part[:rows].astype(bf16)
            pb[...] = part[rows:].astype(bf16)

    early = lambda i: jnp.minimum(i, n - 1)
    late = lambda i: jnp.maximum(i - n, 0)
    return run_kernel(
        body,
        2 * n,
        [
            pl.BlockSpec((rows, TILE), lambda i: (0, early(i))),
            pl.BlockSpec((rows, TILE), lambda i: (0, early(i))),
            pl.BlockSpec((2 * rows, 2 * ff), lambda i: (0, 0)),
            pl.BlockSpec((TILE, ff), lambda i: (early(i), 2)),
            pl.BlockSpec((TILE, 2 * ff), lambda i: (late(i), 0)),
        ],
        [
            pl.BlockSpec((2 * rows, 2 * ff), lambda i: (0, 0)),
            pl.BlockSpec((rows, TILE), lambda i: (0, late(i))),
            pl.BlockSpec((rows, TILE), lambda i: (0, late(i))),
        ],
        [
            pltpu.HBM((2 * rows, 2 * ff), bf16),
            jax.ShapeDtypeStruct((rows, features), bf16),
            jax.ShapeDtypeStruct((rows, features), bf16),
        ],
        (ga, gb, gu, weights, weights),
        (pltpu.VMEM((2 * rows, ff), f32),),
        free=2,
    )


def outer(slots, pairs, parts=1):
    rows, features = slots[0].shape
    width = pairs[0].shape[1] // parts

    def body(s0, s1, s2, s3, b0, b1, *outs):
        first = jnp.concatenate([s0[...], s1[...]], axis=0)
        second = jnp.concatenate([s2[...], s3[...]], axis=0)
        for index, out in enumerate(outs):
            at = slice(index * width, (index + 1) * width)
            out[...] = (t_dot(first, b0[:, at]) + t_dot(second, b1[:, at])).astype(bf16)

    return run_kernel(
        body,
        features // OUTER_TILE,
        [pl.BlockSpec((rows, OUTER_TILE), lambda i: (0, i)) for _ in slots]
        + [pl.BlockSpec((2 * rows, parts * width), lambda i: (0, 0)) for _ in pairs],
        [pl.BlockSpec((OUTER_TILE, width), lambda i: (i, 0)) for _ in range(parts)],
        [pltpu.HBM((features, width), bf16) for _ in range(parts)],
        (*slots, *pairs),
        room=24,
    )


def whole_kernel(body, out_shape, args, scratch=(), free=0):
    return pl.pallas_call(
        body,
        out_shape=out_shape,
        scratch_shapes=scratch,
        cost_estimate=thin_cost(),
        compiler_params=pltpu.CompilerParams(vmem_limit_bytes=40 * 1024 * 1024),
    )(*pinned(args, free))


def slot_results(rows, features):
    return [
        (jax.ShapeDtypeStruct if slot == 1 else pltpu.HBM)((rows, features), bf16)
        for slot in range(4)
    ]


def turn_heads(values, cosine, sine):
    half_width = HD // 2
    parts = []
    for at in range(0, values.shape[0], HD):
        first = values[at : at + half_width]
        second = values[at + half_width : at + HD]
        parts += [first * cosine - second * sine, second * cosine + first * sine]
    return jnp.concatenate(parts, axis=0)


def attention_forward(slots, weights, bias, cosine, sine, widths):
    q_width, k_width = widths
    rows, features = slots[0].shape
    total = rows * len(slots)
    heads = q_width // HD
    repeat = heads // (k_width // HD)
    qkv_width = q_width + 2 * k_width
    scale = HD ** (-0.5)

    def body(*refs):
        xs, (w, bias, cosine, sine) = refs[: len(slots)], refs[len(slots) : len(slots) + 4]
        qt, kvt, lse, mixed, *parts = refs[len(slots) + 4 : -2]
        mt, keys = refs[-2:]
        x = jnp.concatenate([r[...] for r in xs], axis=0)
        qkv = dot(x, w[:, :qkv_width]).T
        cos, sin = cosine[...], sine[...]
        qt[...] = turn_heads(qkv[:q_width], cos, sin).astype(bf16)
        kt = turn_heads(qkv[q_width : q_width + k_width], cos, sin).astype(bf16)
        kvt[:k_width] = kt
        kvt[k_width:] = qkv[q_width + k_width :].astype(bf16)
        keys[...] = kt.astype(f32).T.astype(bf16)

        def head(h, carry):
            at = pl.ds(h * HD, HD)
            group = h // repeat
            vt = kvt[pl.ds(k_width + group * HD, HD)]
            k = keys[...] if k_width == HD else keys[:, pl.ds(group * HD, HD)]
            q = qt[at] * jnp.asarray(scale, bf16)
            s = dot(k, q) + bias[...]
            largest = jnp.max(s, axis=0, keepdims=True)
            e = jnp.exp(s - largest)
            t = jnp.sum(e, axis=0, keepdims=True)
            p = (e * (1.0 / t)).astype(bf16)
            mt[at] = dot(vt, p)
            lse[pl.ds(h, 1)] = largest + jnp.log(t)
            return carry

        lax.fori_loop(0, heads, head, 0, unroll=4 if heads % 4 == 0 else 1)
        m = mt[...].T.astype(bf16)
        mixed[...] = m
        out = dot_t(m, w[:, qkv_width:])
        for index, part in enumerate(parts):
            part[...] = out[index * rows : (index + 1) * rows].astype(bf16)

    return whole_kernel(
        body,
        [
            pltpu.HBM((q_width, total), bf16),
            pltpu.HBM((2 * k_width, total), bf16),
            pltpu.HBM((heads, total), f32),
            pltpu.HBM((total, q_width), bf16),
        ]
        + slot_results(rows, features),
        (*slots, weights, bias, cosine, sine),
        (pltpu.VMEM((q_width, total), f32), pltpu.VMEM((total, k_width), bf16)),
        free=4,
    )


def attention_backward(slots, weights, bias, cosine, sine, qt, kvt, lse, widths):
    q_width, k_width = widths
    rows, features = slots[0].shape
    total = rows * len(slots)
    heads = q_width // HD
    repeat = heads // (k_width // HD)
    qkv_width = q_width + 2 * k_width
    scale = HD ** (-0.5)

    def body(*refs):
        ms, (w, bias, cosine, sine, qt, kvt, lse) = refs[: len(slots)], refs[len(slots) : len(slots) + 7]
        grad, *parts = refs[len(slots) + 7 : -4]
        gt, gq, kv, gkv = refs[-4:]
        m = jnp.concatenate([r[...] for r in ms], axis=0)
        gt[...] = dot(m, w[:, qkv_width:]).T.astype(bf16)
        kv[...] = kvt[...].astype(f32).T.astype(bf16)
        gkv[...] = jnp.zeros(gkv.shape, f32)

        def head(h, carry):
            at = pl.ds(h * HD, HD)
            group = h // repeat
            k_at = 0 if k_width == HD else group * HD
            kt = kvt[pl.ds(k_at, HD)]
            k = kv[:, pl.ds(k_at, HD)]
            v = kv[:, pl.ds(k_width + k_at, HD)]
            q = qt[at]
            g = gt[at]
            s = dot(k, q * jnp.asarray(scale, bf16)) + bias[...]
            p = jnp.exp(s - lse[pl.ds(h, 1)])
            gp = dot(v, g)
            inner = jnp.sum(p * gp, axis=0, keepdims=True)
            gs = (p * (gp - inner) * scale).astype(bf16)
            gq[at] = dot(kt, gs)
            gk = dot_t(gs, q)
            gv = dot_t(p.astype(bf16), g)
            gkv[pl.ds(group, 1)] += jnp.concatenate([gk, gv], axis=1)[None]
            return carry

        lax.fori_loop(0, heads, head, 0, unroll=4 if heads % 4 == 0 else 1)
        cos, sin = cosine[...], -sine[...]
        both = [gkv[index].T for index in range(k_width // HD)]
        gk = jnp.concatenate([b[:HD] for b in both], axis=0)
        gv = jnp.concatenate([b[HD:] for b in both], axis=0)
        found = jnp.concatenate(
            [turn_heads(gq[...], cos, sin), turn_heads(gk, cos, sin), gv], axis=0
        ).T.astype(bf16)
        grad[...] = found
        out = dot_t(found, w[:, :qkv_width])
        for index, part in enumerate(parts):
            part[...] = out[index * rows : (index + 1) * rows].astype(bf16)

    return whole_kernel(
        body,
        [pltpu.HBM((total, qkv_width), bf16)]
        + slot_results(rows, features),
        (*slots, weights, bias, cosine, sine, qt, kvt, lse),
        (
            pltpu.VMEM((q_width, total), bf16),
            pltpu.VMEM((q_width, total), f32),
            pltpu.VMEM((total, 2 * k_width), bf16),
            pltpu.VMEM((k_width // HD, total, 2 * HD), f32),
        ),
        free=4,
    )


def shard_of(layer, columns, row):
    depth, rows, _ = columns[0].shape
    widths = [c.shape[2] for c in columns] + [row.shape[1]]

    def body(*refs):
        out = refs[-1]
        at, pending = 0, []
        for ref, width in zip(refs[:-2], widths):
            pending.append(ref[...])
            if sum(p.shape[1] for p in pending) % 128 == 0:
                part = pending[0] if len(pending) == 1 else jnp.concatenate(pending, axis=1)
                out[:, at : at + part.shape[1]] = part
                at, pending = at + part.shape[1], []
        assert not pending
        out[:, at:] = refs[-2][...].astype(f32).T.astype(bf16)

    return pl.pallas_call(
        body,
        grid=(1,),
        in_specs=[
            pl.BlockSpec((None, *v.shape[1:]), lambda i: (layer, 0, 0)) for v in (*columns, row)
        ],
        out_specs=pl.BlockSpec((rows, sum(widths)), lambda i: (0, 0)),
        out_shape=pltpu.HBM((rows, sum(widths)), bf16),
        cost_estimate=thin_cost(),
        compiler_params=pltpu.CompilerParams(vmem_limit_bytes=32 * 1024 * 1024),
    )(*pinned((*columns, row)))


def split_outer(groups, order_pair):
    size = lax.axis_size("fsdp")
    rows, features = groups[0][0][0].shape
    block = features // size
    if block % 128:
        whole = []
        for slots, wide, parts in groups:
            whole += outer(slots, halves(wide, rows), parts)
        return whole, [Scatter(v, o).send() for v, o in zip(whole, order_pair)]
    operands, specs, plan = [], [], []
    for slots, wide, parts in groups:
        plan.append((len(operands), len(wide), wide[0].shape[1] // parts, parts))
        for other in (1, 0):
            operands += slots
            specs += [
                pl.BlockSpec((rows, block), lambda i, c, o=other: (0, 2 * i + (c[0] + o) % 2))
                for _ in slots
            ]
        operands += wide
        specs += [pl.BlockSpec(v.shape, lambda i, c: (0, 0)) for v in wide]
    widths = [width for _, _, width, parts in plan for _ in range(parts)]

    def body(c, *refs):
        outs = list(refs[len(operands) :])
        for start, count, width, parts in plan:
            wides = refs[start + 8 : start + 8 + count]
            lefts = [
                jnp.concatenate([r[...] for r in refs[at : at + 4]], axis=0)
                for at in (start, start + 4)
            ]
            each = 4 * rows // count
            for part in range(parts):
                columns = slice(part * width, (part + 1) * width)
                for left in lefts:
                    found = sum(
                        t_dot(left[k * each : (k + 1) * each], w[:, columns])
                        for k, w in enumerate(wides)
                    )
                    outs.pop(0)[...] = found.astype(bf16)

    core = (lax.axis_index("fsdp") % 2).astype(jnp.int32)[None]
    found = pl.pallas_call(
        body,
        grid_spec=pltpu.PrefetchScalarGridSpec(
            num_scalar_prefetch=1,
            grid=(size // 2,),
            in_specs=specs,
            out_specs=[pl.BlockSpec((block, w), lambda i, c: (i, 0)) for w in widths for _ in (0, 1)],
        ),
        out_shape=[pltpu.HBM((features // 2, w), bf16) for w in widths for _ in (0, 1)],
        cost_estimate=thin_cost(),
        compiler_params=pltpu.CompilerParams(
            dimension_semantics=("arbitrary",), vmem_limit_bytes=32 * 1024 * 1024
        ),
    )(core, *pinned(operands))
    return found[1::2], found[0::2]


def halves(wide, rows):
    return wide if len(wide) == 2 else [wide[0][: 2 * rows], wide[0][2 * rows :]]


def slots_by_down(slots, weights):
    rows, features = slots[0].shape
    ff = weights.shape[1] // 3
    total = rows * len(slots)

    def body(*refs):
        i = pl.program_id(0)
        out = refs[-1]
        part = dot(jnp.concatenate([r[...] for r in refs[:-2]], axis=0), refs[-2][...])

        @pl.when(i == 0)
        def _():
            out[...] = part

        @pl.when(i > 0)
        def _():
            out[...] += part

    return run_kernel(
        body,
        features // OUTER_TILE,
        [pl.BlockSpec((rows, OUTER_TILE), lambda i: (0, i)) for _ in slots]
        + [pl.BlockSpec((OUTER_TILE, ff), lambda i: (i, 2))],
        pl.BlockSpec((total, ff), lambda i: (0, 0)),
        pltpu.HBM((total, ff), f32),
        (*slots, weights),
        room=24,
    )


def down_of(pairs, weights):
    both, ff = pairs[0].shape
    rows = both // 2
    features = weights.shape[0]

    def body(*refs):
        acts, w, outs = refs[:2], refs[2], refs[3:]
        part = dot_t(jnp.concatenate([r[...] for r in acts], axis=0), w[...])
        for index, out in enumerate(outs):
            out[...] = part[index * rows : (index + 1) * rows].astype(bf16)

    return run_kernel(
        body,
        features // OUTER_TILE,
        [pl.BlockSpec((both, ff), lambda i: (0, 0)) for _ in pairs]
        + [pl.BlockSpec((OUTER_TILE, ff), lambda i: (i, 2))],
        [pl.BlockSpec((rows, OUTER_TILE), lambda i: (0, i)) for _ in range(4)],
        [pltpu.HBM((rows, features), bf16) for _ in range(4)],
        (*pairs, weights),
        room=24,
    )


def gather_weight(values):
    return lax.all_gather(values, "fsdp", axis=0, tiled=True)


def scatter_weight(values):
    return lax.psum_scatter(values.astype(bf16), "fsdp", scatter_dimension=0, tiled=True)


def step(moving, work=None, inputs=(), launch=(), land=()):
    moving, inputs, sent = lax.optimization_barrier(
        (tuple(moving), tuple(inputs), tuple(a for a, _ in launch))
    )
    moved = tuple(shift(m) for m in moving)
    flying = tuple(exchange(a, bit) for a, (_, bit) in zip(sent, launch))
    results = () if work is None else work(*inputs)
    moved, results, landed = lax.optimization_barrier((moved, results, tuple(land)))
    return moved, results, flying, landed


def exchange(values, bit, axis="fsdp"):
    size = lax.axis_size(axis)
    return lax.ppermute(values, axis, [(i, i ^ (1 << bit)) for i in range(size)])


def fsdp_bits():
    count = lax.axis_size("fsdp").bit_length() - 1
    width = (count - 1) // 2
    return [0], list(range(1, 1 + width)), list(range(1 + width, count))


def my_bit(bit):
    return (lax.axis_index("fsdp") // (1 << bit)) % 2


def sends(*tracks):
    def work(*values):
        values, found = list(values), []
        for track in tracks:
            held, track.terms = track.terms, [values.pop(0) for _ in track.terms]
            found.append(track.send())
            track.terms = held
        return tuple(found)

    return work


def held(*tracks):
    return tuple(t for track in tracks for t in track.terms)


def flights(tracks, arrays):
    return tuple((a, t.bit) for t, a in zip(tracks, arrays))


def arrive(tracks, arrays):
    for track, values in zip(tracks, arrays):
        track.arrived(values)


def run_down(tracks, arrays, left):
    arrays = list(arrays)
    for index, track in enumerate(tracks):
        while len(track.order) - track.stage > left:
            track.arrived(exchange(arrays[index], track.bit))
            arrays[index] = track.send()
    return arrays


class Scatter:
    def __init__(self, partial, order, features=None):
        self.size = lax.axis_size("fsdp")
        self.me = lax.axis_index("fsdp")
        self.order = list(order)
        self.stage = 0
        self.terms = [partial]
        bits = sorted(order, reverse=True)
        if features is not None and partial.shape[0] < features:
            bits = bits[:-1]
        self.rows = partial.shape[0] >> len(bits)
        self.free = [bits]

    @property
    def bit(self):
        return self.order[self.stage]

    @property
    def last(self):
        return self.stage == len(self.order) - 1

    def sum_blocks(self, blocks, dtype):
        ids = jnp.stack(
            [
                sum(
                    (((blocks >> b) & 1) << (len(free) - 1 - k) for k, b in enumerate(free)),
                    jnp.zeros_like(blocks),
                )
                for free in self.free
            ]
        ).astype(jnp.int32)
        width = self.terms[0].shape[1]
        rows, count = self.rows, blocks.shape[0]

        def body(ids, *refs):
            refs[-1][...] = sum(r[...].astype(f32) for r in refs[:-1]).astype(dtype)

        return pl.pallas_call(
            body,
            grid_spec=pltpu.PrefetchScalarGridSpec(
                num_scalar_prefetch=1,
                grid=(count,),
                in_specs=[
                    pl.BlockSpec((rows, width), lambda i, ids, term=term: (ids[term, i], 0))
                    for term in range(len(self.terms))
                ],
                out_specs=pl.BlockSpec((rows, width), lambda i, ids: (i, 0)),
            ),
            out_shape=jax.ShapeDtypeStruct((count * rows, width), dtype),
            cost_estimate=thin_cost(),
            compiler_params=pltpu.CompilerParams(
                dimension_semantics=("arbitrary",), vmem_limit_bytes=16 * 1024 * 1024
            ),
        )(ids, *pinned(self.terms))

    def send(self):
        free = self.free[self.stage]
        left = [b for b in free if b != self.bit]
        each = jnp.arange(1 << len(left))
        blocks = (self.me ^ (1 << self.bit)) + jnp.zeros_like(each)
        for k, b in enumerate(left):
            blocks = (blocks & ~(1 << b)) | (((each >> (len(left) - 1 - k)) & 1) << b)
        return self.sum_blocks(blocks, bf16)

    def arrived(self, values):
        self.terms.append(values)
        self.free.append([b for b in self.free[-1] if b != self.bit])
        self.stage += 1

    def finish(self):
        total = 0.0
        for values, free in zip(self.terms, self.free):
            at = sum((((self.me >> b) & 1) << (len(free) - 1 - k) for k, b in enumerate(free)), 0)
            blocks = values.reshape(-1, self.rows, values.shape[1])
            total += lax.dynamic_index_in_dim(blocks, at, 0, keepdims=False).astype(f32)
        return total


def sum_all(values, axis):
    for bit in range(lax.axis_size(axis).bit_length() - 1):
        values = values + exchange(values, bit, axis)
    return values


def sum_to_owner(values):
    for bit in reversed(range(lax.axis_size("fsdp").bit_length() - 1)):
        low, high = jnp.split(values, 2, axis=-1)
        upper = my_bit(bit) == 1
        values = jnp.where(upper, high, low) + exchange(jnp.where(upper, low, high), bit)
    return values


def local(
    tokens,
    cotangent,
    attention_gain,
    query_weight,
    key_weight,
    value_weight,
    output_weight,
    feed_gain,
    gate_weight,
    up_weight,
    down_weight,
):
    layer_count = query_weight.shape[0]
    local_rows = tokens.shape[0]
    size = lax.axis_size("tp")
    me = lax.axis_index("tp")
    group_rows = local_rows * size
    q_width = query_weight.shape[2]
    k_width = key_weight.shape[2]
    qkv_width = q_width + 2 * k_width
    ff = gate_weight.shape[2]
    assert size == 4 and layer_count == 2

    row_index = (
        ((me - jnp.arange(size)) % size)[:, None] * local_rows + jnp.arange(local_rows)[None, :]
    ).reshape(group_rows)
    cosine, sine = (table.T for table in angle_tables(row_index % SEQ_LEN))
    seen = (row_index[:, None] <= row_index[None, :]) & (
        (row_index // SEQ_LEN)[:, None] == (row_index // SEQ_LEN)[None, :]
    )
    bias = jnp.where(seen, 0.0, masked_score).astype(f32)
    core, xs, ys = fsdp_bits()
    me_f = lax.axis_index("fsdp")
    shards = lax.axis_size("fsdp")
    shard_rows = query_weight.shape[1]
    features = shards * shard_rows

    def attention_shard(l):
        return shard_of(l, [query_weight, key_weight, value_weight], output_weight)

    def feed_shard(l):
        return shard_of(l, [gate_weight, up_weight], down_weight)

    def cat(parts):
        return jnp.concatenate(parts, axis=0)

    def norm_low(values, gain):
        return norm_rows(values, gain).astype(bf16)

    def attention(x0, x1, x2, x3, w, bias, cosine, sine):
        return tuple(
            attention_forward([x0, x1, x2, x3], w, bias, cosine, sine, (q_width, k_width))
        )

    def attention_back(m0, m1, m2, m3, w, bias, cosine, sine, qt, kvt, lse):
        return tuple(
            attention_backward(
                [m0, m1, m2, m3], w, bias, cosine, sine, qt, kvt, lse, (q_width, k_width)
            )
        )

    def add_low(moved, part):
        return (moved.astype(f32) + part).astype(bf16)

    weights_a0 = gather_weight(attention_shard(0))
    gains = jnp.zeros((shards, 2 * layer_count, shard_rows), bf16)
    gains = lax.dynamic_update_slice(
        gains, jnp.concatenate([attention_gain, feed_gain], axis=0)[None], (me_f, 0, 0)
    )
    bits = core + xs + ys

    (t1,), (gains, shard_f0), _, _ = step(
        [tokens], lambda g: (g + exchange(g, bits[0]), feed_shard(0)), (gains,)
    )
    weights_f = [gather_weight(shard_f0), None]

    def gather_gains(gains):
        for bit in bits[1:]:
            gains = gains + exchange(gains, bit)
        return (gains,)

    (t2,), (gains,), _, _ = step([t1], gather_gains, (gains,))
    gains = jnp.moveaxis(gains.astype(f32), 0, 1).reshape(2 * layer_count, features)
    gain_a, gain_f = gains[:layer_count], gains[layer_count:]

    def norm_slots(gain, *slots):
        return tuple(norm_low(v.astype(f32), gain) for v in slots)

    (t3,), (x0, x1, x2), _, _ = step([t2], norm_slots, (gain_a[0], tokens, t1, t2))
    tables = (bias, cosine, sine)
    normed0 = [x0, x1, x2, *norm_slots(gain_a[0], t3)]
    (c1,), (*saved0, mixed0, p0, p1, p2, p3), _, _ = step(
        [cotangent], attention, (*normed0, weights_a0, *tables)
    )
    residual0 = tokens.astype(f32)

    (r,), (shard_a1,), _, _ = step([p1], lambda: (attention_shard(1),))
    (r,), (shard_f1,), _, _ = step([add_low(r, p2)], lambda: (feed_shard(1),))
    weights_a1 = gather_weight(shard_a1)
    weights_f[1] = gather_weight(shard_f1)
    (r,), _, _, _ = step([add_low(r, p3)])
    hidden0 = residual0 + (r.astype(f32) + p0)

    w = weights_f[0]
    x0 = norm_low(hidden0, gain_f[0])
    (x1,), _, _, _ = step([x0])
    (x2,), _, _, _ = step([x1])
    (x3,), _, _, _ = step([x2])
    (c2,), (gu01, act01, p0, p1), _, _ = step([c1], pair_forward, (x0, x1, w))
    (r,), (gu23, act23, p2, p3), _, _ = step([p1], pair_forward, (x2, x3, w))
    (r,), _, _, _ = step([add_low(r, p2)])
    (r,), _, _, _ = step([add_low(r, p3)])
    residual1 = hidden0 + (r.astype(f32) + p0)
    feed0, gu0, act0 = [x0, x1, x2, x3], [gu01, gu23], [act01, act23]

    n0 = norm_low(residual1, gain_a[1])
    (n1,), _, _, _ = step([n0])
    (n2,), _, _, _ = step([n1])
    (n3,), _, _, _ = step([n2])
    normed1 = [n0, n1, n2, n3]
    (c3,), (*saved1, mixed1, p0, p1, p2, p3), _, _ = step(
        [c2], attention, (*normed1, weights_a1, *tables)
    )
    cots = [cotangent, c1, c2, c3]
    (r,), _, _, _ = step([p1])
    (r,), _, _, _ = step([add_low(r, p2)])
    (r,), _, _, _ = step([add_low(r, p3)])
    hidden1 = residual1 + (r.astype(f32) + p0)

    w = weights_f[1]

    x0 = norm_low(hidden1, gain_f[1])
    (x1,), (grad_act,), _, _ = step(
        [x0], lambda v, *c: (slots_by_down(c, v),), (w, *cots)
    )
    (x2,), (a01, q01, p0, p1), _, _ = step(
        [x1], lambda x, y, g, v: pair_up_back(x, y, g, 0, v), (x0, x1, grad_act, w)
    )
    (x3,), _, _, _ = step([x2])
    (r,), (a23, q23, p2, p3), _, _ = step(
        [p1], lambda x, y, g, v: pair_up_back(x, y, g, 1, v), (x2, x3, grad_act, w)
    )
    (r,), (down_part1,), _, _ = step(
        [add_low(r, p2)], lambda *v: outer(v[:4], v[4:]), (*cots, a01, a23)
    )
    down_grad1 = scatter_weight(down_part1)
    (r,), (gu_part1,), _, _ = step(
        [add_low(r, p3)],
        lambda *v: outer(v[:4], v[4:]),
        (x0, x1, x2, x3, q01, q23),
    )
    gu_grad1 = scatter_weight(gu_part1)
    grad_normed = r.astype(f32) + p0
    grad_hidden, feed_gain_part1 = jax.vjp(norm_rows, hidden1, gain_f[1])[1](grad_normed)
    grad_resid = cotangent.astype(f32) + grad_hidden

    m0 = grad_resid.astype(bf16)
    (m1,), (low0, low1, low2, low3), _, _ = step(
        [m0], lambda a, b, v: tuple(down_of([a, b], v)), (a01, a23, w)
    )
    (m2,), _, _, _ = step([m1])
    (m3,), _, _, _ = step([m2])
    (lowr,), (g, p0, p1, p2, p3), _, _ = step(
        [low1],
        attention_back,
        (m0, m1, m2, m3, weights_a1, *tables, *saved1),
    )

    order_a, order_b = core + ys + xs, core + xs + ys

    second_axis = len(ys)
    assert len(xs) == second_axis

    def outer_attention(n0, n1, n2, n3, g, m0, m1, m2, m3, mixed):
        kept, sent = split_outer(
            [([n0, n1, n2, n3], [g], 1), ([m0, m1, m2, m3], [mixed], 1)], (order_a, order_b)
        )
        return (*kept, *(exchange(v, 0) for v in sent))

    (r,), (qkv, out, *landed), _, (down_grad1,) = step(
        [p1],
        outer_attention,
        (*normed1, g, m0, m1, m2, m3, mixed1),
        land=(down_grad1,),
    )
    att_1 = (Scatter(qkv, order_a, features), Scatter(out, order_b, features))

    arrive(att_1, landed)
    (r,), arrays, _, _ = step([add_low(r, p2)], sends(*att_1), held(*att_1))
    arrays = run_down(att_1, arrays, 1 + second_axis)
    (r,), _, flying, _ = step([add_low(r, p3)], launch=flights(att_1, arrays))
    grad_normed = r.astype(f32) + p0
    grad_before, attention_gain_part1 = jax.vjp(norm_rows, residual1, gain_a[1])[1](grad_normed)
    grad_resid = grad_resid + grad_before

    w = weights_f[0]

    g0 = grad_resid.astype(bf16)
    (g1,), _, _, landed = step([g0], land=flying)
    arrive(att_1, landed)
    (g2,), (q01, p0, p1), _, _ = step([g1], pair_back, (g0, g1, gu0[0], w))
    (g3,), arrays, _, _ = step([g2], sends(*att_1), held(*att_1))
    arrays = run_down(att_1, arrays, 1)
    (r,), (q23, p2, p3), flying, (gu_grad1,) = step(
        [p1],
        pair_back,
        (g2, g3, gu0[1], w),
        launch=flights(att_1, arrays),
        land=(gu_grad1,),
    )

    def gate_up(*v):
        kept, sent = split_outer([(list(v[:4]), list(v[4:]), 2)], (order_a, order_b))
        return (*kept, *sent)

    (r,), (gate, up, gate_s, up_s), _, landed = step(
        [add_low(r, p2)], gate_up, (*feed0, q01, q23), land=flying
    )
    arrive(att_1, landed)
    (r,), (gate_r, up_r, down_part0), _, _ = step(
        [add_low(r, p3)],
        lambda a, b, *v: (exchange(a, 0), exchange(b, 0), *outer(v[:4], v[4:])),
        (gate_s, up_s, g0, g1, g2, g3, *act0),
    )
    down_grad0 = scatter_weight(down_part0)
    gu_0 = (Scatter(gate, order_a, features), Scatter(up, order_b, features))
    arrive(gu_0, (gate_r, up_r))
    grad_normed = r.astype(f32) + p0
    grad_hidden, feed_gain_part0 = jax.vjp(norm_rows, hidden0, gain_f[0])[1](grad_normed)
    grad_resid = grad_resid + grad_hidden

    m0 = grad_resid.astype(bf16)
    (m1,), arrays, _, _ = step([m0], sends(*gu_0), held(*gu_0))
    arrays = run_down(gu_0, arrays, 1 + second_axis)
    (m2,), _, flying, _ = step([m1], launch=flights(gu_0, arrays))
    (m3,), _, _, _ = step([m2])
    (lowr,), (g, p0, p1, p2, p3), _, _ = step(
        [add_low(lowr, low2)],
        attention_back,
        (m0, m1, m2, m3, weights_a0, *tables, *saved0),
    )
    (r,), (qkv, out, *got), _, (down_grad0, *landed) = step(
        [p1],
        outer_attention,
        (*normed0, g, m0, m1, m2, m3, mixed0),
        land=(down_grad0, *flying),
    )
    arrive(gu_0, landed)
    att_0 = (Scatter(qkv, order_a, features), Scatter(out, order_b, features))
    arrive(att_0, got)
    (r,), arrays, _, _ = step(
        [add_low(r, p2)], sends(*gu_0, *att_0), held(*gu_0, *att_0)
    )
    gu_arrays = run_down(gu_0, arrays[:2], 1)
    att_arrays = run_down(att_0, arrays[2:], 1 + second_axis)
    done_1 = (*att_1[0].terms, *att_1[1].terms, gu_grad1, down_grad0, down_grad1)
    (r,), _, flying, done_1 = step(
        [add_low(r, p3)],
        launch=flights(gu_0, gu_arrays) + flights(att_0, att_arrays),
        land=done_1,
    )
    count = len(att_1[0].terms)
    att_1[0].terms, att_1[1].terms = list(done_1[:count]), list(done_1[count : 2 * count])
    gu_grad1, down_grad0, down_grad1 = done_1[2 * count :]

    grad_before, attention_gain_part0 = jax.vjp(norm_rows, residual0, gain_a[0])[1](
        r.astype(f32) + p0
    )
    grad_resid = grad_resid + grad_before
    gain_sums = jnp.stack(
        [attention_gain_part0, attention_gain_part1, feed_gain_part0, feed_gain_part1]
    )
    gain_sums = sum_all(sum_to_owner(gain_sums), "tp")
    (lowr,), _, _, landed = step([add_low(lowr, low3)], land=flying)
    arrive(gu_0, landed[:2])
    arrive(att_0, landed[2:])
    _, arrays, _, _ = step([], sends(*att_0), held(*att_0))
    arrays = run_down(att_0, arrays, 1)

    arrive(att_0, [exchange(a, t.bit) for a, t in zip(arrays, att_0)])
    gate_grad0, up_grad0 = (t.finish() for t in gu_0)
    qkv_grads = [t[0].finish() for t in (att_0, att_1)]
    out_grads = [t[1].finish() for t in (att_0, att_1)]
    block_out = (hidden1 + (lowr.astype(f32) + low0)).astype(bf16)

    return (
        block_out,
        grad_resid,
        gain_sums[:layer_count],
        jnp.stack([p[:, :q_width] for p in qkv_grads]),
        jnp.stack([p[:, q_width : q_width + k_width] for p in qkv_grads]),
        jnp.stack([p[:, q_width + k_width :] for p in qkv_grads]),
        jnp.stack([p.T for p in out_grads]),
        gain_sums[layer_count:],
        jnp.stack([gate_grad0, gu_grad1[:, :ff].astype(f32)]),
        jnp.stack([up_grad0, gu_grad1[:, ff:].astype(f32)]),
        jnp.stack([g.astype(f32).T for g in (down_grad0, down_grad1)]),
    )


def solution(mesh):
    rows = P(("fsdp", "tp"), None)
    gain = P(None, "fsdp")
    column = P(None, "fsdp", "tp")
    row = P(None, "tp", "fsdp")
    weights = (gain, column, column, column, row, gain, column, column, row)
    return jax.shard_map(
        local,
        mesh=mesh,
        in_specs=(rows, rows) + weights,
        out_specs=(rows, rows) + weights,
        check_vma=False,
    )
```

```python
import jax
import jax.numpy as jnp
from jax import lax
from jax.experimental import pallas as pl
from jax.experimental.pallas import tpu as pltpu
from jax.sharding import PartitionSpec as P

HD = 64
SEQ_LEN = 512
epsilon = 1e-05
theta = 10000.0
masked_score = -1e30
f32 = jnp.float32
bf16 = jnp.bfloat16


def norm_rows(residual, scales):
    inverse = lax.rsqrt(jnp.mean(residual * residual, axis=-1, keepdims=True) + epsilon)
    return residual * inverse * scales


def swiglu(gate_lin, up_lin):
    return jax.nn.silu(gate_lin) * up_lin


def angle_tables(positions):
    half_width = HD // 2
    exponent = 2.0 * jnp.arange(half_width).astype(f32) / HD
    frequency = theta ** (-exponent)
    angles = positions.astype(f32)[:, None] * frequency[None, :]
    return jnp.cos(angles), jnp.sin(angles)


def shift(values):
    size = lax.axis_size("tp")
    return lax.ppermute(values, "tp", [(i, (i + 1) % size) for i in range(size)])


def dot(a, b):
    return jnp.dot(a, b, preferred_element_type=f32)


def dot_t(a, b):
    return lax.dot_general(a, b, (((1,), (1,)), ((), ())), preferred_element_type=f32)


def t_dot(a, b):
    return lax.dot_general(a, b, (((0,), (0,)), ((), ())), preferred_element_type=f32)


def thin_cost():
    return pl.CostEstimate(flops=1, bytes_accessed=1, transcendentals=0)


def pinned(args, free=0):
    return [
        a if index < free else pltpu.with_memory_space_constraint(a, pltpu.HBM)
        for index, a in enumerate(args)
    ]


def run_kernel(body, grid, in_specs, out_specs, out_shape, args, scratch=(), room=36, free=0):
    return pl.pallas_call(
        body,
        grid=(grid,),
        in_specs=in_specs,
        out_specs=out_specs,
        out_shape=out_shape,
        scratch_shapes=scratch,
        cost_estimate=thin_cost(),
        compiler_params=pltpu.CompilerParams(
            dimension_semantics=("arbitrary",), vmem_limit_bytes=room * 1024 * 1024
        ),
    )(*pinned(args, free))


TILE = 1024
OUTER_TILE = 512


def swiglu_back(gate, up, grad):
    sig = 1.0 / (1.0 + jnp.exp(-gate))
    return grad * up * (sig * (1.0 + gate * (1.0 - sig))), grad * (gate * sig), gate * sig * up


def pair_forward(xa, xb, weights):
    rows, features = xa.shape
    ff = weights.shape[1] // 3
    n = features // TILE

    def body(xa, xb, wgu, wd, gu, act, pa, pb):
        i = pl.program_id(0)

        @pl.when(i == 0)
        def _():
            gu[...] = jnp.zeros(gu.shape, f32)

        @pl.when(i < n)
        def _():
            gu[...] += dot(jnp.concatenate([xa[...], xb[...]], axis=0), wgu[...])

        @pl.when(i == n - 1)
        def _():
            gate = gu[:, :ff]
            act[...] = (gate / (1.0 + jnp.exp(-gate)) * gu[:, ff:]).astype(bf16)

        @pl.when(i >= n)
        def _():
            part = dot_t(act[...], wd[...])
            pa[...] = part[:rows].astype(bf16)
            pb[...] = part[rows:].astype(bf16)

    early = lambda i: jnp.minimum(i, n - 1)
    late = lambda i: jnp.maximum(i - n, 0)
    return run_kernel(
        body,
        2 * n,
        [
            pl.BlockSpec((rows, TILE), lambda i: (0, early(i))),
            pl.BlockSpec((rows, TILE), lambda i: (0, early(i))),
            pl.BlockSpec((TILE, 2 * ff), lambda i: (early(i), 0)),
            pl.BlockSpec((TILE, ff), lambda i: (late(i), 2)),
        ],
        [
            pl.BlockSpec((2 * rows, 2 * ff), lambda i: (0, 0)),
            pl.BlockSpec((2 * rows, ff), lambda i: (0, 0)),
            pl.BlockSpec((rows, TILE), lambda i: (0, late(i))),
            pl.BlockSpec((rows, TILE), lambda i: (0, late(i))),
        ],
        [
            pltpu.HBM((2 * rows, 2 * ff), f32),
            pltpu.HBM((2 * rows, ff), bf16),
            jax.ShapeDtypeStruct((rows, features), bf16),
            jax.ShapeDtypeStruct((rows, features), bf16),
        ],
        (xa, xb, weights, weights),
        free=2,
    )


def pair_up_back(xa, xb, grad_act, which, weights):
    rows, features = xa.shape
    ff = weights.shape[1] // 3
    n = features // TILE

    def body(xa, xb, ga, w, act, grads, pa, pb, gu):
        i = pl.program_id(0)

        @pl.when(i == 0)
        def _():
            gu[...] = jnp.zeros(gu.shape, f32)

        @pl.when(i < n)
        def _():
            gu[...] += dot(jnp.concatenate([xa[...], xb[...]], axis=0), w[...])

        @pl.when(i == n - 1)
        def _():
            dgate, dup, a = swiglu_back(gu[:, :ff], gu[:, ff:], ga[...])
            grads[:, :ff] = dgate.astype(bf16)
            grads[:, ff:] = dup.astype(bf16)
            act[...] = a.astype(bf16)

        @pl.when(i >= n)
        def _():
            part = dot_t(grads[...], w[...])
            pa[...] = part[:rows].astype(bf16)
            pb[...] = part[rows:].astype(bf16)

    early = lambda i: jnp.minimum(i, n - 1)
    late = lambda i: jnp.maximum(i - n, 0)
    return run_kernel(
        body,
        2 * n,
        [
            pl.BlockSpec((rows, TILE), lambda i: (0, early(i))),
            pl.BlockSpec((rows, TILE), lambda i: (0, early(i))),
            pl.BlockSpec((2 * rows, ff), lambda i: (which, 0)),
            pl.BlockSpec((TILE, 2 * ff), lambda i: (i % n, 0)),
        ],
        [
            pl.BlockSpec((2 * rows, ff), lambda i: (0, 0)),
            pl.BlockSpec((2 * rows, 2 * ff), lambda i: (0, 0)),
            pl.BlockSpec((rows, TILE), lambda i: (0, late(i))),
            pl.BlockSpec((rows, TILE), lambda i: (0, late(i))),
        ],
        [
            pltpu.HBM((2 * rows, ff), bf16),
            pltpu.HBM((2 * rows, 2 * ff), bf16),
            jax.ShapeDtypeStruct((rows, features), bf16),
            jax.ShapeDtypeStruct((rows, features), bf16),
        ],
        (xa, xb, grad_act, weights),
        (pltpu.VMEM((2 * rows, 2 * ff), f32),),
        free=2,
    )


def pair_back(ga, gb, gu, weights):
    rows, features = ga.shape
    ff = weights.shape[1] // 3
    n = features // TILE

    def body(ga, gb, gu, wd, wgu, grads, pa, pb, acc):
        i = pl.program_id(0)

        @pl.when(i == 0)
        def _():
            acc[...] = jnp.zeros(acc.shape, f32)

        @pl.when(i < n)
        def _():
            acc[...] += dot(jnp.concatenate([ga[...], gb[...]], axis=0), wd[...])

        @pl.when(i == n - 1)
        def _():
            dgate, dup, _ = swiglu_back(gu[:, :ff], gu[:, ff:], acc[...])
            grads[:, :ff] = dgate.astype(bf16)
            grads[:, ff:] = dup.astype(bf16)

        @pl.when(i >= n)
        def _():
            part = dot_t(grads[...], wgu[...])
            pa[...] = part[:rows].astype(bf16)
            pb[...] = part[rows:].astype(bf16)

    early = lambda i: jnp.minimum(i, n - 1)
    late = lambda i: jnp.maximum(i - n, 0)
    return run_kernel(
        body,
        2 * n,
        [
            pl.BlockSpec((rows, TILE), lambda i: (0, early(i))),
            pl.BlockSpec((rows, TILE), lambda i: (0, early(i))),
            pl.BlockSpec((2 * rows, 2 * ff), lambda i: (0, 0)),
            pl.BlockSpec((TILE, ff), lambda i: (early(i), 2)),
            pl.BlockSpec((TILE, 2 * ff), lambda i: (late(i), 0)),
        ],
        [
            pl.BlockSpec((2 * rows, 2 * ff), lambda i: (0, 0)),
            pl.BlockSpec((rows, TILE), lambda i: (0, late(i))),
            pl.BlockSpec((rows, TILE), lambda i: (0, late(i))),
        ],
        [
            pltpu.HBM((2 * rows, 2 * ff), bf16),
            jax.ShapeDtypeStruct((rows, features), bf16),
            jax.ShapeDtypeStruct((rows, features), bf16),
        ],
        (ga, gb, gu, weights, weights),
        (pltpu.VMEM((2 * rows, ff), f32),),
        free=2,
    )


def outer(slots, pairs, parts=1):
    rows, features = slots[0].shape
    width = pairs[0].shape[1] // parts

    def body(s0, s1, s2, s3, b0, b1, *outs):
        first = jnp.concatenate([s0[...], s1[...]], axis=0)
        second = jnp.concatenate([s2[...], s3[...]], axis=0)
        for index, out in enumerate(outs):
            at = slice(index * width, (index + 1) * width)
            out[...] = (t_dot(first, b0[:, at]) + t_dot(second, b1[:, at])).astype(bf16)

    return run_kernel(
        body,
        features // OUTER_TILE,
        [pl.BlockSpec((rows, OUTER_TILE), lambda i: (0, i)) for _ in slots]
        + [pl.BlockSpec((2 * rows, parts * width), lambda i: (0, 0)) for _ in pairs],
        [pl.BlockSpec((OUTER_TILE, width), lambda i: (i, 0)) for _ in range(parts)],
        [pltpu.HBM((features, width), bf16) for _ in range(parts)],
        (*slots, *pairs),
        room=24,
    )


def whole_kernel(body, out_shape, args, scratch=(), free=0):
    return pl.pallas_call(
        body,
        out_shape=out_shape,
        scratch_shapes=scratch,
        cost_estimate=thin_cost(),
        compiler_params=pltpu.CompilerParams(vmem_limit_bytes=40 * 1024 * 1024),
    )(*pinned(args, free))


def turn_heads(values, cosine, sine):
    half_width = HD // 2
    parts = []
    for at in range(0, values.shape[0], HD):
        first = values[at : at + half_width]
        second = values[at + half_width : at + HD]
        parts += [first * cosine - second * sine, second * cosine + first * sine]
    return jnp.concatenate(parts, axis=0)


def attention_forward(slots, weights, bias, cosine, sine, widths):
    q_width, k_width = widths
    rows, features = slots[0].shape
    total = rows * len(slots)
    heads = q_width // HD
    repeat = heads // (k_width // HD)
    qkv_width = q_width + 2 * k_width
    scale = HD ** (-0.5)

    def body(*refs):
        xs, (w, bias, cosine, sine) = refs[: len(slots)], refs[len(slots) : len(slots) + 4]
        qt, kvt, lse, mixed, *parts = refs[len(slots) + 4 : -2]
        mt, keys = refs[-2:]
        x = jnp.concatenate([r[...] for r in xs], axis=0)
        qkv = dot(x, w[:, :qkv_width]).T
        cos, sin = cosine[...], sine[...]
        qt[...] = turn_heads(qkv[:q_width], cos, sin).astype(bf16)
        kt = turn_heads(qkv[q_width : q_width + k_width], cos, sin).astype(bf16)
        kvt[:k_width] = kt
        kvt[k_width:] = qkv[q_width + k_width :].astype(bf16)
        keys[...] = kt.astype(f32).T.astype(bf16)

        def head(h, carry):
            at = pl.ds(h * HD, HD)
            group = h // repeat
            vt = kvt[pl.ds(k_width + group * HD, HD)]
            k = keys[...] if k_width == HD else keys[:, pl.ds(group * HD, HD)]
            q = qt[at] * jnp.asarray(scale, bf16)
            s = dot(k, q) + bias[...]
            largest = jnp.max(s, axis=0, keepdims=True)
            e = jnp.exp(s - largest)
            t = jnp.sum(e, axis=0, keepdims=True)
            p = (e * (1.0 / t)).astype(bf16)
            mt[at] = dot(vt, p)
            lse[pl.ds(h, 1)] = largest + jnp.log(t)
            return carry

        lax.fori_loop(0, heads, head, 0, unroll=4 if heads % 4 == 0 else 1)
        m = mt[...].T.astype(bf16)
        mixed[...] = m
        out = dot_t(m, w[:, qkv_width:])
        for index, part in enumerate(parts):
            part[...] = out[index * rows : (index + 1) * rows].astype(bf16)

    return whole_kernel(
        body,
        [
            pltpu.HBM((q_width, total), bf16),
            pltpu.HBM((2 * k_width, total), bf16),
            pltpu.HBM((heads, total), f32),
            pltpu.HBM((total, q_width), bf16),
        ]
        + [jax.ShapeDtypeStruct((rows, features), bf16) for _ in slots],
        (*slots, weights, bias, cosine, sine),
        (pltpu.VMEM((q_width, total), f32), pltpu.VMEM((total, k_width), bf16)),
        free=4,
    )


def attention_backward(slots, weights, bias, cosine, sine, qt, kvt, lse, widths):
    q_width, k_width = widths
    rows, features = slots[0].shape
    total = rows * len(slots)
    heads = q_width // HD
    repeat = heads // (k_width // HD)
    qkv_width = q_width + 2 * k_width
    scale = HD ** (-0.5)

    def body(*refs):
        ms, (w, bias, cosine, sine, qt, kvt, lse) = refs[: len(slots)], refs[len(slots) : len(slots) + 7]
        grad, *parts = refs[len(slots) + 7 : -4]
        gt, gq, kv, gkv = refs[-4:]
        m = jnp.concatenate([r[...] for r in ms], axis=0)
        gt[...] = dot(m, w[:, qkv_width:]).T.astype(bf16)
        kv[...] = kvt[...].astype(f32).T.astype(bf16)
        gkv[...] = jnp.zeros(gkv.shape, f32)

        def head(h, carry):
            at = pl.ds(h * HD, HD)
            group = h // repeat
            k_at = 0 if k_width == HD else group * HD
            kt = kvt[pl.ds(k_at, HD)]
            k = kv[:, pl.ds(k_at, HD)]
            v = kv[:, pl.ds(k_width + k_at, HD)]
            q = qt[at]
            g = gt[at]
            s = dot(k, q * jnp.asarray(scale, bf16)) + bias[...]
            p = jnp.exp(s - lse[pl.ds(h, 1)])
            gp = dot(v, g)
            inner = jnp.sum(p * gp, axis=0, keepdims=True)
            gs = (p * (gp - inner) * scale).astype(bf16)
            gq[at] = dot(kt, gs)
            gk = dot_t(gs, q)
            gv = dot_t(p.astype(bf16), g)
            gkv[pl.ds(group, 1)] += jnp.concatenate([gk, gv], axis=1)[None]
            return carry

        lax.fori_loop(0, heads, head, 0, unroll=4 if heads % 4 == 0 else 1)
        cos, sin = cosine[...], -sine[...]
        both = [gkv[index].T for index in range(k_width // HD)]
        gk = jnp.concatenate([b[:HD] for b in both], axis=0)
        gv = jnp.concatenate([b[HD:] for b in both], axis=0)
        found = jnp.concatenate(
            [turn_heads(gq[...], cos, sin), turn_heads(gk, cos, sin), gv], axis=0
        ).T.astype(bf16)
        grad[...] = found
        out = dot_t(found, w[:, :qkv_width])
        for index, part in enumerate(parts):
            part[...] = out[index * rows : (index + 1) * rows].astype(bf16)

    return whole_kernel(
        body,
        [pltpu.HBM((total, qkv_width), bf16)]
        + [jax.ShapeDtypeStruct((rows, features), bf16) for _ in slots],
        (*slots, weights, bias, cosine, sine, qt, kvt, lse),
        (
            pltpu.VMEM((q_width, total), bf16),
            pltpu.VMEM((q_width, total), f32),
            pltpu.VMEM((total, 2 * k_width), bf16),
            pltpu.VMEM((k_width // HD, total, 2 * HD), f32),
        ),
        free=4,
    )


def shard_of(layer, columns, row):
    depth, rows, _ = columns[0].shape
    widths = [c.shape[2] for c in columns] + [row.shape[1]]

    def body(*refs):
        out = refs[-1]
        at, pending = 0, []
        for ref, width in zip(refs[:-2], widths):
            pending.append(ref[...])
            if sum(p.shape[1] for p in pending) % 128 == 0:
                part = pending[0] if len(pending) == 1 else jnp.concatenate(pending, axis=1)
                out[:, at : at + part.shape[1]] = part
                at, pending = at + part.shape[1], []
        assert not pending
        out[:, at:] = refs[-2][...].astype(f32).T.astype(bf16)

    return pl.pallas_call(
        body,
        grid=(1,),
        in_specs=[
            pl.BlockSpec((None, *v.shape[1:]), lambda i: (layer, 0, 0)) for v in (*columns, row)
        ],
        out_specs=pl.BlockSpec((rows, sum(widths)), lambda i: (0, 0)),
        out_shape=pltpu.HBM((rows, sum(widths)), bf16),
        cost_estimate=thin_cost(),
        compiler_params=pltpu.CompilerParams(vmem_limit_bytes=32 * 1024 * 1024),
    )(*pinned((*columns, row)))


def split_outer(groups, order_pair):
    size = lax.axis_size("fsdp")
    rows, features = groups[0][0][0].shape
    block = features // size
    if block % 128:
        whole = []
        for slots, wide, parts in groups:
            whole += outer(slots, halves(wide, rows), parts)
        return whole, [Scatter(v, o).send() for v, o in zip(whole, order_pair)]
    operands, specs, plan = [], [], []
    for slots, wide, parts in groups:
        plan.append((len(operands), len(wide), wide[0].shape[1] // parts, parts))
        for other in (1, 0):
            operands += slots
            specs += [
                pl.BlockSpec((rows, block), lambda i, c, o=other: (0, 2 * i + (c[0] + o) % 2))
                for _ in slots
            ]
        operands += wide
        specs += [pl.BlockSpec(v.shape, lambda i, c: (0, 0)) for v in wide]
    widths = [width for _, _, width, parts in plan for _ in range(parts)]

    def body(c, *refs):
        outs = list(refs[len(operands) :])
        for start, count, width, parts in plan:
            wides = refs[start + 8 : start + 8 + count]
            lefts = [
                jnp.concatenate([r[...] for r in refs[at : at + 4]], axis=0)
                for at in (start, start + 4)
            ]
            each = 4 * rows // count
            for part in range(parts):
                columns = slice(part * width, (part + 1) * width)
                for left in lefts:
                    found = sum(
                        t_dot(left[k * each : (k + 1) * each], w[:, columns])
                        for k, w in enumerate(wides)
                    )
                    outs.pop(0)[...] = found.astype(bf16)

    core = (lax.axis_index("fsdp") % 2).astype(jnp.int32)[None]
    found = pl.pallas_call(
        body,
        grid_spec=pltpu.PrefetchScalarGridSpec(
            num_scalar_prefetch=1,
            grid=(size // 2,),
            in_specs=specs,
            out_specs=[pl.BlockSpec((block, w), lambda i, c: (i, 0)) for w in widths for _ in (0, 1)],
        ),
        out_shape=[pltpu.HBM((features // 2, w), bf16) for w in widths for _ in (0, 1)],
        cost_estimate=thin_cost(),
        compiler_params=pltpu.CompilerParams(
            dimension_semantics=("arbitrary",), vmem_limit_bytes=32 * 1024 * 1024
        ),
    )(core, *pinned(operands))
    return found[1::2], found[0::2]


def halves(wide, rows):
    return wide if len(wide) == 2 else [wide[0][: 2 * rows], wide[0][2 * rows :]]


def slots_by_down(slots, weights):
    rows, features = slots[0].shape
    ff = weights.shape[1] // 3
    total = rows * len(slots)

    def body(*refs):
        i = pl.program_id(0)
        out = refs[-1]
        part = dot(jnp.concatenate([r[...] for r in refs[:-2]], axis=0), refs[-2][...])

        @pl.when(i == 0)
        def _():
            out[...] = part

        @pl.when(i > 0)
        def _():
            out[...] += part

    return run_kernel(
        body,
        features // OUTER_TILE,
        [pl.BlockSpec((rows, OUTER_TILE), lambda i: (0, i)) for _ in slots]
        + [pl.BlockSpec((OUTER_TILE, ff), lambda i: (i, 2))],
        pl.BlockSpec((total, ff), lambda i: (0, 0)),
        jax.ShapeDtypeStruct((total, ff), f32),
        (*slots, weights),
        room=24,
    )


def down_of(pairs, weights):
    both, ff = pairs[0].shape
    rows = both // 2
    features = weights.shape[0]

    def body(*refs):
        acts, w, outs = refs[:2], refs[2], refs[3:]
        part = dot_t(jnp.concatenate([r[...] for r in acts], axis=0), w[...])
        for index, out in enumerate(outs):
            out[...] = part[index * rows : (index + 1) * rows].astype(bf16)

    return run_kernel(
        body,
        features // OUTER_TILE,
        [pl.BlockSpec((both, ff), lambda i: (0, 0)) for _ in pairs]
        + [pl.BlockSpec((OUTER_TILE, ff), lambda i: (i, 2))],
        [pl.BlockSpec((rows, OUTER_TILE), lambda i: (0, i)) for _ in range(4)],
        [jax.ShapeDtypeStruct((rows, features), bf16) for _ in range(4)],
        (*pairs, weights),
        room=24,
    )


def gather_weight(values):
    return lax.all_gather(values, "fsdp", axis=0, tiled=True)


def scatter_weight(values):
    return lax.psum_scatter(values.astype(bf16), "fsdp", scatter_dimension=0, tiled=True)


def step(moving, work=None, inputs=(), launch=(), land=()):
    moving, inputs, sent = lax.optimization_barrier(
        (tuple(moving), tuple(inputs), tuple(a for a, _ in launch))
    )
    moved = tuple(shift(m) for m in moving)
    flying = tuple(exchange(a, bit) for a, (_, bit) in zip(sent, launch))
    results = () if work is None else work(*inputs)
    moved, results, landed = lax.optimization_barrier((moved, results, tuple(land)))
    return moved, results, flying, landed


def exchange(values, bit, axis="fsdp"):
    size = lax.axis_size(axis)
    return lax.ppermute(values, axis, [(i, i ^ (1 << bit)) for i in range(size)])


def fsdp_bits():
    count = lax.axis_size("fsdp").bit_length() - 1
    width = (count - 1) // 2
    return [0], list(range(1, 1 + width)), list(range(1 + width, count))


def my_bit(bit):
    return (lax.axis_index("fsdp") // (1 << bit)) % 2


def sends(*tracks):
    def work(*values):
        values, found = list(values), []
        for track in tracks:
            held, track.terms = track.terms, [values.pop(0) for _ in track.terms]
            found.append(track.send())
            track.terms = held
        return tuple(found)

    return work


def held(*tracks):
    return tuple(t for track in tracks for t in track.terms)


def flights(tracks, arrays):
    return tuple((a, t.bit) for t, a in zip(tracks, arrays))


def arrive(tracks, arrays):
    for track, values in zip(tracks, arrays):
        track.arrived(values)


def run_down(tracks, arrays, left):
    arrays = list(arrays)
    for index, track in enumerate(tracks):
        while len(track.order) - track.stage > left:
            track.arrived(exchange(arrays[index], track.bit))
            arrays[index] = track.send()
    return arrays


class Scatter:
    def __init__(self, partial, order, features=None):
        self.size = lax.axis_size("fsdp")
        self.me = lax.axis_index("fsdp")
        self.order = list(order)
        self.stage = 0
        self.terms = [partial]
        bits = sorted(order, reverse=True)
        if features is not None and partial.shape[0] < features:
            bits = bits[:-1]
        self.rows = partial.shape[0] >> len(bits)
        self.free = [bits]

    @property
    def bit(self):
        return self.order[self.stage]

    @property
    def last(self):
        return self.stage == len(self.order) - 1

    def sum_blocks(self, blocks, dtype):
        ids = jnp.stack(
            [
                sum(
                    (((blocks >> b) & 1) << (len(free) - 1 - k) for k, b in enumerate(free)),
                    jnp.zeros_like(blocks),
                )
                for free in self.free
            ]
        ).astype(jnp.int32)
        width = self.terms[0].shape[1]
        rows, count = self.rows, blocks.shape[0]

        def body(ids, *refs):
            refs[-1][...] = sum(r[...].astype(f32) for r in refs[:-1]).astype(dtype)

        return pl.pallas_call(
            body,
            grid_spec=pltpu.PrefetchScalarGridSpec(
                num_scalar_prefetch=1,
                grid=(count,),
                in_specs=[
                    pl.BlockSpec((rows, width), lambda i, ids, term=term: (ids[term, i], 0))
                    for term in range(len(self.terms))
                ],
                out_specs=pl.BlockSpec((rows, width), lambda i, ids: (i, 0)),
            ),
            out_shape=jax.ShapeDtypeStruct((count * rows, width), dtype),
            cost_estimate=thin_cost(),
            compiler_params=pltpu.CompilerParams(
                dimension_semantics=("arbitrary",), vmem_limit_bytes=16 * 1024 * 1024
            ),
        )(ids, *pinned(self.terms))

    def send(self):
        free = self.free[self.stage]
        left = [b for b in free if b != self.bit]
        each = jnp.arange(1 << len(left))
        blocks = (self.me ^ (1 << self.bit)) + jnp.zeros_like(each)
        for k, b in enumerate(left):
            blocks = (blocks & ~(1 << b)) | (((each >> (len(left) - 1 - k)) & 1) << b)
        return self.sum_blocks(blocks, bf16)

    def arrived(self, values):
        self.terms.append(values)
        self.free.append([b for b in self.free[-1] if b != self.bit])
        self.stage += 1

    def finish(self):
        total = 0.0
        for values, free in zip(self.terms, self.free):
            at = sum((((self.me >> b) & 1) << (len(free) - 1 - k) for k, b in enumerate(free)), 0)
            blocks = values.reshape(-1, self.rows, values.shape[1])
            total += lax.dynamic_index_in_dim(blocks, at, 0, keepdims=False).astype(f32)
        return total


def sum_all(values, axis):
    for bit in range(lax.axis_size(axis).bit_length() - 1):
        values = values + exchange(values, bit, axis)
    return values


def sum_to_owner(values):
    for bit in reversed(range(lax.axis_size("fsdp").bit_length() - 1)):
        low, high = jnp.split(values, 2, axis=-1)
        upper = my_bit(bit) == 1
        values = jnp.where(upper, high, low) + exchange(jnp.where(upper, low, high), bit)
    return values


def local(
    tokens,
    cotangent,
    attention_gain,
    query_weight,
    key_weight,
    value_weight,
    output_weight,
    feed_gain,
    gate_weight,
    up_weight,
    down_weight,
):
    layer_count = query_weight.shape[0]
    local_rows = tokens.shape[0]
    size = lax.axis_size("tp")
    me = lax.axis_index("tp")
    group_rows = local_rows * size
    q_width = query_weight.shape[2]
    k_width = key_weight.shape[2]
    qkv_width = q_width + 2 * k_width
    ff = gate_weight.shape[2]
    assert size == 4 and layer_count == 2

    row_index = (
        ((me - jnp.arange(size)) % size)[:, None] * local_rows + jnp.arange(local_rows)[None, :]
    ).reshape(group_rows)
    cosine, sine = (table.T for table in angle_tables(row_index % SEQ_LEN))
    seen = (row_index[:, None] <= row_index[None, :]) & (
        (row_index // SEQ_LEN)[:, None] == (row_index // SEQ_LEN)[None, :]
    )
    bias = jnp.where(seen, 0.0, masked_score).astype(f32)
    core, xs, ys = fsdp_bits()
    me_f = lax.axis_index("fsdp")
    shards = lax.axis_size("fsdp")
    shard_rows = query_weight.shape[1]
    features = shards * shard_rows

    def attention_shard(l):
        return shard_of(l, [query_weight, key_weight, value_weight], output_weight)

    def feed_shard(l):
        return shard_of(l, [gate_weight, up_weight], down_weight)

    def cat(parts):
        return jnp.concatenate(parts, axis=0)

    def norm_low(values, gain):
        return norm_rows(values, gain).astype(bf16)

    def attention(x0, x1, x2, x3, w, bias, cosine, sine):
        return tuple(
            attention_forward([x0, x1, x2, x3], w, bias, cosine, sine, (q_width, k_width))
        )

    def attention_back(m0, m1, m2, m3, w, bias, cosine, sine, qt, kvt, lse):
        return tuple(
            attention_backward(
                [m0, m1, m2, m3], w, bias, cosine, sine, qt, kvt, lse, (q_width, k_width)
            )
        )

    def add_low(moved, part):
        return (moved.astype(f32) + part).astype(bf16)

    weights_a0 = gather_weight(attention_shard(0))
    gains = jnp.zeros((shards, 2 * layer_count, shard_rows), bf16)
    gains = lax.dynamic_update_slice(
        gains, jnp.concatenate([attention_gain, feed_gain], axis=0)[None], (me_f, 0, 0)
    )
    bits = core + xs + ys

    (t1,), (gains, shard_f0), _, _ = step(
        [tokens], lambda g: (g + exchange(g, bits[0]), feed_shard(0)), (gains,)
    )
    weights_f = [gather_weight(shard_f0), None]

    def gather_gains(gains):
        for bit in bits[1:]:
            gains = gains + exchange(gains, bit)
        return (gains,)

    (t2,), (gains,), _, _ = step([t1], gather_gains, (gains,))
    gains = jnp.moveaxis(gains.astype(f32), 0, 1).reshape(2 * layer_count, features)
    gain_a, gain_f = gains[:layer_count], gains[layer_count:]

    def norm_slots(gain, *slots):
        return tuple(norm_low(v.astype(f32), gain) for v in slots)

    (t3,), (x0, x1, x2), _, _ = step([t2], norm_slots, (gain_a[0], tokens, t1, t2))
    tables = (bias, cosine, sine)
    normed0 = [x0, x1, x2, *norm_slots(gain_a[0], t3)]
    (c1,), (*saved0, mixed0, p0, p1, p2, p3), _, _ = step(
        [cotangent], attention, (*normed0, weights_a0, *tables)
    )
    residual0 = tokens.astype(f32)

    (r,), (shard_a1,), _, _ = step([p1], lambda: (attention_shard(1),))
    (r,), (shard_f1,), _, _ = step([add_low(r, p2)], lambda: (feed_shard(1),))
    weights_a1 = gather_weight(shard_a1)
    weights_f[1] = gather_weight(shard_f1)
    (r,), _, _, _ = step([add_low(r, p3)])
    hidden0 = residual0 + (r.astype(f32) + p0)

    w = weights_f[0]
    x0 = norm_low(hidden0, gain_f[0])
    (x1,), _, _, _ = step([x0])
    (x2,), _, _, _ = step([x1])
    (x3,), _, _, _ = step([x2])
    (c2,), (gu01, act01, p0, p1), _, _ = step([c1], pair_forward, (x0, x1, w))
    (r,), (gu23, act23, p2, p3), _, _ = step([p1], pair_forward, (x2, x3, w))
    (r,), _, _, _ = step([add_low(r, p2)])
    (r,), _, _, _ = step([add_low(r, p3)])
    residual1 = hidden0 + (r.astype(f32) + p0)
    feed0, gu0, act0 = [x0, x1, x2, x3], [gu01, gu23], [act01, act23]

    n0 = norm_low(residual1, gain_a[1])
    (n1,), _, _, _ = step([n0])
    (n2,), _, _, _ = step([n1])
    (n3,), _, _, _ = step([n2])
    normed1 = [n0, n1, n2, n3]
    (c3,), (*saved1, mixed1, p0, p1, p2, p3), _, _ = step(
        [c2], attention, (*normed1, weights_a1, *tables)
    )
    cots = [cotangent, c1, c2, c3]
    (r,), _, _, _ = step([p1])
    (r,), _, _, _ = step([add_low(r, p2)])
    (r,), _, _, _ = step([add_low(r, p3)])
    hidden1 = residual1 + (r.astype(f32) + p0)

    w = weights_f[1]

    x0 = norm_low(hidden1, gain_f[1])
    (x1,), (grad_act,), _, _ = step(
        [x0], lambda v, *c: (slots_by_down(c, v),), (w, *cots)
    )
    (x2,), (a01, q01, p0, p1), _, _ = step(
        [x1], lambda x, y, g, v: pair_up_back(x, y, g, 0, v), (x0, x1, grad_act, w)
    )
    (x3,), _, _, _ = step([x2])
    (r,), (a23, q23, p2, p3), _, _ = step(
        [p1], lambda x, y, g, v: pair_up_back(x, y, g, 1, v), (x2, x3, grad_act, w)
    )
    (r,), (down_part1,), _, _ = step(
        [add_low(r, p2)], lambda *v: outer(v[:4], v[4:]), (*cots, a01, a23)
    )
    down_grad1 = scatter_weight(down_part1)
    (r,), (gu_part1,), _, _ = step(
        [add_low(r, p3)],
        lambda *v: outer(v[:4], v[4:]),
        (x0, x1, x2, x3, q01, q23),
    )
    gu_grad1 = scatter_weight(gu_part1)
    grad_normed = r.astype(f32) + p0
    grad_hidden, feed_gain_part1 = jax.vjp(norm_rows, hidden1, gain_f[1])[1](grad_normed)
    grad_resid = cotangent.astype(f32) + grad_hidden

    m0 = grad_resid.astype(bf16)
    (m1,), (low0, low1, low2, low3), _, _ = step(
        [m0], lambda a, b, v: tuple(down_of([a, b], v)), (a01, a23, w)
    )
    (m2,), _, _, _ = step([m1])
    (m3,), _, _, _ = step([m2])
    (lowr,), (g, p0, p1, p2, p3), _, _ = step(
        [low1],
        attention_back,
        (m0, m1, m2, m3, weights_a1, *tables, *saved1),
    )

    order_a, order_b = core + ys + xs, core + xs + ys

    second_axis = len(ys)
    assert len(xs) == second_axis

    def outer_attention(n0, n1, n2, n3, g, m0, m1, m2, m3, mixed):
        kept, sent = split_outer(
            [([n0, n1, n2, n3], [g], 1), ([m0, m1, m2, m3], [mixed], 1)], (order_a, order_b)
        )
        return (*kept, *sent)

    (r,), (qkv, out, qkv_s, out_s), _, (down_grad1,) = step(
        [p1],
        outer_attention,
        (*normed1, g, m0, m1, m2, m3, mixed1),
        land=(down_grad1,),
    )
    att_1 = (Scatter(qkv, order_a, features), Scatter(out, order_b, features))

    def core_then_send(*tracks):
        def work(*values):
            values = list(values)
            got = [exchange(values.pop(0), 0) for _ in tracks]
            fresh = [Scatter(v, t.order, features) for t, v in zip(tracks, values)]
            arrive(fresh, got)
            return (*got, *(t.send() for t in fresh))

        return work

    (r,), landed, _, _ = step(
        [add_low(r, p2)], lambda a, b: (exchange(a, 0), exchange(b, 0)), (qkv_s, out_s)
    )
    arrive(att_1, landed)
    (r,), arrays, _, _ = step([add_low(r, p3)], sends(*att_1), held(*att_1))
    arrays = run_down(att_1, arrays, 1 + second_axis)
    grad_normed = r.astype(f32) + p0
    grad_before, attention_gain_part1 = jax.vjp(norm_rows, residual1, gain_a[1])[1](grad_normed)
    grad_resid = grad_resid + grad_before

    w = weights_f[0]

    g0 = grad_resid.astype(bf16)
    (g1,), _, flying, _ = step([g0], launch=flights(att_1, arrays))
    (g2,), (q01, p0, p1), _, landed = step(
        [g1], pair_back, (g0, g1, gu0[0], w), land=flying
    )
    arrive(att_1, landed)
    (g3,), arrays, _, _ = step([g2], sends(*att_1), held(*att_1))
    arrays = run_down(att_1, arrays, 1)
    (r,), (q23, p2, p3), flying, (gu_grad1,) = step(
        [p1],
        pair_back,
        (g2, g3, gu0[1], w),
        launch=flights(att_1, arrays),
        land=(gu_grad1,),
    )

    def gate_up(*v):
        kept, sent = split_outer([(list(v[:4]), list(v[4:]), 2)], (order_a, order_b))
        return (*kept, *sent)

    (r,), (gate, up, gate_s, up_s), _, landed = step(
        [add_low(r, p2)], gate_up, (*feed0, q01, q23), land=flying
    )
    arrive(att_1, landed)
    (r,), (gate_r, up_r, down_part0), _, _ = step(
        [add_low(r, p3)],
        lambda a, b, *v: (exchange(a, 0), exchange(b, 0), *outer(v[:4], v[4:])),
        (gate_s, up_s, g0, g1, g2, g3, *act0),
    )
    down_grad0 = scatter_weight(down_part0)
    gu_0 = (Scatter(gate, order_a, features), Scatter(up, order_b, features))
    arrive(gu_0, (gate_r, up_r))
    grad_normed = r.astype(f32) + p0
    grad_hidden, feed_gain_part0 = jax.vjp(norm_rows, hidden0, gain_f[0])[1](grad_normed)
    grad_resid = grad_resid + grad_hidden

    m0 = grad_resid.astype(bf16)
    (m1,), arrays, _, _ = step([m0], sends(*gu_0), held(*gu_0))
    arrays = run_down(gu_0, arrays, 1 + second_axis)
    (m2,), _, flying, _ = step([m1], launch=flights(gu_0, arrays))
    (m3,), _, _, _ = step([m2])
    (lowr,), (g, p0, p1, p2, p3), _, _ = step(
        [add_low(lowr, low2)],
        attention_back,
        (m0, m1, m2, m3, weights_a0, *tables, *saved0),
    )
    (r,), (qkv, out, qkv_s, out_s), _, (down_grad0, *landed) = step(
        [p1],
        outer_attention,
        (*normed0, g, m0, m1, m2, m3, mixed0),
        land=(down_grad0, *flying),
    )
    arrive(gu_0, landed)
    att_0 = (Scatter(qkv, order_a, features), Scatter(out, order_b, features))
    (r,), (qkv_r, out_r, *arrays), _, _ = step(
        [add_low(r, p2)],
        lambda *v: (*core_then_send(*att_0)(*v[:4]), *sends(*gu_0)(*v[4:])),
        (qkv_s, out_s, qkv, out, *held(*gu_0)),
    )
    arrive(att_0, (qkv_r, out_r))
    att_arrays = run_down(att_0, arrays[:2], 1 + second_axis)
    gu_arrays = run_down(gu_0, arrays[2:], 1)
    done_1 = (*att_1[0].terms, *att_1[1].terms, gu_grad1, down_grad0, down_grad1)
    (r,), landed, _, done_1 = step(
        [add_low(r, p3)],
        lambda a, b: (exchange(a, att_0[0].bit), exchange(b, att_0[1].bit)),
        att_arrays,
        land=done_1,
    )
    arrive(att_0, landed)
    count = len(att_1[0].terms)
    att_1[0].terms, att_1[1].terms = list(done_1[:count]), list(done_1[count : 2 * count])
    gu_grad1, down_grad0, down_grad1 = done_1[2 * count :]

    def last_step(r, p0, grad_resid, a, b, *att):
        landed = exchange(a, gu_0[0].bit), exchange(b, gu_0[1].bit)
        arrays = sends(*att_0)(*att)
        if att_0[0].last:
            arrays = tuple(exchange(v, t.bit) for v, t in zip(arrays, att_0))
        grad_before, gain_part = jax.vjp(norm_rows, residual0, gain_a[0])[1](r.astype(f32) + p0)
        return (grad_resid + grad_before, gain_part, *landed, *arrays)

    (lowr,), (grad_resid, attention_gain_part0, *landed), _, _ = step(
        [add_low(lowr, low3)],
        last_step,
        (r, p0, grad_resid, *gu_arrays, *held(*att_0)),
    )
    arrive(gu_0, landed[:2])
    if att_0[0].last:
        arrive(att_0, landed[2:])
    else:
        arrays = run_down(att_0, landed[2:], 1)
        arrive(att_0, [exchange(a, t.bit) for a, t in zip(arrays, att_0)])
    gain_sums = jnp.stack(
        [attention_gain_part0, attention_gain_part1, feed_gain_part0, feed_gain_part1]
    )
    gate_grad0, up_grad0 = (t.finish() for t in gu_0)
    qkv_grads = [t[0].finish() for t in (att_0, att_1)]
    out_grads = [t[1].finish() for t in (att_0, att_1)]
    block_out = (hidden1 + (lowr.astype(f32) + low0)).astype(bf16)

    gain_sums = sum_all(sum_to_owner(gain_sums), "tp")
    return (
        block_out,
        grad_resid,
        gain_sums[:layer_count],
        jnp.stack([p[:, :q_width] for p in qkv_grads]),
        jnp.stack([p[:, q_width : q_width + k_width] for p in qkv_grads]),
        jnp.stack([p[:, q_width + k_width :] for p in qkv_grads]),
        jnp.stack([p.T for p in out_grads]),
        gain_sums[layer_count:],
        jnp.stack([gate_grad0, gu_grad1[:, :ff].astype(f32)]),
        jnp.stack([up_grad0, gu_grad1[:, ff:].astype(f32)]),
        jnp.stack([g.astype(f32).T for g in (down_grad0, down_grad1)]),
    )


def solution(mesh):
    rows = P(("fsdp", "tp"), None)
    gain = P(None, "fsdp")
    column = P(None, "fsdp", "tp")
    row = P(None, "tp", "fsdp")
    weights = (gain, column, column, column, row, gain, column, column, row)
    return jax.shard_map(
        local,
        mesh=mesh,
        in_specs=(rows, rows) + weights,
        out_specs=(rows, rows) + weights,
        check_vma=False,
    )
```

```python
import jax
import jax.numpy as jnp
from jax import lax
from jax.experimental import pallas as pl
from jax.experimental.pallas import tpu as pltpu
from jax.sharding import PartitionSpec as P

HD = 64
SEQ_LEN = 512
epsilon = 1e-05
theta = 10000.0
masked_score = -1e30
f32 = jnp.float32
bf16 = jnp.bfloat16


def norm_rows(residual, scales):
    inverse = lax.rsqrt(jnp.mean(residual * residual, axis=-1, keepdims=True) + epsilon)
    return residual * inverse * scales


def swiglu(gate_lin, up_lin):
    return jax.nn.silu(gate_lin) * up_lin


def angle_tables(positions):
    half_width = HD // 2
    exponent = 2.0 * jnp.arange(half_width).astype(f32) / HD
    frequency = theta ** (-exponent)
    angles = positions.astype(f32)[:, None] * frequency[None, :]
    return jnp.cos(angles), jnp.sin(angles)


def shift(values):
    size = lax.axis_size("tp")
    return lax.ppermute(values, "tp", [(i, (i + 1) % size) for i in range(size)])


def dot(a, b):
    return jnp.dot(a, b, preferred_element_type=f32)


def dot_t(a, b):
    return lax.dot_general(a, b, (((1,), (1,)), ((), ())), preferred_element_type=f32)


def t_dot(a, b):
    return lax.dot_general(a, b, (((0,), (0,)), ((), ())), preferred_element_type=f32)


def thin_cost():
    return pl.CostEstimate(flops=1, bytes_accessed=1, transcendentals=0)


def pinned(args, free=0):
    return [
        a if index < free else pltpu.with_memory_space_constraint(a, pltpu.HBM)
        for index, a in enumerate(args)
    ]


def run_kernel(body, grid, in_specs, out_specs, out_shape, args, scratch=(), room=36, free=0):
    return pl.pallas_call(
        body,
        grid=(grid,),
        in_specs=in_specs,
        out_specs=out_specs,
        out_shape=out_shape,
        scratch_shapes=scratch,
        cost_estimate=thin_cost(),
        compiler_params=pltpu.CompilerParams(
            dimension_semantics=("arbitrary",), vmem_limit_bytes=room * 1024 * 1024
        ),
    )(*pinned(args, free))


TILE = 1024
OUTER_TILE = 512


def swiglu_back(gate, up, grad):
    sig = 1.0 / (1.0 + jnp.exp(-gate))
    return grad * up * (sig * (1.0 + gate * (1.0 - sig))), grad * (gate * sig), gate * sig * up


def pair_forward(xa, xb, weights):
    rows, features = xa.shape
    ff = weights.shape[1] // 3
    n = features // TILE

    def body(xa, xb, wgu, wd, gu, act, pa, pb):
        i = pl.program_id(0)

        @pl.when(i == 0)
        def _():
            gu[...] = jnp.zeros(gu.shape, f32)

        @pl.when(i < n)
        def _():
            gu[...] += dot(jnp.concatenate([xa[...], xb[...]], axis=0), wgu[...])

        @pl.when(i == n - 1)
        def _():
            gate = gu[:, :ff]
            act[...] = (gate / (1.0 + jnp.exp(-gate)) * gu[:, ff:]).astype(bf16)

        @pl.when(i >= n)
        def _():
            part = dot_t(act[...], wd[...])
            pa[...] = part[:rows].astype(bf16)
            pb[...] = part[rows:].astype(bf16)

    early = lambda i: jnp.minimum(i, n - 1)
    late = lambda i: jnp.maximum(i - n, 0)
    return run_kernel(
        body,
        2 * n,
        [
            pl.BlockSpec((rows, TILE), lambda i: (0, early(i))),
            pl.BlockSpec((rows, TILE), lambda i: (0, early(i))),
            pl.BlockSpec((TILE, 2 * ff), lambda i: (early(i), 0)),
            pl.BlockSpec((TILE, ff), lambda i: (late(i), 2)),
        ],
        [
            pl.BlockSpec((2 * rows, 2 * ff), lambda i: (0, 0)),
            pl.BlockSpec((2 * rows, ff), lambda i: (0, 0)),
            pl.BlockSpec((rows, TILE), lambda i: (0, late(i))),
            pl.BlockSpec((rows, TILE), lambda i: (0, late(i))),
        ],
        [
            pltpu.HBM((2 * rows, 2 * ff), f32),
            pltpu.HBM((2 * rows, ff), bf16),
            jax.ShapeDtypeStruct((rows, features), bf16),
            jax.ShapeDtypeStruct((rows, features), bf16),
        ],
        (xa, xb, weights, weights),
        free=2,
    )


def pair_up_back(xa, xb, grad_act, which, weights):
    rows, features = xa.shape
    ff = weights.shape[1] // 3
    n = features // TILE

    def body(xa, xb, ga, w, act, grads, pa, pb, gu):
        i = pl.program_id(0)

        @pl.when(i == 0)
        def _():
            gu[...] = jnp.zeros(gu.shape, f32)

        @pl.when(i < n)
        def _():
            gu[...] += dot(jnp.concatenate([xa[...], xb[...]], axis=0), w[...])

        @pl.when(i == n - 1)
        def _():
            dgate, dup, a = swiglu_back(gu[:, :ff], gu[:, ff:], ga[...])
            grads[:, :ff] = dgate.astype(bf16)
            grads[:, ff:] = dup.astype(bf16)
            act[...] = a.astype(bf16)

        @pl.when(i >= n)
        def _():
            part = dot_t(grads[...], w[...])
            pa[...] = part[:rows].astype(bf16)
            pb[...] = part[rows:].astype(bf16)

    early = lambda i: jnp.minimum(i, n - 1)
    late = lambda i: jnp.maximum(i - n, 0)
    return run_kernel(
        body,
        2 * n,
        [
            pl.BlockSpec((rows, TILE), lambda i: (0, early(i))),
            pl.BlockSpec((rows, TILE), lambda i: (0, early(i))),
            pl.BlockSpec((2 * rows, ff), lambda i: (which, 0)),
            pl.BlockSpec((TILE, 2 * ff), lambda i: (i % n, 0)),
        ],
        [
            pl.BlockSpec((2 * rows, ff), lambda i: (0, 0)),
            pl.BlockSpec((2 * rows, 2 * ff), lambda i: (0, 0)),
            pl.BlockSpec((rows, TILE), lambda i: (0, late(i))),
            pl.BlockSpec((rows, TILE), lambda i: (0, late(i))),
        ],
        [
            pltpu.HBM((2 * rows, ff), bf16),
            pltpu.HBM((2 * rows, 2 * ff), bf16),
            jax.ShapeDtypeStruct((rows, features), bf16),
            jax.ShapeDtypeStruct((rows, features), bf16),
        ],
        (xa, xb, grad_act, weights),
        (pltpu.VMEM((2 * rows, 2 * ff), f32),),
        free=2,
    )


def pair_back(ga, gb, gu, weights):
    rows, features = ga.shape
    ff = weights.shape[1] // 3
    n = features // TILE

    def body(ga, gb, gu, wd, wgu, grads, pa, pb, acc):
        i = pl.program_id(0)

        @pl.when(i == 0)
        def _():
            acc[...] = jnp.zeros(acc.shape, f32)

        @pl.when(i < n)
        def _():
            acc[...] += dot(jnp.concatenate([ga[...], gb[...]], axis=0), wd[...])

        @pl.when(i == n - 1)
        def _():
            dgate, dup, _ = swiglu_back(gu[:, :ff], gu[:, ff:], acc[...])
            grads[:, :ff] = dgate.astype(bf16)
            grads[:, ff:] = dup.astype(bf16)

        @pl.when(i >= n)
        def _():
            part = dot_t(grads[...], wgu[...])
            pa[...] = part[:rows].astype(bf16)
            pb[...] = part[rows:].astype(bf16)

    early = lambda i: jnp.minimum(i, n - 1)
    late = lambda i: jnp.maximum(i - n, 0)
    return run_kernel(
        body,
        2 * n,
        [
            pl.BlockSpec((rows, TILE), lambda i: (0, early(i))),
            pl.BlockSpec((rows, TILE), lambda i: (0, early(i))),
            pl.BlockSpec((2 * rows, 2 * ff), lambda i: (0, 0)),
            pl.BlockSpec((TILE, ff), lambda i: (early(i), 2)),
            pl.BlockSpec((TILE, 2 * ff), lambda i: (late(i), 0)),
        ],
        [
            pl.BlockSpec((2 * rows, 2 * ff), lambda i: (0, 0)),
            pl.BlockSpec((rows, TILE), lambda i: (0, late(i))),
            pl.BlockSpec((rows, TILE), lambda i: (0, late(i))),
        ],
        [
            pltpu.HBM((2 * rows, 2 * ff), bf16),
            jax.ShapeDtypeStruct((rows, features), bf16),
            jax.ShapeDtypeStruct((rows, features), bf16),
        ],
        (ga, gb, gu, weights, weights),
        (pltpu.VMEM((2 * rows, ff), f32),),
        free=2,
    )


def outer(slots, pairs, parts=1):
    rows, features = slots[0].shape
    width = pairs[0].shape[1] // parts

    def body(s0, s1, s2, s3, b0, b1, *outs):
        first = jnp.concatenate([s0[...], s1[...]], axis=0)
        second = jnp.concatenate([s2[...], s3[...]], axis=0)
        for index, out in enumerate(outs):
            at = slice(index * width, (index + 1) * width)
            out[...] = (t_dot(first, b0[:, at]) + t_dot(second, b1[:, at])).astype(bf16)

    return run_kernel(
        body,
        features // OUTER_TILE,
        [pl.BlockSpec((rows, OUTER_TILE), lambda i: (0, i)) for _ in slots]
        + [pl.BlockSpec((2 * rows, parts * width), lambda i: (0, 0)) for _ in pairs],
        [pl.BlockSpec((OUTER_TILE, width), lambda i: (i, 0)) for _ in range(parts)],
        [pltpu.HBM((features, width), bf16) for _ in range(parts)],
        (*slots, *pairs),
        room=24,
    )


def whole_kernel(body, out_shape, args, scratch=(), free=0):
    return pl.pallas_call(
        body,
        out_shape=out_shape,
        scratch_shapes=scratch,
        cost_estimate=thin_cost(),
        compiler_params=pltpu.CompilerParams(vmem_limit_bytes=40 * 1024 * 1024),
    )(*pinned(args, free))


def turn_heads(values, cosine, sine):
    half_width = HD // 2
    parts = []
    for at in range(0, values.shape[0], HD):
        first = values[at : at + half_width]
        second = values[at + half_width : at + HD]
        parts += [first * cosine - second * sine, second * cosine + first * sine]
    return jnp.concatenate(parts, axis=0)


def attention_forward(slots, weights, bias, cosine, sine, widths):
    q_width, k_width = widths
    rows, features = slots[0].shape
    total = rows * len(slots)
    heads = q_width // HD
    repeat = heads // (k_width // HD)
    qkv_width = q_width + 2 * k_width
    scale = HD ** (-0.5)

    def body(*refs):
        xs, (w, bias, cosine, sine) = refs[: len(slots)], refs[len(slots) : len(slots) + 4]
        qt, kvt, lse, mixed, *parts = refs[len(slots) + 4 : -2]
        mt, keys = refs[-2:]
        x = jnp.concatenate([r[...] for r in xs], axis=0)
        qkv = dot(x, w[:, :qkv_width]).T
        cos, sin = cosine[...], sine[...]
        qt[...] = turn_heads(qkv[:q_width], cos, sin).astype(bf16)
        kt = turn_heads(qkv[q_width : q_width + k_width], cos, sin).astype(bf16)
        kvt[:k_width] = kt
        kvt[k_width:] = qkv[q_width + k_width :].astype(bf16)
        keys[...] = kt.astype(f32).T.astype(bf16)

        def head(h, carry):
            at = pl.ds(h * HD, HD)
            group = h // repeat
            vt = kvt[pl.ds(k_width + group * HD, HD)]
            k = keys[...] if k_width == HD else keys[:, pl.ds(group * HD, HD)]
            q = qt[at] * jnp.asarray(scale, bf16)
            s = dot(k, q) + bias[...]
            largest = jnp.max(s, axis=0, keepdims=True)
            e = jnp.exp(s - largest)
            t = jnp.sum(e, axis=0, keepdims=True)
            p = (e * (1.0 / t)).astype(bf16)
            mt[at] = dot(vt, p)
            lse[pl.ds(h, 1)] = largest + jnp.log(t)
            return carry

        lax.fori_loop(0, heads, head, 0, unroll=4 if heads % 4 == 0 else 1)
        m = mt[...].T.astype(bf16)
        mixed[...] = m
        out = dot_t(m, w[:, qkv_width:])
        for index, part in enumerate(parts):
            part[...] = out[index * rows : (index + 1) * rows].astype(bf16)

    return whole_kernel(
        body,
        [
            pltpu.HBM((q_width, total), bf16),
            pltpu.HBM((2 * k_width, total), bf16),
            pltpu.HBM((heads, total), f32),
            pltpu.HBM((total, q_width), bf16),
        ]
        + [jax.ShapeDtypeStruct((rows, features), bf16) for _ in slots],
        (*slots, weights, bias, cosine, sine),
        (pltpu.VMEM((q_width, total), f32), pltpu.VMEM((total, k_width), bf16)),
        free=4,
    )


def attention_backward(slots, weights, bias, cosine, sine, qt, kvt, lse, widths):
    q_width, k_width = widths
    rows, features = slots[0].shape
    total = rows * len(slots)
    heads = q_width // HD
    repeat = heads // (k_width // HD)
    qkv_width = q_width + 2 * k_width
    scale = HD ** (-0.5)

    def body(*refs):
        ms, (w, bias, cosine, sine, qt, kvt, lse) = refs[: len(slots)], refs[len(slots) : len(slots) + 7]
        grad, *parts = refs[len(slots) + 7 : -4]
        gt, gq, kv, gkv = refs[-4:]
        m = jnp.concatenate([r[...] for r in ms], axis=0)
        gt[...] = dot(m, w[:, qkv_width:]).T.astype(bf16)
        kv[...] = kvt[...].astype(f32).T.astype(bf16)
        gkv[...] = jnp.zeros(gkv.shape, f32)

        def head(h, carry):
            at = pl.ds(h * HD, HD)
            group = h // repeat
            k_at = 0 if k_width == HD else group * HD
            kt = kvt[pl.ds(k_at, HD)]
            k = kv[:, pl.ds(k_at, HD)]
            v = kv[:, pl.ds(k_width + k_at, HD)]
            q = qt[at]
            g = gt[at]
            s = dot(k, q * jnp.asarray(scale, bf16)) + bias[...]
            p = jnp.exp(s - lse[pl.ds(h, 1)])
            gp = dot(v, g)
            inner = jnp.sum(p * gp, axis=0, keepdims=True)
            gs = (p * (gp - inner) * scale).astype(bf16)
            gq[at] = dot(kt, gs)
            gk = dot_t(gs, q)
            gv = dot_t(p.astype(bf16), g)
            gkv[pl.ds(group, 1)] += jnp.concatenate([gk, gv], axis=1)[None]
            return carry

        lax.fori_loop(0, heads, head, 0, unroll=4 if heads % 4 == 0 else 1)
        cos, sin = cosine[...], -sine[...]
        both = [gkv[index].T for index in range(k_width // HD)]
        gk = jnp.concatenate([b[:HD] for b in both], axis=0)
        gv = jnp.concatenate([b[HD:] for b in both], axis=0)
        found = jnp.concatenate(
            [turn_heads(gq[...], cos, sin), turn_heads(gk, cos, sin), gv], axis=0
        ).T.astype(bf16)
        grad[...] = found
        out = dot_t(found, w[:, :qkv_width])
        for index, part in enumerate(parts):
            part[...] = out[index * rows : (index + 1) * rows].astype(bf16)

    return whole_kernel(
        body,
        [pltpu.HBM((total, qkv_width), bf16)]
        + [jax.ShapeDtypeStruct((rows, features), bf16) for _ in slots],
        (*slots, weights, bias, cosine, sine, qt, kvt, lse),
        (
            pltpu.VMEM((q_width, total), bf16),
            pltpu.VMEM((q_width, total), f32),
            pltpu.VMEM((total, 2 * k_width), bf16),
            pltpu.VMEM((k_width // HD, total, 2 * HD), f32),
        ),
        free=4,
    )


def shard_of(layer, columns, row):
    depth, rows, _ = columns[0].shape
    widths = [c.shape[2] for c in columns] + [row.shape[1]]

    def body(*refs):
        out = refs[-1]
        at, pending = 0, []
        for ref, width in zip(refs[:-2], widths):
            pending.append(ref[...])
            if sum(p.shape[1] for p in pending) % 128 == 0:
                part = pending[0] if len(pending) == 1 else jnp.concatenate(pending, axis=1)
                out[:, at : at + part.shape[1]] = part
                at, pending = at + part.shape[1], []
        assert not pending
        out[:, at:] = refs[-2][...].astype(f32).T.astype(bf16)

    return pl.pallas_call(
        body,
        grid=(1,),
        in_specs=[
            pl.BlockSpec((None, *v.shape[1:]), lambda i: (layer, 0, 0)) for v in (*columns, row)
        ],
        out_specs=pl.BlockSpec((rows, sum(widths)), lambda i: (0, 0)),
        out_shape=pltpu.HBM((rows, sum(widths)), bf16),
        cost_estimate=thin_cost(),
        compiler_params=pltpu.CompilerParams(vmem_limit_bytes=32 * 1024 * 1024),
    )(*pinned((*columns, row)))


def split_outer(groups, order_pair):
    size = lax.axis_size("fsdp")
    rows, features = groups[0][0][0].shape
    block = features // size
    if block % 128:
        whole = []
        for slots, wide, parts in groups:
            whole += outer(slots, halves(wide, rows), parts)
        return whole, [Scatter(v, o).send() for v, o in zip(whole, order_pair)]
    operands, specs, plan = [], [], []
    for slots, wide, parts in groups:
        plan.append((len(operands), len(wide), wide[0].shape[1] // parts, parts))
        for other in (1, 0):
            operands += slots
            specs += [
                pl.BlockSpec((rows, block), lambda i, c, o=other: (0, 2 * i + (c[0] + o) % 2))
                for _ in slots
            ]
        operands += wide
        specs += [pl.BlockSpec(v.shape, lambda i, c: (0, 0)) for v in wide]
    widths = [width for _, _, width, parts in plan for _ in range(parts)]

    def body(c, *refs):
        outs = list(refs[len(operands) :])
        for start, count, width, parts in plan:
            wides = refs[start + 8 : start + 8 + count]
            lefts = [
                jnp.concatenate([r[...] for r in refs[at : at + 4]], axis=0)
                for at in (start, start + 4)
            ]
            each = 4 * rows // count
            for part in range(parts):
                columns = slice(part * width, (part + 1) * width)
                for left in lefts:
                    found = sum(
                        t_dot(left[k * each : (k + 1) * each], w[:, columns])
                        for k, w in enumerate(wides)
                    )
                    outs.pop(0)[...] = found.astype(bf16)

    core = (lax.axis_index("fsdp") % 2).astype(jnp.int32)[None]
    found = pl.pallas_call(
        body,
        grid_spec=pltpu.PrefetchScalarGridSpec(
            num_scalar_prefetch=1,
            grid=(size // 2,),
            in_specs=specs,
            out_specs=[pl.BlockSpec((block, w), lambda i, c: (i, 0)) for w in widths for _ in (0, 1)],
        ),
        out_shape=[pltpu.HBM((features // 2, w), bf16) for w in widths for _ in (0, 1)],
        cost_estimate=thin_cost(),
        compiler_params=pltpu.CompilerParams(
            dimension_semantics=("arbitrary",), vmem_limit_bytes=32 * 1024 * 1024
        ),
    )(core, *pinned(operands))
    return found[1::2], found[0::2]


def halves(wide, rows):
    return wide if len(wide) == 2 else [wide[0][: 2 * rows], wide[0][2 * rows :]]


def slots_by_down(slots, weights):
    rows, features = slots[0].shape
    ff = weights.shape[1] // 3
    total = rows * len(slots)

    def body(*refs):
        i = pl.program_id(0)
        out = refs[-1]
        part = dot(jnp.concatenate([r[...] for r in refs[:-2]], axis=0), refs[-2][...])

        @pl.when(i == 0)
        def _():
            out[...] = part

        @pl.when(i > 0)
        def _():
            out[...] += part

    return run_kernel(
        body,
        features // OUTER_TILE,
        [pl.BlockSpec((rows, OUTER_TILE), lambda i: (0, i)) for _ in slots]
        + [pl.BlockSpec((OUTER_TILE, ff), lambda i: (i, 2))],
        pl.BlockSpec((total, ff), lambda i: (0, 0)),
        jax.ShapeDtypeStruct((total, ff), f32),
        (*slots, weights),
        room=24,
    )


def down_of(pairs, weights):
    both, ff = pairs[0].shape
    rows = both // 2
    features = weights.shape[0]

    def body(*refs):
        acts, w, outs = refs[:2], refs[2], refs[3:]
        part = dot_t(jnp.concatenate([r[...] for r in acts], axis=0), w[...])
        for index, out in enumerate(outs):
            out[...] = part[index * rows : (index + 1) * rows].astype(bf16)

    return run_kernel(
        body,
        features // OUTER_TILE,
        [pl.BlockSpec((both, ff), lambda i: (0, 0)) for _ in pairs]
        + [pl.BlockSpec((OUTER_TILE, ff), lambda i: (i, 2))],
        [pl.BlockSpec((rows, OUTER_TILE), lambda i: (0, i)) for _ in range(4)],
        [jax.ShapeDtypeStruct((rows, features), bf16) for _ in range(4)],
        (*pairs, weights),
        room=24,
    )


def gather_weight(values):
    return lax.all_gather(values, "fsdp", axis=0, tiled=True)


def scatter_weight(values):
    return lax.psum_scatter(values.astype(bf16), "fsdp", scatter_dimension=0, tiled=True)


def step(moving, work=None, inputs=(), launch=(), land=()):
    moving, inputs, sent = lax.optimization_barrier(
        (tuple(moving), tuple(inputs), tuple(a for a, _ in launch))
    )
    moved = tuple(shift(m) for m in moving)
    flying = tuple(exchange(a, bit) for a, (_, bit) in zip(sent, launch))
    results = () if work is None else work(*inputs)
    moved, results, landed = lax.optimization_barrier((moved, results, tuple(land)))
    return moved, results, flying, landed


def exchange(values, bit, axis="fsdp"):
    size = lax.axis_size(axis)
    return lax.ppermute(values, axis, [(i, i ^ (1 << bit)) for i in range(size)])


def fsdp_bits():
    count = lax.axis_size("fsdp").bit_length() - 1
    width = (count - 1) // 2
    return [0], list(range(1, 1 + width)), list(range(1 + width, count))


def my_bit(bit):
    return (lax.axis_index("fsdp") // (1 << bit)) % 2


def sends(*tracks):
    def work(*values):
        values, found = list(values), []
        for track in tracks:
            held, track.terms = track.terms, [values.pop(0) for _ in track.terms]
            found.append(track.send())
            track.terms = held
        return tuple(found)

    return work


def held(*tracks):
    return tuple(t for track in tracks for t in track.terms)


def flights(tracks, arrays):
    return tuple((a, t.bit) for t, a in zip(tracks, arrays))


def arrive(tracks, arrays):
    for track, values in zip(tracks, arrays):
        track.arrived(values)


def run_down(tracks, arrays, left):
    arrays = list(arrays)
    for index, track in enumerate(tracks):
        while len(track.order) - track.stage > left:
            track.arrived(exchange(arrays[index], track.bit))
            arrays[index] = track.send()
    return arrays


class Scatter:
    def __init__(self, partial, order, features=None):
        self.size = lax.axis_size("fsdp")
        self.me = lax.axis_index("fsdp")
        self.order = list(order)
        self.stage = 0
        self.terms = [partial]
        bits = sorted(order, reverse=True)
        if features is not None and partial.shape[0] < features:
            bits = bits[:-1]
        self.rows = partial.shape[0] >> len(bits)
        self.free = [bits]

    @property
    def bit(self):
        return self.order[self.stage]

    @property
    def last(self):
        return self.stage == len(self.order) - 1

    def sum_blocks(self, blocks, dtype):
        ids = jnp.stack(
            [
                sum(
                    (((blocks >> b) & 1) << (len(free) - 1 - k) for k, b in enumerate(free)),
                    jnp.zeros_like(blocks),
                )
                for free in self.free
            ]
        ).astype(jnp.int32)
        width = self.terms[0].shape[1]
        rows, count = self.rows, blocks.shape[0]

        def body(ids, *refs):
            refs[-1][...] = sum(r[...].astype(f32) for r in refs[:-1]).astype(dtype)

        return pl.pallas_call(
            body,
            grid_spec=pltpu.PrefetchScalarGridSpec(
                num_scalar_prefetch=1,
                grid=(count,),
                in_specs=[
                    pl.BlockSpec((rows, width), lambda i, ids, term=term: (ids[term, i], 0))
                    for term in range(len(self.terms))
                ],
                out_specs=pl.BlockSpec((rows, width), lambda i, ids: (i, 0)),
            ),
            out_shape=jax.ShapeDtypeStruct((count * rows, width), dtype),
            cost_estimate=thin_cost(),
            compiler_params=pltpu.CompilerParams(
                dimension_semantics=("arbitrary",), vmem_limit_bytes=16 * 1024 * 1024
            ),
        )(ids, *pinned(self.terms))

    def send(self):
        free = self.free[self.stage]
        left = [b for b in free if b != self.bit]
        each = jnp.arange(1 << len(left))
        blocks = (self.me ^ (1 << self.bit)) + jnp.zeros_like(each)
        for k, b in enumerate(left):
            blocks = (blocks & ~(1 << b)) | (((each >> (len(left) - 1 - k)) & 1) << b)
        return self.sum_blocks(blocks, bf16)

    def arrived(self, values):
        self.terms.append(values)
        self.free.append([b for b in self.free[-1] if b != self.bit])
        self.stage += 1

    def finish(self):
        total = 0.0
        for values, free in zip(self.terms, self.free):
            at = sum((((self.me >> b) & 1) << (len(free) - 1 - k) for k, b in enumerate(free)), 0)
            blocks = values.reshape(-1, self.rows, values.shape[1])
            total += lax.dynamic_index_in_dim(blocks, at, 0, keepdims=False).astype(f32)
        return total


def sum_all(values, axis):
    for bit in range(lax.axis_size(axis).bit_length() - 1):
        values = values + exchange(values, bit, axis)
    return values


def keep_half(values, bit):
    low, high = jnp.split(values, 2, axis=-1)
    upper = my_bit(bit) == 1
    return jnp.where(upper, high, low) + exchange(jnp.where(upper, low, high), bit)


def local(
    tokens,
    cotangent,
    attention_gain,
    query_weight,
    key_weight,
    value_weight,
    output_weight,
    feed_gain,
    gate_weight,
    up_weight,
    down_weight,
):
    layer_count = query_weight.shape[0]
    local_rows = tokens.shape[0]
    size = lax.axis_size("tp")
    me = lax.axis_index("tp")
    group_rows = local_rows * size
    q_width = query_weight.shape[2]
    k_width = key_weight.shape[2]
    qkv_width = q_width + 2 * k_width
    ff = gate_weight.shape[2]
    assert size == 4 and layer_count == 2

    row_index = (
        ((me - jnp.arange(size)) % size)[:, None] * local_rows + jnp.arange(local_rows)[None, :]
    ).reshape(group_rows)
    cosine, sine = (table.T for table in angle_tables(row_index % SEQ_LEN))
    seen = (row_index[:, None] <= row_index[None, :]) & (
        (row_index // SEQ_LEN)[:, None] == (row_index // SEQ_LEN)[None, :]
    )
    bias = jnp.where(seen, 0.0, masked_score).astype(f32)
    core, xs, ys = fsdp_bits()
    me_f = lax.axis_index("fsdp")
    shards = lax.axis_size("fsdp")
    shard_rows = query_weight.shape[1]
    features = shards * shard_rows

    def attention_shard(l):
        return shard_of(l, [query_weight, key_weight, value_weight], output_weight)

    def feed_shard(l):
        return shard_of(l, [gate_weight, up_weight], down_weight)

    def cat(parts):
        return jnp.concatenate(parts, axis=0)

    def norm_low(values, gain):
        return norm_rows(values, gain).astype(bf16)

    def attention(x0, x1, x2, x3, w, bias, cosine, sine):
        return tuple(
            attention_forward([x0, x1, x2, x3], w, bias, cosine, sine, (q_width, k_width))
        )

    def attention_back(m0, m1, m2, m3, w, bias, cosine, sine, qt, kvt, lse):
        return tuple(
            attention_backward(
                [m0, m1, m2, m3], w, bias, cosine, sine, qt, kvt, lse, (q_width, k_width)
            )
        )

    def add_low(moved, part):
        return (moved.astype(f32) + part).astype(bf16)

    weights_a0 = gather_weight(attention_shard(0))
    gains = jnp.zeros((shards, 2 * layer_count, shard_rows), bf16)
    gains = lax.dynamic_update_slice(
        gains, jnp.concatenate([attention_gain, feed_gain], axis=0)[None], (me_f, 0, 0)
    )
    bits = core + xs + ys

    (t1,), (gains, shard_f0), _, _ = step(
        [tokens], lambda g: (g + exchange(g, bits[0]), feed_shard(0)), (gains,)
    )
    weights_f = [gather_weight(shard_f0), None]

    def gather_gains(gains):
        for bit in bits[1:]:
            gains = gains + exchange(gains, bit)
        return (gains,)

    (t2,), (gains,), _, _ = step([t1], gather_gains, (gains,))
    gains = jnp.moveaxis(gains.astype(f32), 0, 1).reshape(2 * layer_count, features)
    gain_a, gain_f = gains[:layer_count], gains[layer_count:]

    def norm_slots(gain, *slots):
        return tuple(norm_low(v.astype(f32), gain) for v in slots)

    (t3,), (x0, x1, x2), _, _ = step([t2], norm_slots, (gain_a[0], tokens, t1, t2))
    tables = (bias, cosine, sine)
    normed0 = [x0, x1, x2, *norm_slots(gain_a[0], t3)]
    (c1,), (*saved0, mixed0, p0, p1, p2, p3), _, _ = step(
        [cotangent], attention, (*normed0, weights_a0, *tables)
    )
    residual0 = tokens.astype(f32)

    (r,), (shard_a1,), _, _ = step([p1], lambda: (attention_shard(1),))
    (r,), (shard_f1,), _, _ = step([add_low(r, p2)], lambda: (feed_shard(1),))
    weights_a1 = gather_weight(shard_a1)
    weights_f[1] = gather_weight(shard_f1)
    (r,), _, _, _ = step([add_low(r, p3)])
    hidden0 = residual0 + (r.astype(f32) + p0)

    w = weights_f[0]
    x0 = norm_low(hidden0, gain_f[0])
    (x1,), _, _, _ = step([x0])
    (x2,), _, _, _ = step([x1])
    (x3,), _, _, _ = step([x2])
    (c2,), (gu01, act01, p0, p1), _, _ = step([c1], pair_forward, (x0, x1, w))
    (r,), (gu23, act23, p2, p3), _, _ = step([p1], pair_forward, (x2, x3, w))
    (r,), _, _, _ = step([add_low(r, p2)])
    (r,), _, _, _ = step([add_low(r, p3)])
    residual1 = hidden0 + (r.astype(f32) + p0)
    feed0, gu0, act0 = [x0, x1, x2, x3], [gu01, gu23], [act01, act23]

    n0 = norm_low(residual1, gain_a[1])
    (n1,), _, _, _ = step([n0])
    (n2,), _, _, _ = step([n1])
    (n3,), _, _, _ = step([n2])
    normed1 = [n0, n1, n2, n3]
    (c3,), (*saved1, mixed1, p0, p1, p2, p3), _, _ = step(
        [c2], attention, (*normed1, weights_a1, *tables)
    )
    cots = [cotangent, c1, c2, c3]
    (r,), _, _, _ = step([p1])
    (r,), _, _, _ = step([add_low(r, p2)])
    (r,), _, _, _ = step([add_low(r, p3)])
    hidden1 = residual1 + (r.astype(f32) + p0)

    w = weights_f[1]

    x0 = norm_low(hidden1, gain_f[1])
    (x1,), (grad_act,), _, _ = step(
        [x0], lambda v, *c: (slots_by_down(c, v),), (w, *cots)
    )
    (x2,), (a01, q01, p0, p1), _, _ = step(
        [x1], lambda x, y, g, v: pair_up_back(x, y, g, 0, v), (x0, x1, grad_act, w)
    )
    (x3,), _, _, _ = step([x2])
    (r,), (a23, q23, p2, p3), _, _ = step(
        [p1], lambda x, y, g, v: pair_up_back(x, y, g, 1, v), (x2, x3, grad_act, w)
    )
    (r,), (down_part1,), _, _ = step(
        [add_low(r, p2)], lambda *v: outer(v[:4], v[4:]), (*cots, a01, a23)
    )
    down_grad1 = scatter_weight(down_part1)
    (r,), (gu_part1,), _, _ = step(
        [add_low(r, p3)],
        lambda *v: outer(v[:4], v[4:]),
        (x0, x1, x2, x3, q01, q23),
    )
    gu_grad1 = scatter_weight(gu_part1)
    grad_normed = r.astype(f32) + p0
    grad_hidden, feed_gain_part1 = jax.vjp(norm_rows, hidden1, gain_f[1])[1](grad_normed)
    grad_resid = cotangent.astype(f32) + grad_hidden

    m0 = grad_resid.astype(bf16)
    (m1,), (low0, low1, low2, low3), _, _ = step(
        [m0], lambda a, b, v: tuple(down_of([a, b], v)), (a01, a23, w)
    )
    (m2,), _, _, _ = step([m1])
    (m3,), _, _, _ = step([m2])
    (lowr,), (g, p0, p1, p2, p3), _, _ = step(
        [low1],
        attention_back,
        (m0, m1, m2, m3, weights_a1, *tables, *saved1),
    )

    order_a, order_b = core + ys + xs, core + xs + ys

    second_axis = len(ys)
    assert len(xs) == second_axis

    def outer_attention(n0, n1, n2, n3, g, m0, m1, m2, m3, mixed):
        kept, sent = split_outer(
            [([n0, n1, n2, n3], [g], 1), ([m0, m1, m2, m3], [mixed], 1)], (order_a, order_b)
        )
        return (*kept, *sent)

    (r,), (qkv, out, qkv_s, out_s), _, (down_grad1,) = step(
        [p1],
        outer_attention,
        (*normed1, g, m0, m1, m2, m3, mixed1),
        land=(down_grad1,),
    )
    att_1 = (Scatter(qkv, order_a, features), Scatter(out, order_b, features))

    def core_then_send(*tracks):
        def work(*values):
            values = list(values)
            got = [exchange(values.pop(0), 0) for _ in tracks]
            fresh = [Scatter(v, t.order, features) for t, v in zip(tracks, values)]
            arrive(fresh, got)
            return (*got, *(t.send() for t in fresh))

        return work

    (r,), landed, _, _ = step(
        [add_low(r, p2)], lambda a, b: (exchange(a, 0), exchange(b, 0)), (qkv_s, out_s)
    )
    arrive(att_1, landed)
    (r,), arrays, _, _ = step([add_low(r, p3)], sends(*att_1), held(*att_1))
    arrays = run_down(att_1, arrays, 1 + second_axis)
    grad_normed = r.astype(f32) + p0
    grad_before, attention_gain_part1 = jax.vjp(norm_rows, residual1, gain_a[1])[1](grad_normed)
    grad_resid = grad_resid + grad_before

    w = weights_f[0]

    g0 = grad_resid.astype(bf16)
    (g1,), _, flying, _ = step([g0], launch=flights(att_1, arrays))
    (g2,), (q01, p0, p1), _, landed = step(
        [g1], pair_back, (g0, g1, gu0[0], w), land=flying
    )
    arrive(att_1, landed)
    (g3,), arrays, _, _ = step([g2], sends(*att_1), held(*att_1))
    arrays = run_down(att_1, arrays, 1)
    (r,), (q23, p2, p3), flying, (gu_grad1,) = step(
        [p1],
        pair_back,
        (g2, g3, gu0[1], w),
        launch=flights(att_1, arrays),
        land=(gu_grad1,),
    )

    def gate_up(*v):
        kept, sent = split_outer([(list(v[:4]), list(v[4:]), 2)], (order_a, order_b))
        return (*kept, *sent)

    (r,), (gate, up, gate_s, up_s), _, landed = step(
        [add_low(r, p2)], gate_up, (*feed0, q01, q23), land=flying
    )
    arrive(att_1, landed)
    (r,), (gate_r, up_r, down_part0), _, _ = step(
        [add_low(r, p3)],
        lambda a, b, *v: (exchange(a, 0), exchange(b, 0), *outer(v[:4], v[4:])),
        (gate_s, up_s, g0, g1, g2, g3, *act0),
    )
    down_grad0 = scatter_weight(down_part0)
    gu_0 = (Scatter(gate, order_a, features), Scatter(up, order_b, features))
    arrive(gu_0, (gate_r, up_r))
    grad_normed = r.astype(f32) + p0
    grad_hidden, feed_gain_part0 = jax.vjp(norm_rows, hidden0, gain_f[0])[1](grad_normed)
    grad_resid = grad_resid + grad_hidden

    m0 = grad_resid.astype(bf16)
    (m1,), arrays, _, _ = step([m0], sends(*gu_0), held(*gu_0))
    arrays = run_down(gu_0, arrays, 1 + second_axis)
    (m2,), _, flying, _ = step([m1], launch=flights(gu_0, arrays))
    (m3,), _, _, _ = step([m2])
    (lowr,), (g, p0, p1, p2, p3), _, _ = step(
        [add_low(lowr, low2)],
        attention_back,
        (m0, m1, m2, m3, weights_a0, *tables, *saved0),
    )
    (r,), (qkv, out, qkv_s, out_s), _, (down_grad0, *landed) = step(
        [p1],
        outer_attention,
        (*normed0, g, m0, m1, m2, m3, mixed0),
        land=(down_grad0, *flying),
    )
    arrive(gu_0, landed)
    att_0 = (Scatter(qkv, order_a, features), Scatter(out, order_b, features))
    (r,), (qkv_r, out_r, *arrays), _, _ = step(
        [add_low(r, p2)],
        lambda *v: (*core_then_send(*att_0)(*v[:4]), *sends(*gu_0)(*v[4:])),
        (qkv_s, out_s, qkv, out, *held(*gu_0)),
    )
    arrive(att_0, (qkv_r, out_r))
    att_arrays = run_down(att_0, arrays[:2], 1 + second_axis)
    gu_arrays = run_down(gu_0, arrays[2:], 1)
    done_1 = (*att_1[0].terms, *att_1[1].terms, gu_grad1, down_grad0, down_grad1)
    (r,), _, flying, done_1 = step(
        [add_low(r, p3)],
        launch=flights(gu_0, gu_arrays) + flights(att_0, att_arrays),
        land=done_1,
    )
    count = len(att_1[0].terms)
    att_1[0].terms, att_1[1].terms = list(done_1[:count]), list(done_1[count : 2 * count])
    gu_grad1, down_grad0, down_grad1 = done_1[2 * count :]

    def last_norm(r, p0, grad_resid):
        grad_before, gain_part = jax.vjp(norm_rows, residual0, gain_a[0])[1](r.astype(f32) + p0)
        return grad_resid + grad_before, gain_part

    (lowr,), (grad_resid, attention_gain_part0), _, landed = step(
        [add_low(lowr, low3)], last_norm, (r, p0, grad_resid), land=flying
    )
    arrive(gu_0, landed[:2])
    arrive(att_0, landed[2:])
    gain_sums = jnp.stack(
        [attention_gain_part0, attention_gain_part1, feed_gain_part0, feed_gain_part1]
    )
    count = shards.bit_length() - 1
    _, (gain_sums, *arrays), _, _ = step(
        [],
        lambda v, *h: (keep_half(v, count - 1), *sends(*att_0)(*h)),
        (gain_sums, *held(*att_0)),
    )
    arrays = run_down(att_0, arrays, 1)

    def finished(track, other, terms):
        before, track.terms = track.terms, list(terms)
        total = track.finish()
        track.terms = before
        return jnp.stack([total, other.astype(f32)])

    _, (gain_sums, qkv_r, out_r, gate_grads), _, _ = step(
        [],
        lambda v, a, b, o, *h: (
            keep_half(v, count - 2),
            exchange(a, att_0[0].bit),
            exchange(b, att_0[1].bit),
            finished(gu_0[0], o, h),
        ),
        (gain_sums, *arrays, gu_grad1[:, :ff], *held(gu_0[0])),
    )
    arrive(att_0, (qkv_r, out_r))
    _, (gain_sums, up_grads), _, _ = step(
        [],
        lambda v, o, *h: (keep_half(v, count - 3), finished(gu_0[1], o, h)),
        (gain_sums, gu_grad1[:, ff:], *held(gu_0[1])),
    )
    for bit in reversed(range(count - 3)):
        gain_sums = keep_half(gain_sums, bit)
    gain_sums = sum_all(gain_sums, "tp")
    qkv_grads = [t[0].finish() for t in (att_0, att_1)]
    out_grads = [t[1].finish() for t in (att_0, att_1)]
    block_out = (hidden1 + (lowr.astype(f32) + low0)).astype(bf16)

    return (
        block_out,
        grad_resid,
        gain_sums[:layer_count],
        jnp.stack([p[:, :q_width] for p in qkv_grads]),
        jnp.stack([p[:, q_width : q_width + k_width] for p in qkv_grads]),
        jnp.stack([p[:, q_width + k_width :] for p in qkv_grads]),
        jnp.stack([p.T for p in out_grads]),
        gain_sums[layer_count:],
        gate_grads,
        up_grads,
        jnp.stack([g.astype(f32).T for g in (down_grad0, down_grad1)]),
    )


def solution(mesh):
    rows = P(("fsdp", "tp"), None)
    gain = P(None, "fsdp")
    column = P(None, "fsdp", "tp")
    row = P(None, "tp", "fsdp")
    weights = (gain, column, column, column, row, gain, column, column, row)
    return jax.shard_map(
        local,
        mesh=mesh,
        in_specs=(rows, rows) + weights,
        out_specs=(rows, rows) + weights,
        check_vma=False,
    )
```

```python
import jax
import jax.numpy as jnp
from jax import lax
from jax.experimental import pallas as pl
from jax.experimental.pallas import tpu as pltpu
from jax.sharding import PartitionSpec as P

HD = 64
SEQ_LEN = 512
epsilon = 1e-05
theta = 10000.0
masked_score = -1e30
f32 = jnp.float32
bf16 = jnp.bfloat16


def norm_rows(residual, scales):
    inverse = lax.rsqrt(jnp.mean(residual * residual, axis=-1, keepdims=True) + epsilon)
    return residual * inverse * scales


def swiglu(gate_lin, up_lin):
    return jax.nn.silu(gate_lin) * up_lin


def angle_tables(positions):
    half_width = HD // 2
    exponent = 2.0 * jnp.arange(half_width).astype(f32) / HD
    frequency = theta ** (-exponent)
    angles = positions.astype(f32)[:, None] * frequency[None, :]
    return jnp.cos(angles), jnp.sin(angles)


def shift(values):
    size = lax.axis_size("tp")
    return lax.ppermute(values, "tp", [(i, (i + 1) % size) for i in range(size)])


def dot(a, b):
    return jnp.dot(a, b, preferred_element_type=f32)


def dot_t(a, b):
    return lax.dot_general(a, b, (((1,), (1,)), ((), ())), preferred_element_type=f32)


def t_dot(a, b):
    return lax.dot_general(a, b, (((0,), (0,)), ((), ())), preferred_element_type=f32)


def thin_cost():
    return pl.CostEstimate(flops=1, bytes_accessed=1, transcendentals=0)


def pinned(args, free=0):
    return [
        a if index < free else pltpu.with_memory_space_constraint(a, pltpu.HBM)
        for index, a in enumerate(args)
    ]


def run_kernel(body, grid, in_specs, out_specs, out_shape, args, scratch=(), room=36, free=0):
    return pl.pallas_call(
        body,
        grid=(grid,),
        in_specs=in_specs,
        out_specs=out_specs,
        out_shape=out_shape,
        scratch_shapes=scratch,
        cost_estimate=thin_cost(),
        compiler_params=pltpu.CompilerParams(
            dimension_semantics=("arbitrary",), vmem_limit_bytes=room * 1024 * 1024
        ),
    )(*pinned(args, free))


TILE = 1024
OUTER_TILE = 512


def swiglu_back(gate, up, grad):
    sig = 1.0 / (1.0 + jnp.exp(-gate))
    return grad * up * (sig * (1.0 + gate * (1.0 - sig))), grad * (gate * sig), gate * sig * up


def pair_forward(xa, xb, weights):
    rows, features = xa.shape
    ff = weights.shape[1] // 3
    n = features // TILE

    def body(xa, xb, wgu, wd, gu, act, pa, pb):
        i = pl.program_id(0)

        @pl.when(i == 0)
        def _():
            gu[...] = jnp.zeros(gu.shape, f32)

        @pl.when(i < n)
        def _():
            gu[...] += dot(jnp.concatenate([xa[...], xb[...]], axis=0), wgu[...])

        @pl.when(i == n - 1)
        def _():
            gate = gu[:, :ff]
            act[...] = (gate / (1.0 + jnp.exp(-gate)) * gu[:, ff:]).astype(bf16)

        @pl.when(i >= n)
        def _():
            part = dot_t(act[...], wd[...])
            pa[...] = part[:rows].astype(bf16)
            pb[...] = part[rows:].astype(bf16)

    early = lambda i: jnp.minimum(i, n - 1)
    late = lambda i: jnp.maximum(i - n, 0)
    return run_kernel(
        body,
        2 * n,
        [
            pl.BlockSpec((rows, TILE), lambda i: (0, early(i))),
            pl.BlockSpec((rows, TILE), lambda i: (0, early(i))),
            pl.BlockSpec((TILE, 2 * ff), lambda i: (early(i), 0)),
            pl.BlockSpec((TILE, ff), lambda i: (late(i), 2)),
        ],
        [
            pl.BlockSpec((2 * rows, 2 * ff), lambda i: (0, 0)),
            pl.BlockSpec((2 * rows, ff), lambda i: (0, 0)),
            pl.BlockSpec((rows, TILE), lambda i: (0, late(i))),
            pl.BlockSpec((rows, TILE), lambda i: (0, late(i))),
        ],
        [
            pltpu.HBM((2 * rows, 2 * ff), f32),
            pltpu.HBM((2 * rows, ff), bf16),
            jax.ShapeDtypeStruct((rows, features), bf16),
            jax.ShapeDtypeStruct((rows, features), bf16),
        ],
        (xa, xb, weights, weights),
        free=2,
    )


def pair_up_back(xa, xb, grad_act, which, weights):
    rows, features = xa.shape
    ff = weights.shape[1] // 3
    n = features // TILE

    def body(xa, xb, ga, w, act, grads, pa, pb, gu):
        i = pl.program_id(0)

        @pl.when(i == 0)
        def _():
            gu[...] = jnp.zeros(gu.shape, f32)

        @pl.when(i < n)
        def _():
            gu[...] += dot(jnp.concatenate([xa[...], xb[...]], axis=0), w[...])

        @pl.when(i == n - 1)
        def _():
            dgate, dup, a = swiglu_back(gu[:, :ff], gu[:, ff:], ga[...])
            grads[:, :ff] = dgate.astype(bf16)
            grads[:, ff:] = dup.astype(bf16)
            act[...] = a.astype(bf16)

        @pl.when(i >= n)
        def _():
            part = dot_t(grads[...], w[...])
            pa[...] = part[:rows].astype(bf16)
            pb[...] = part[rows:].astype(bf16)

    early = lambda i: jnp.minimum(i, n - 1)
    late = lambda i: jnp.maximum(i - n, 0)
    return run_kernel(
        body,
        2 * n,
        [
            pl.BlockSpec((rows, TILE), lambda i: (0, early(i))),
            pl.BlockSpec((rows, TILE), lambda i: (0, early(i))),
            pl.BlockSpec((2 * rows, ff), lambda i: (which, 0)),
            pl.BlockSpec((TILE, 2 * ff), lambda i: (i % n, 0)),
        ],
        [
            pl.BlockSpec((2 * rows, ff), lambda i: (0, 0)),
            pl.BlockSpec((2 * rows, 2 * ff), lambda i: (0, 0)),
            pl.BlockSpec((rows, TILE), lambda i: (0, late(i))),
            pl.BlockSpec((rows, TILE), lambda i: (0, late(i))),
        ],
        [
            pltpu.HBM((2 * rows, ff), bf16),
            pltpu.HBM((2 * rows, 2 * ff), bf16),
            jax.ShapeDtypeStruct((rows, features), bf16),
            jax.ShapeDtypeStruct((rows, features), bf16),
        ],
        (xa, xb, grad_act, weights),
        (pltpu.VMEM((2 * rows, 2 * ff), f32),),
        free=2,
    )


def pair_back(ga, gb, gu, weights):
    rows, features = ga.shape
    ff = weights.shape[1] // 3
    n = features // TILE

    def body(ga, gb, gu, wd, wgu, grads, pa, pb, acc):
        i = pl.program_id(0)

        @pl.when(i == 0)
        def _():
            acc[...] = jnp.zeros(acc.shape, f32)

        @pl.when(i < n)
        def _():
            acc[...] += dot(jnp.concatenate([ga[...], gb[...]], axis=0), wd[...])

        @pl.when(i == n - 1)
        def _():
            dgate, dup, _ = swiglu_back(gu[:, :ff], gu[:, ff:], acc[...])
            grads[:, :ff] = dgate.astype(bf16)
            grads[:, ff:] = dup.astype(bf16)

        @pl.when(i >= n)
        def _():
            part = dot_t(grads[...], wgu[...])
            pa[...] = part[:rows].astype(bf16)
            pb[...] = part[rows:].astype(bf16)

    early = lambda i: jnp.minimum(i, n - 1)
    late = lambda i: jnp.maximum(i - n, 0)
    return run_kernel(
        body,
        2 * n,
        [
            pl.BlockSpec((rows, TILE), lambda i: (0, early(i))),
            pl.BlockSpec((rows, TILE), lambda i: (0, early(i))),
            pl.BlockSpec((2 * rows, 2 * ff), lambda i: (0, 0)),
            pl.BlockSpec((TILE, ff), lambda i: (early(i), 2)),
            pl.BlockSpec((TILE, 2 * ff), lambda i: (late(i), 0)),
        ],
        [
            pl.BlockSpec((2 * rows, 2 * ff), lambda i: (0, 0)),
            pl.BlockSpec((rows, TILE), lambda i: (0, late(i))),
            pl.BlockSpec((rows, TILE), lambda i: (0, late(i))),
        ],
        [
            pltpu.HBM((2 * rows, 2 * ff), bf16),
            jax.ShapeDtypeStruct((rows, features), bf16),
            jax.ShapeDtypeStruct((rows, features), bf16),
        ],
        (ga, gb, gu, weights, weights),
        (pltpu.VMEM((2 * rows, ff), f32),),
        free=2,
    )


def outer(slots, pairs, parts=1):
    rows, features = slots[0].shape
    width = pairs[0].shape[1] // parts

    def body(s0, s1, s2, s3, b0, b1, *outs):
        first = jnp.concatenate([s0[...], s1[...]], axis=0)
        second = jnp.concatenate([s2[...], s3[...]], axis=0)
        for index, out in enumerate(outs):
            at = slice(index * width, (index + 1) * width)
            out[...] = (t_dot(first, b0[:, at]) + t_dot(second, b1[:, at])).astype(bf16)

    return run_kernel(
        body,
        features // OUTER_TILE,
        [pl.BlockSpec((rows, OUTER_TILE), lambda i: (0, i)) for _ in slots]
        + [pl.BlockSpec((2 * rows, parts * width), lambda i: (0, 0)) for _ in pairs],
        [pl.BlockSpec((OUTER_TILE, width), lambda i: (i, 0)) for _ in range(parts)],
        [pltpu.HBM((features, width), bf16) for _ in range(parts)],
        (*slots, *pairs),
        room=24,
    )


def whole_kernel(body, out_shape, args, scratch=(), free=0):
    return pl.pallas_call(
        body,
        out_shape=out_shape,
        scratch_shapes=scratch,
        cost_estimate=thin_cost(),
        compiler_params=pltpu.CompilerParams(vmem_limit_bytes=40 * 1024 * 1024),
    )(*pinned(args, free))


def turn_heads(values, cosine, sine):
    half_width = HD // 2
    parts = []
    for at in range(0, values.shape[0], HD):
        first = values[at : at + half_width]
        second = values[at + half_width : at + HD]
        parts += [first * cosine - second * sine, second * cosine + first * sine]
    return jnp.concatenate(parts, axis=0)


def attention_forward(slots, weights, bias, cosine, sine, widths):
    q_width, k_width = widths
    rows, features = slots[0].shape
    total = rows * len(slots)
    heads = q_width // HD
    repeat = heads // (k_width // HD)
    qkv_width = q_width + 2 * k_width
    scale = HD ** (-0.5)

    def body(*refs):
        xs, (w, bias, cosine, sine) = refs[: len(slots)], refs[len(slots) : len(slots) + 4]
        qt, kvt, lse, mixed, *parts = refs[len(slots) + 4 : -2]
        mt, keys = refs[-2:]
        x = jnp.concatenate([r[...] for r in xs], axis=0)
        qkv = dot(x, w[:, :qkv_width]).T
        cos, sin = cosine[...], sine[...]
        qt[...] = turn_heads(qkv[:q_width], cos, sin).astype(bf16)
        kt = turn_heads(qkv[q_width : q_width + k_width], cos, sin).astype(bf16)
        kvt[:k_width] = kt
        kvt[k_width:] = qkv[q_width + k_width :].astype(bf16)
        keys[...] = kt.astype(f32).T.astype(bf16)

        def head(h, carry):
            at = pl.ds(h * HD, HD)
            group = h // repeat
            vt = kvt[pl.ds(k_width + group * HD, HD)]
            k = keys[...] if k_width == HD else keys[:, pl.ds(group * HD, HD)]
            q = qt[at] * jnp.asarray(scale, bf16)
            s = dot(k, q) + bias[...]
            largest = jnp.max(s, axis=0, keepdims=True)
            e = jnp.exp(s - largest)
            t = jnp.sum(e, axis=0, keepdims=True)
            p = (e * (1.0 / t)).astype(bf16)
            mt[at] = dot(vt, p)
            lse[pl.ds(h, 1)] = largest + jnp.log(t)
            return carry

        lax.fori_loop(0, heads, head, 0, unroll=4 if heads % 4 == 0 else 1)
        m = mt[...].T.astype(bf16)
        mixed[...] = m
        out = dot_t(m, w[:, qkv_width:])
        for index, part in enumerate(parts):
            part[...] = out[index * rows : (index + 1) * rows].astype(bf16)

    return whole_kernel(
        body,
        [
            pltpu.HBM((q_width, total), bf16),
            pltpu.HBM((2 * k_width, total), bf16),
            pltpu.HBM((heads, total), f32),
            pltpu.HBM((total, q_width), bf16),
        ]
        + [jax.ShapeDtypeStruct((rows, features), bf16) for _ in slots],
        (*slots, weights, bias, cosine, sine),
        (pltpu.VMEM((q_width, total), f32), pltpu.VMEM((total, k_width), bf16)),
        free=4,
    )


def attention_backward(slots, weights, bias, cosine, sine, qt, kvt, lse, widths):
    q_width, k_width = widths
    rows, features = slots[0].shape
    total = rows * len(slots)
    heads = q_width // HD
    repeat = heads // (k_width // HD)
    qkv_width = q_width + 2 * k_width
    scale = HD ** (-0.5)

    def body(*refs):
        ms, (w, bias, cosine, sine, qt, kvt, lse) = refs[: len(slots)], refs[len(slots) : len(slots) + 7]
        grad, *parts = refs[len(slots) + 7 : -4]
        gt, gq, kv, gkv = refs[-4:]
        m = jnp.concatenate([r[...] for r in ms], axis=0)
        gt[...] = dot(m, w[:, qkv_width:]).T.astype(bf16)
        kv[...] = kvt[...].astype(f32).T.astype(bf16)
        gkv[...] = jnp.zeros(gkv.shape, f32)

        def head(h, carry):
            at = pl.ds(h * HD, HD)
            group = h // repeat
            k_at = 0 if k_width == HD else group * HD
            kt = kvt[pl.ds(k_at, HD)]
            k = kv[:, pl.ds(k_at, HD)]
            v = kv[:, pl.ds(k_width + k_at, HD)]
            q = qt[at]
            g = gt[at]
            s = dot(k, q * jnp.asarray(scale, bf16)) + bias[...]
            p = jnp.exp(s - lse[pl.ds(h, 1)])
            gp = dot(v, g)
            inner = jnp.sum(p * gp, axis=0, keepdims=True)
            gs = (p * (gp - inner) * scale).astype(bf16)
            gq[at] = dot(kt, gs)
            gk = dot_t(gs, q)
            gv = dot_t(p.astype(bf16), g)
            gkv[pl.ds(group, 1)] += jnp.concatenate([gk, gv], axis=1)[None]
            return carry

        lax.fori_loop(0, heads, head, 0, unroll=4 if heads % 4 == 0 else 1)
        cos, sin = cosine[...], -sine[...]
        both = [gkv[index].T for index in range(k_width // HD)]
        gk = jnp.concatenate([b[:HD] for b in both], axis=0)
        gv = jnp.concatenate([b[HD:] for b in both], axis=0)
        found = jnp.concatenate(
            [turn_heads(gq[...], cos, sin), turn_heads(gk, cos, sin), gv], axis=0
        ).T.astype(bf16)
        grad[...] = found
        out = dot_t(found, w[:, :qkv_width])
        for index, part in enumerate(parts):
            part[...] = out[index * rows : (index + 1) * rows].astype(bf16)

    return whole_kernel(
        body,
        [pltpu.HBM((total, qkv_width), bf16)]
        + [jax.ShapeDtypeStruct((rows, features), bf16) for _ in slots],
        (*slots, weights, bias, cosine, sine, qt, kvt, lse),
        (
            pltpu.VMEM((q_width, total), bf16),
            pltpu.VMEM((q_width, total), f32),
            pltpu.VMEM((total, 2 * k_width), bf16),
            pltpu.VMEM((k_width // HD, total, 2 * HD), f32),
        ),
        free=4,
    )


def shard_of(layer, columns, row):
    depth, rows, _ = columns[0].shape
    widths = [c.shape[2] for c in columns] + [row.shape[1]]

    def body(*refs):
        out = refs[-1]
        at, pending = 0, []
        for ref, width in zip(refs[:-2], widths):
            pending.append(ref[...])
            if sum(p.shape[1] for p in pending) % 128 == 0:
                part = pending[0] if len(pending) == 1 else jnp.concatenate(pending, axis=1)
                out[:, at : at + part.shape[1]] = part
                at, pending = at + part.shape[1], []
        assert not pending
        out[:, at:] = refs[-2][...].astype(f32).T.astype(bf16)

    return pl.pallas_call(
        body,
        grid=(1,),
        in_specs=[
            pl.BlockSpec((None, *v.shape[1:]), lambda i: (layer, 0, 0)) for v in (*columns, row)
        ],
        out_specs=pl.BlockSpec((rows, sum(widths)), lambda i: (0, 0)),
        out_shape=pltpu.HBM((rows, sum(widths)), bf16),
        cost_estimate=thin_cost(),
        compiler_params=pltpu.CompilerParams(vmem_limit_bytes=32 * 1024 * 1024),
    )(*pinned((*columns, row)))


def split_outer(groups, order_pair):
    size = lax.axis_size("fsdp")
    rows, features = groups[0][0][0].shape
    block = features // size
    if block % 128:
        whole = []
        for slots, wide, parts in groups:
            whole += outer(slots, halves(wide, rows), parts)
        return whole, [Scatter(v, o).send() for v, o in zip(whole, order_pair)]
    operands, specs, plan = [], [], []
    for slots, wide, parts in groups:
        plan.append((len(operands), len(wide), wide[0].shape[1] // parts, parts))
        for other in (1, 0):
            operands += slots
            specs += [
                pl.BlockSpec((rows, block), lambda i, c, o=other: (0, 2 * i + (c[0] + o) % 2))
                for _ in slots
            ]
        operands += wide
        specs += [pl.BlockSpec(v.shape, lambda i, c: (0, 0)) for v in wide]
    widths = [width for _, _, width, parts in plan for _ in range(parts)]

    def body(c, *refs):
        outs = list(refs[len(operands) :])
        for start, count, width, parts in plan:
            wides = refs[start + 8 : start + 8 + count]
            lefts = [
                jnp.concatenate([r[...] for r in refs[at : at + 4]], axis=0)
                for at in (start, start + 4)
            ]
            each = 4 * rows // count
            for part in range(parts):
                columns = slice(part * width, (part + 1) * width)
                for left in lefts:
                    found = sum(
                        t_dot(left[k * each : (k + 1) * each], w[:, columns])
                        for k, w in enumerate(wides)
                    )
                    outs.pop(0)[...] = found.astype(bf16)

    core = (lax.axis_index("fsdp") % 2).astype(jnp.int32)[None]
    found = pl.pallas_call(
        body,
        grid_spec=pltpu.PrefetchScalarGridSpec(
            num_scalar_prefetch=1,
            grid=(size // 2,),
            in_specs=specs,
            out_specs=[pl.BlockSpec((block, w), lambda i, c: (i, 0)) for w in widths for _ in (0, 1)],
        ),
        out_shape=[pltpu.HBM((features // 2, w), bf16) for w in widths for _ in (0, 1)],
        cost_estimate=thin_cost(),
        compiler_params=pltpu.CompilerParams(
            dimension_semantics=("arbitrary",), vmem_limit_bytes=32 * 1024 * 1024
        ),
    )(core, *pinned(operands))
    return found[1::2], found[0::2]


def halves(wide, rows):
    return wide if len(wide) == 2 else [wide[0][: 2 * rows], wide[0][2 * rows :]]


def slots_by_down(slots, weights):
    rows, features = slots[0].shape
    ff = weights.shape[1] // 3
    total = rows * len(slots)

    def body(*refs):
        i = pl.program_id(0)
        out = refs[-1]
        part = dot(jnp.concatenate([r[...] for r in refs[:-2]], axis=0), refs[-2][...])

        @pl.when(i == 0)
        def _():
            out[...] = part

        @pl.when(i > 0)
        def _():
            out[...] += part

    return run_kernel(
        body,
        features // OUTER_TILE,
        [pl.BlockSpec((rows, OUTER_TILE), lambda i: (0, i)) for _ in slots]
        + [pl.BlockSpec((OUTER_TILE, ff), lambda i: (i, 2))],
        pl.BlockSpec((total, ff), lambda i: (0, 0)),
        pltpu.HBM((total, ff), f32),
        (*slots, weights),
        room=24,
    )


def down_of(pairs, weights):
    both, ff = pairs[0].shape
    rows = both // 2
    features = weights.shape[0]

    def body(*refs):
        acts, w, outs = refs[:2], refs[2], refs[3:]
        part = dot_t(jnp.concatenate([r[...] for r in acts], axis=0), w[...])
        for index, out in enumerate(outs):
            out[...] = part[index * rows : (index + 1) * rows].astype(bf16)

    return run_kernel(
        body,
        features // OUTER_TILE,
        [pl.BlockSpec((both, ff), lambda i: (0, 0)) for _ in pairs]
        + [pl.BlockSpec((OUTER_TILE, ff), lambda i: (i, 2))],
        [pl.BlockSpec((rows, OUTER_TILE), lambda i: (0, i)) for _ in range(4)],
        [pltpu.HBM((rows, features), bf16) for _ in range(4)],
        (*pairs, weights),
        room=24,
    )


def gather_weight(values):
    return lax.all_gather(values, "fsdp", axis=0, tiled=True)


def scatter_weight(values):
    return lax.psum_scatter(values.astype(bf16), "fsdp", scatter_dimension=0, tiled=True)


def step(moving, work=None, inputs=(), launch=(), land=()):
    moving, inputs, sent = lax.optimization_barrier(
        (tuple(moving), tuple(inputs), tuple(a for a, _ in launch))
    )
    moved = tuple(shift(m) for m in moving)
    flying = tuple(exchange(a, bit) for a, (_, bit) in zip(sent, launch))
    results = () if work is None else work(*inputs)
    moved, results, landed = lax.optimization_barrier((moved, results, tuple(land)))
    return moved, results, flying, landed


def exchange(values, bit, axis="fsdp"):
    size = lax.axis_size(axis)
    return lax.ppermute(values, axis, [(i, i ^ (1 << bit)) for i in range(size)])


def fsdp_bits():
    count = lax.axis_size("fsdp").bit_length() - 1
    width = (count - 1) // 2
    return [0], list(range(1, 1 + width)), list(range(1 + width, count))


def my_bit(bit):
    return (lax.axis_index("fsdp") // (1 << bit)) % 2


def sends(*tracks):
    def work(*values):
        values, found = list(values), []
        for track in tracks:
            held, track.terms = track.terms, [values.pop(0) for _ in track.terms]
            found.append(track.send())
            track.terms = held
        return tuple(found)

    return work


def held(*tracks):
    return tuple(t for track in tracks for t in track.terms)


def flights(tracks, arrays):
    return tuple((a, t.bit) for t, a in zip(tracks, arrays))


def arrive(tracks, arrays):
    for track, values in zip(tracks, arrays):
        track.arrived(values)


def run_down(tracks, arrays, left):
    arrays = list(arrays)
    for index, track in enumerate(tracks):
        while len(track.order) - track.stage > left:
            track.arrived(exchange(arrays[index], track.bit))
            arrays[index] = track.send()
    return arrays


class Scatter:
    def __init__(self, partial, order, features=None):
        self.size = lax.axis_size("fsdp")
        self.me = lax.axis_index("fsdp")
        self.order = list(order)
        self.stage = 0
        self.terms = [partial]
        bits = sorted(order, reverse=True)
        if features is not None and partial.shape[0] < features:
            bits = bits[:-1]
        self.rows = partial.shape[0] >> len(bits)
        self.free = [bits]

    @property
    def bit(self):
        return self.order[self.stage]

    @property
    def last(self):
        return self.stage == len(self.order) - 1

    def sum_blocks(self, blocks, dtype):
        ids = jnp.stack(
            [
                sum(
                    (((blocks >> b) & 1) << (len(free) - 1 - k) for k, b in enumerate(free)),
                    jnp.zeros_like(blocks),
                )
                for free in self.free
            ]
        ).astype(jnp.int32)
        width = self.terms[0].shape[1]
        rows, count = self.rows, blocks.shape[0]

        def body(ids, *refs):
            refs[-1][...] = sum(r[...].astype(f32) for r in refs[:-1]).astype(dtype)

        return pl.pallas_call(
            body,
            grid_spec=pltpu.PrefetchScalarGridSpec(
                num_scalar_prefetch=1,
                grid=(count,),
                in_specs=[
                    pl.BlockSpec((rows, width), lambda i, ids, term=term: (ids[term, i], 0))
                    for term in range(len(self.terms))
                ],
                out_specs=pl.BlockSpec((rows, width), lambda i, ids: (i, 0)),
            ),
            out_shape=jax.ShapeDtypeStruct((count * rows, width), dtype),
            cost_estimate=thin_cost(),
            compiler_params=pltpu.CompilerParams(
                dimension_semantics=("arbitrary",), vmem_limit_bytes=16 * 1024 * 1024
            ),
        )(ids, *pinned(self.terms))

    def send(self):
        free = self.free[self.stage]
        left = [b for b in free if b != self.bit]
        each = jnp.arange(1 << len(left))
        blocks = (self.me ^ (1 << self.bit)) + jnp.zeros_like(each)
        for k, b in enumerate(left):
            blocks = (blocks & ~(1 << b)) | (((each >> (len(left) - 1 - k)) & 1) << b)
        return self.sum_blocks(blocks, bf16)

    def arrived(self, values):
        self.terms.append(values)
        self.free.append([b for b in self.free[-1] if b != self.bit])
        self.stage += 1

    def finish(self):
        total = 0.0
        for values, free in zip(self.terms, self.free):
            at = sum((((self.me >> b) & 1) << (len(free) - 1 - k) for k, b in enumerate(free)), 0)
            blocks = values.reshape(-1, self.rows, values.shape[1])
            total += lax.dynamic_index_in_dim(blocks, at, 0, keepdims=False).astype(f32)
        return total


def sum_all(values, axis):
    for bit in range(lax.axis_size(axis).bit_length() - 1):
        values = values + exchange(values, bit, axis)
    return values


def sum_to_owner(values):
    for bit in reversed(range(lax.axis_size("fsdp").bit_length() - 1)):
        low, high = jnp.split(values, 2, axis=-1)
        upper = my_bit(bit) == 1
        values = jnp.where(upper, high, low) + exchange(jnp.where(upper, low, high), bit)
    return values


def local(
    tokens,
    cotangent,
    attention_gain,
    query_weight,
    key_weight,
    value_weight,
    output_weight,
    feed_gain,
    gate_weight,
    up_weight,
    down_weight,
):
    layer_count = query_weight.shape[0]
    local_rows = tokens.shape[0]
    size = lax.axis_size("tp")
    me = lax.axis_index("tp")
    group_rows = local_rows * size
    q_width = query_weight.shape[2]
    k_width = key_weight.shape[2]
    qkv_width = q_width + 2 * k_width
    ff = gate_weight.shape[2]
    assert size == 4 and layer_count == 2

    row_index = (
        ((me - jnp.arange(size)) % size)[:, None] * local_rows + jnp.arange(local_rows)[None, :]
    ).reshape(group_rows)
    cosine, sine = (table.T for table in angle_tables(row_index % SEQ_LEN))
    seen = (row_index[:, None] <= row_index[None, :]) & (
        (row_index // SEQ_LEN)[:, None] == (row_index // SEQ_LEN)[None, :]
    )
    bias = jnp.where(seen, 0.0, masked_score).astype(f32)
    core, xs, ys = fsdp_bits()
    me_f = lax.axis_index("fsdp")
    shards = lax.axis_size("fsdp")
    shard_rows = query_weight.shape[1]
    features = shards * shard_rows

    def attention_shard(l):
        return shard_of(l, [query_weight, key_weight, value_weight], output_weight)

    def feed_shard(l):
        return shard_of(l, [gate_weight, up_weight], down_weight)

    def cat(parts):
        return jnp.concatenate(parts, axis=0)

    def norm_low(values, gain):
        return norm_rows(values, gain).astype(bf16)

    def attention(x0, x1, x2, x3, w, bias, cosine, sine):
        return tuple(
            attention_forward([x0, x1, x2, x3], w, bias, cosine, sine, (q_width, k_width))
        )

    def attention_back(m0, m1, m2, m3, w, bias, cosine, sine, qt, kvt, lse):
        return tuple(
            attention_backward(
                [m0, m1, m2, m3], w, bias, cosine, sine, qt, kvt, lse, (q_width, k_width)
            )
        )

    def add_low(moved, part):
        return (moved.astype(f32) + part).astype(bf16)

    weights_a0 = gather_weight(attention_shard(0))
    gains = jnp.zeros((shards, 2 * layer_count, shard_rows), bf16)
    gains = lax.dynamic_update_slice(
        gains, jnp.concatenate([attention_gain, feed_gain], axis=0)[None], (me_f, 0, 0)
    )
    bits = core + xs + ys

    (t1,), (gains, shard_f0), _, _ = step(
        [tokens], lambda g: (g + exchange(g, bits[0]), feed_shard(0)), (gains,)
    )
    weights_f = [gather_weight(shard_f0), None]

    def gather_gains(gains):
        for bit in bits[1:]:
            gains = gains + exchange(gains, bit)
        return (gains,)

    (t2,), (gains,), _, _ = step([t1], gather_gains, (gains,))
    gains = jnp.moveaxis(gains.astype(f32), 0, 1).reshape(2 * layer_count, features)
    gain_a, gain_f = gains[:layer_count], gains[layer_count:]

    def norm_slots(gain, *slots):
        return tuple(norm_low(v.astype(f32), gain) for v in slots)

    (t3,), (x0, x1, x2), _, _ = step([t2], norm_slots, (gain_a[0], tokens, t1, t2))
    tables = (bias, cosine, sine)
    normed0 = [x0, x1, x2, *norm_slots(gain_a[0], t3)]
    (c1,), (*saved0, mixed0, p0, p1, p2, p3), _, _ = step(
        [cotangent], attention, (*normed0, weights_a0, *tables)
    )
    residual0 = tokens.astype(f32)

    (r,), (shard_a1,), _, _ = step([p1], lambda: (attention_shard(1),))
    (r,), (shard_f1,), _, _ = step([add_low(r, p2)], lambda: (feed_shard(1),))
    weights_a1 = gather_weight(shard_a1)
    weights_f[1] = gather_weight(shard_f1)
    (r,), _, _, _ = step([add_low(r, p3)])
    hidden0 = residual0 + (r.astype(f32) + p0)

    w = weights_f[0]
    x0 = norm_low(hidden0, gain_f[0])
    (x1,), _, _, _ = step([x0])
    (x2,), _, _, _ = step([x1])
    (x3,), _, _, _ = step([x2])
    (c2,), (gu01, act01, p0, p1), _, _ = step([c1], pair_forward, (x0, x1, w))
    (r,), (gu23, act23, p2, p3), _, _ = step([p1], pair_forward, (x2, x3, w))
    (r,), _, _, _ = step([add_low(r, p2)])
    (r,), _, _, _ = step([add_low(r, p3)])
    residual1 = hidden0 + (r.astype(f32) + p0)
    feed0, gu0, act0 = [x0, x1, x2, x3], [gu01, gu23], [act01, act23]

    n0 = norm_low(residual1, gain_a[1])
    (n1,), _, _, _ = step([n0])
    (n2,), _, _, _ = step([n1])
    (n3,), _, _, _ = step([n2])
    normed1 = [n0, n1, n2, n3]
    (c3,), (*saved1, mixed1, p0, p1, p2, p3), _, _ = step(
        [c2], attention, (*normed1, weights_a1, *tables)
    )
    cots = [cotangent, c1, c2, c3]
    (r,), _, _, _ = step([p1])
    (r,), _, _, _ = step([add_low(r, p2)])
    (r,), _, _, _ = step([add_low(r, p3)])
    hidden1 = residual1 + (r.astype(f32) + p0)

    w = weights_f[1]

    x0 = norm_low(hidden1, gain_f[1])
    (x1,), (grad_act,), _, _ = step(
        [x0], lambda v, *c: (slots_by_down(c, v),), (w, *cots)
    )
    (x2,), (a01, q01, p0, p1), _, _ = step(
        [x1], lambda x, y, g, v: pair_up_back(x, y, g, 0, v), (x0, x1, grad_act, w)
    )
    (x3,), _, _, _ = step([x2])
    (r,), (a23, q23, p2, p3), _, _ = step(
        [p1], lambda x, y, g, v: pair_up_back(x, y, g, 1, v), (x2, x3, grad_act, w)
    )
    (r,), (down_part1,), _, _ = step(
        [add_low(r, p2)], lambda *v: outer(v[:4], v[4:]), (*cots, a01, a23)
    )
    down_grad1 = scatter_weight(down_part1)
    (r,), (gu_part1,), _, _ = step(
        [add_low(r, p3)],
        lambda *v: outer(v[:4], v[4:]),
        (x0, x1, x2, x3, q01, q23),
    )
    gu_grad1 = scatter_weight(gu_part1)
    grad_normed = r.astype(f32) + p0
    grad_hidden, feed_gain_part1 = jax.vjp(norm_rows, hidden1, gain_f[1])[1](grad_normed)
    grad_resid = cotangent.astype(f32) + grad_hidden

    m0 = grad_resid.astype(bf16)
    (m1,), (low0, low1, low2, low3), _, _ = step(
        [m0], lambda a, b, v: tuple(down_of([a, b], v)), (a01, a23, w)
    )
    (m2,), _, _, _ = step([m1])
    (m3,), _, _, _ = step([m2])
    (lowr,), (g, p0, p1, p2, p3), _, _ = step(
        [low1],
        attention_back,
        (m0, m1, m2, m3, weights_a1, *tables, *saved1),
    )

    order_a, order_b = core + ys + xs, core + xs + ys

    second_axis = len(ys)
    assert len(xs) == second_axis

    def outer_attention(n0, n1, n2, n3, g, m0, m1, m2, m3, mixed):
        kept, sent = split_outer(
            [([n0, n1, n2, n3], [g], 1), ([m0, m1, m2, m3], [mixed], 1)], (order_a, order_b)
        )
        return (*kept, *sent)

    (r,), (qkv, out, qkv_s, out_s), _, (down_grad1,) = step(
        [p1],
        outer_attention,
        (*normed1, g, m0, m1, m2, m3, mixed1),
        land=(down_grad1,),
    )
    att_1 = (Scatter(qkv, order_a, features), Scatter(out, order_b, features))

    def core_then_send(*tracks):
        def work(*values):
            values = list(values)
            got = [exchange(values.pop(0), 0) for _ in tracks]
            fresh = [Scatter(v, t.order, features) for t, v in zip(tracks, values)]
            arrive(fresh, got)
            return (*got, *(t.send() for t in fresh))

        return work

    (r,), landed, _, _ = step(
        [add_low(r, p2)], lambda a, b: (exchange(a, 0), exchange(b, 0)), (qkv_s, out_s)
    )
    arrive(att_1, landed)
    (r,), arrays, _, _ = step([add_low(r, p3)], sends(*att_1), held(*att_1))
    arrays = run_down(att_1, arrays, 1 + second_axis)
    grad_normed = r.astype(f32) + p0
    grad_before, attention_gain_part1 = jax.vjp(norm_rows, residual1, gain_a[1])[1](grad_normed)
    grad_resid = grad_resid + grad_before

    w = weights_f[0]

    g0 = grad_resid.astype(bf16)
    (g1,), _, flying, _ = step([g0], launch=flights(att_1, arrays))
    (g2,), (q01, p0, p1), _, landed = step(
        [g1], pair_back, (g0, g1, gu0[0], w), land=flying
    )
    arrive(att_1, landed)
    (g3,), arrays, _, _ = step([g2], sends(*att_1), held(*att_1))
    arrays = run_down(att_1, arrays, 1)
    (r,), (q23, p2, p3), flying, (gu_grad1,) = step(
        [p1],
        pair_back,
        (g2, g3, gu0[1], w),
        launch=flights(att_1, arrays),
        land=(gu_grad1,),
    )

    def gate_up(*v):
        kept, sent = split_outer([(list(v[:4]), list(v[4:]), 2)], (order_a, order_b))
        return (*kept, *sent)

    (r,), (gate, up, gate_s, up_s), _, landed = step(
        [add_low(r, p2)], gate_up, (*feed0, q01, q23), land=flying
    )
    arrive(att_1, landed)
    (r,), (gate_r, up_r, down_part0), _, _ = step(
        [add_low(r, p3)],
        lambda a, b, *v: (exchange(a, 0), exchange(b, 0), *outer(v[:4], v[4:])),
        (gate_s, up_s, g0, g1, g2, g3, *act0),
    )
    down_grad0 = scatter_weight(down_part0)
    gu_0 = (Scatter(gate, order_a, features), Scatter(up, order_b, features))
    arrive(gu_0, (gate_r, up_r))
    grad_normed = r.astype(f32) + p0
    grad_hidden, feed_gain_part0 = jax.vjp(norm_rows, hidden0, gain_f[0])[1](grad_normed)
    grad_resid = grad_resid + grad_hidden

    m0 = grad_resid.astype(bf16)
    (m1,), arrays, _, _ = step([m0], sends(*gu_0), held(*gu_0))
    arrays = run_down(gu_0, arrays, 1 + second_axis)
    (m2,), _, flying, _ = step([m1], launch=flights(gu_0, arrays))
    (m3,), _, _, _ = step([m2])
    (lowr,), (g, p0, p1, p2, p3), _, _ = step(
        [add_low(lowr, low2)],
        attention_back,
        (m0, m1, m2, m3, weights_a0, *tables, *saved0),
    )
    (r,), (qkv, out, qkv_s, out_s), _, (down_grad0, *landed) = step(
        [p1],
        outer_attention,
        (*normed0, g, m0, m1, m2, m3, mixed0),
        land=(down_grad0, *flying),
    )
    arrive(gu_0, landed)
    att_0 = (Scatter(qkv, order_a, features), Scatter(out, order_b, features))
    (r,), (qkv_r, out_r, *arrays), _, _ = step(
        [add_low(r, p2)],
        lambda *v: (*core_then_send(*att_0)(*v[:4]), *sends(*gu_0)(*v[4:])),
        (qkv_s, out_s, qkv, out, *held(*gu_0)),
    )
    arrive(att_0, (qkv_r, out_r))
    att_arrays = run_down(att_0, arrays[:2], 1 + second_axis)
    gu_arrays = run_down(gu_0, arrays[2:], 1)
    done_1 = (*att_1[0].terms, *att_1[1].terms, gu_grad1, down_grad0, down_grad1)
    (r,), _, flying, done_1 = step(
        [add_low(r, p3)],
        launch=flights(gu_0, gu_arrays) + flights(att_0, att_arrays),
        land=done_1,
    )
    count = len(att_1[0].terms)
    att_1[0].terms, att_1[1].terms = list(done_1[:count]), list(done_1[count : 2 * count])
    gu_grad1, down_grad0, down_grad1 = done_1[2 * count :]

    def last_norm(r, p0, grad_resid):
        grad_before, gain_part = jax.vjp(norm_rows, residual0, gain_a[0])[1](r.astype(f32) + p0)
        return grad_resid + grad_before, gain_part

    (lowr,), (grad_resid, attention_gain_part0), _, landed = step(
        [add_low(lowr, low3)], last_norm, (r, p0, grad_resid), land=flying
    )
    arrive(gu_0, landed[:2])
    arrive(att_0, landed[2:])
    gain_sums = jnp.stack(
        [attention_gain_part0, attention_gain_part1, feed_gain_part0, feed_gain_part1]
    )
    _, arrays, _, _ = step([], sends(*att_0), held(*att_0))
    arrays = run_down(att_0, arrays, 1)

    arrive(att_0, [exchange(a, t.bit) for a, t in zip(arrays, att_0)])
    gate_grad0, up_grad0 = (t.finish() for t in gu_0)
    qkv_grads = [t[0].finish() for t in (att_0, att_1)]
    out_grads = [t[1].finish() for t in (att_0, att_1)]
    block_out = (hidden1 + (lowr.astype(f32) + low0)).astype(bf16)

    gain_sums = sum_all(sum_to_owner(gain_sums), "tp")
    return (
        block_out,
        grad_resid,
        gain_sums[:layer_count],
        jnp.stack([p[:, :q_width] for p in qkv_grads]),
        jnp.stack([p[:, q_width : q_width + k_width] for p in qkv_grads]),
        jnp.stack([p[:, q_width + k_width :] for p in qkv_grads]),
        jnp.stack([p.T for p in out_grads]),
        gain_sums[layer_count:],
        jnp.stack([gate_grad0, gu_grad1[:, :ff].astype(f32)]),
        jnp.stack([up_grad0, gu_grad1[:, ff:].astype(f32)]),
        jnp.stack([g.astype(f32).T for g in (down_grad0, down_grad1)]),
    )


def solution(mesh):
    rows = P(("fsdp", "tp"), None)
    gain = P(None, "fsdp")
    column = P(None, "fsdp", "tp")
    row = P(None, "tp", "fsdp")
    weights = (gain, column, column, column, row, gain, column, column, row)
    return jax.shard_map(
        local,
        mesh=mesh,
        in_specs=(rows, rows) + weights,
        out_specs=(rows, rows) + weights,
        check_vma=False,
    )
```
